256 devices in a mesh: expert: 32 (over x, z_hi, core), dp: 8 (over y, z_lo).
Axes of the slice: x: 4, y: 4, z: 8 (z_hi: 4, z_lo: 2; z = z_hi * 2 + z_lo), core: 2. Of those that a mesh axis runs over, the one named last changes fastest.
Arguments:
- tokens: bfloat16 [24576, 2048], P(('expert', 'dp')), may hold values from -6 to 6
- norm_gain: float32 [2048], replicated, may hold values from 0.1 to 1.9
- expert_ids: int32 [24576, 8], P(('expert', 'dp')), may hold values from 0 to 63, all different within a row; in each aligned block of 96 rows (0 to 95, 96 to 191, ...) at most 16 rows name the same one
- route_weights: float32 [24576, 8], P(('expert', 'dp')), may hold values from 0.05 to 1
- gate_weight: bfloat16 [64, 2048, 768], P('expert', 'dp'), may hold values from -0.125 to 0.125
- up_weight: bfloat16 [64, 2048, 768], P('expert', 'dp'), may hold values from -0.125 to 0.125
- down_weight: bfloat16 [64, 768, 2048], P('expert', 'dp'), may hold values from -0.21875 to 0.21875
- pair_list: int32 [32], replicated, may hold values from 0 to 31, as said below
Outputs:
- mixed: bfloat16 [24576, 2048], P(('expert', 'dp'))
- held_gate: bfloat16 [32, 2048, 768], P('expert', 'dp')
- held_up: bfloat16 [32, 2048, 768], P('expert', 'dp')
- held_down: bfloat16 [32, 768, 2048], P('expert', 'dp')
The draws below stay inside these ranges and needn't reach their ends.
Inputs may be any that keep to these rules, and one draw needn't show every extreme that they name: pair_list[pair_list[e]] = e, and pair_list[e] is e itself or differs from e in exactly one bit. `expert_ids`: each row names 8 different experts; among the rows of one device no expert is named more than 16 times, and in every draw some device's rows name one expert exactly 16 times.
All inputs are finite; a program needn't handle non-finite values.
Results may differ from the reference program's by a relative error of at most 0.0075.
Values may be sent and summed in bfloat16 or wider, within the bound.
No kernel may reach another device: no remote copies, remote signals or barrier semaphores. Data moves between devices by JAX's collectives and lax.ppermute only.
A program may use at most 192 MiB of HBM per device.

```python
import math
import jax
import jax.numpy as jnp
import numpy as np
from jax import lax

D = 2048
FF = 768
TOP = 8
EXP_DEV = 2
TOK_DEV = 96
EXPERTS = 64
MOST = 16
TOKENS = 24576
BITS = 5
N_EXPERT = 32
N_DP = 8


def draw_pair_list(key, part):
    positions = jnp.arange(N_EXPERT, dtype=jnp.int32)
    partners = positions
    for bit_number in range(BITS):
        tosses = jax.random.randint(jax.random.fold_in(key, 17 + bit_number), (N_EXPERT,), 0, 4)
        counterpart = jnp.bitwise_xor(positions, 1 << bit_number)
        lowest = jnp.minimum(positions, counterpart)
        unmatched = partners == positions
        chosen = (tosses[lowest] == 0) & unmatched & unmatched[counterpart]
        partners = jnp.where(chosen, counterpart, partners)
    return partners.astype(jnp.int32)


def block_levels(own_key, shape, split, smallest, top_value):
    def one(axis_at, shards_of):
        steps = jax.random.uniform(jax.random.fold_in(jax.random.fold_in(own_key, 6), axis_at), (shards_of,), jnp.float32, smallest / len(split), top_value / len(split))
        return jnp.repeat(jnp.exp(steps), shape[axis_at] // shards_of).reshape((-1,) + (1,) * (len(shape) - axis_at - 1))

    level = one(*split[0])
    for cut in split[1:]:
        level = level * one(*cut)
    return level


def shared_out(own_key, own, number, rows, number_of, top, bound, skew):
    ranking = jax.random.permutation(own_key, number_of)
    packed, ordinary = portions_of(number_of, rows * top, bound, skew, True), portions_of(number_of, rows * top, bound, skew, False)
    places = jnp.arange(number_of)

    def named(sizes, rotation):
        used = int((sizes > 0).sum())
        fixed = max(1, used // 4)
        passed = fixed + (places - fixed + rotation * (used - fixed)) % max(1, number_of - fixed)
        return jnp.zeros((number_of,), jnp.int32).at[ranking[jnp.where(places < fixed, places, passed)]].set(jnp.asarray(sizes, jnp.int32))

    sizes = jnp.where(number % 4 == 0, named(packed, number // 4), named(ordinary, number - number // 4 - 1))
    mixed = jax.random.permutation(jax.random.fold_in(own, 3), number_of)
    donor, sink = mixed[0:number_of // 2 * 2:2], mixed[1:number_of // 2 * 2:2]
    room = jnp.minimum(sizes[donor] - 1, bound - sizes[sink]) // 2
    room = jnp.where((donor == ranking[0]) | (sink == ranking[0]) | (sizes[sink] == 0), 0, jnp.maximum(room, 0))
    passed = jax.random.randint(jax.random.fold_in(own, 4), (number_of // 2,), 0, 1 << 20) % (room + 1)
    sizes = sizes.at[donor].add(-passed).at[sink].add(passed)
    items = jnp.searchsorted(jnp.cumsum(sizes), jnp.arange(rows * top), side="right").astype(jnp.int32)
    listing = items.reshape(top, rows).T
    listing = listing[jax.random.permutation(jax.random.fold_in(own, 1), rows)]
    rotation = jax.random.randint(jax.random.fold_in(own, 2), (rows, 1), 0, top)
    return jnp.take_along_axis(listing, (jnp.arange(top)[None, :] + rotation) % top, axis=1)


def portions_of(number_of, total, reach, slope, full):
    loads = [(1 << 20) // math.isqrt(rank ** slope) + 1 for rank in range(1, number_of + 1)]
    largest = reach if full else min(reach, max(-(-total // number_of), total * loads[0] // sum(loads)))
    least = 1 if total - largest >= number_of - 1 else 0
    counts, spare = [largest] + [least] * (number_of - 1), total - largest - least * (number_of - 1)
    while spare > 0:
        candidates = [i for i in range(1, number_of) if counts[i] < largest] or [i for i in range(1, number_of) if counts[i] < reach]
        pool, budget = sum([loads[i] for i in candidates]), spare
        for i in candidates:
            extra = min(reach - counts[i], max(1, budget * loads[i] // pool), spare)
            counts[i] = counts[i] + extra
            spare = spare - extra
    return np.array(counts)


def normal_values(rng, shape, spread, most, split=(), kind=jnp.bfloat16):
    drawn = jax.random.normal(rng, shape, jnp.float32) * spread
    if len(split) > 0:
        drawn = block_levels(rng, shape, split, -0.22, 0.18) * drawn
    return jnp.clip(drawn, min=-most, max=most).astype(kind)


def setup_inputs(seed: int = 0) -> dict:
    splits = jax.random.split(jax.random.key(seed), 9)
    tokens = normal_values(splits[0], (TOKENS, D), 1.0, 6.0, ((0, 256),))
    norm_gain = jnp.clip(1.0 + 0.18 * jax.random.normal(splits[1], (D,), jnp.float32), 0.1, 1.9)
    expert_ids_keys = jax.random.split(jax.random.fold_in(splits[2], 1), TOKENS // TOK_DEV)
    expert_ids_turns = jax.random.permutation(jax.random.fold_in(splits[2], 3), TOKENS // TOK_DEV)
    expert_ids = jax.vmap(lambda own, number: shared_out(jax.random.fold_in(splits[2], 2), own, number, TOK_DEV, EXPERTS, TOP, MOST, 2))(expert_ids_keys, expert_ids_turns).reshape((TOKENS, TOP))
    route_weights = jnp.clip(0.05 + 0.95 * jax.random.uniform(splits[3], (TOKENS, TOP), jnp.float32) ** block_levels(splits[3], (TOKENS, TOP), ((0, 256),), -0.2, 0.2), 0.05, 1.0)
    gate_weight = normal_values(splits[4], (EXPERTS, D, FF), D ** -0.5, 0.125, ((0, 32), (1, 8)))
    up_weight = normal_values(splits[5], (EXPERTS, D, FF), D ** -0.5, 0.125, ((0, 32), (1, 8)))
    down_weight = normal_values(splits[6], (EXPERTS, FF, D), FF ** -0.5, 0.21875, ((0, 32), (1, 8)))
    pair_list = draw_pair_list(jax.random.fold_in(splits[8], 71), 0)
    return dict(tokens=tokens, norm_gain=norm_gain, expert_ids=expert_ids, route_weights=route_weights, gate_weight=gate_weight, up_weight=up_weight, down_weight=down_weight, pair_list=pair_list)


def reference(tokens, norm_gain, expert_ids, route_weights, gate_weight, up_weight, down_weight, pair_list):
    values = tokens.astype(jnp.float32)
    scale = lax.rsqrt(lax.optimization_barrier(jnp.mean(values * values, axis=-1, keepdims=True)) + 1e-06)
    normed = (values * scale * norm_gain).astype(jnp.bfloat16)
    flat_ids = expert_ids.reshape(-1)
    flat_weights = lax.optimization_barrier(route_weights.reshape(-1).astype(jnp.bfloat16)).astype(jnp.float32)
    capacity = N_EXPERT * N_DP * MOST

    def one_expert(expert, total):
        matching = flat_ids == expert
        chosen = jnp.nonzero(matching, size=capacity, fill_value=0)[0].astype(jnp.int32)
        number = jnp.sum(matching.astype(jnp.int32))
        valid = jnp.arange(capacity, dtype=jnp.int32) < number
        token_rows = (chosen // TOP).astype(jnp.int32)
        inputs = normed[token_rows]
        gate_act = jnp.dot(inputs, gate_weight[expert], preferred_element_type=jnp.float32)
        up_act = jnp.dot(inputs, up_weight[expert], preferred_element_type=jnp.float32)
        hidden = (jax.nn.silu(gate_act) * up_act).astype(jnp.bfloat16)
        result = jnp.dot(hidden, down_weight[expert], preferred_element_type=jnp.float32)
        result = lax.optimization_barrier(result.astype(jnp.bfloat16)).astype(jnp.float32)
        factor = jnp.where(valid, flat_weights[chosen], jnp.zeros((), jnp.float32))
        return total.at[token_rows].add(result * factor[:, None])
    total = lax.fori_loop(0, EXPERTS, one_expert, jnp.zeros((TOKENS, D), jnp.float32))
    mixed = total.astype(jnp.bfloat16)
    source = (EXP_DEV * pair_list).astype(jnp.int32)
    return (mixed, gate_weight[source], up_weight[source], down_weight[source])
```

```python
import functools

import jax
import jax.numpy as jnp
from jax import lax
from jax.experimental import pallas as pl
from jax.experimental.pallas import tpu as pltpu
from jax.sharding import Mesh
from jax.sharding import PartitionSpec as P

EXPERT = ("x", "zh", "c")
DP = ("y", "zl")
PLANE = ("x", "c")
Z = ("zh", "zl")
EXPERT_DP = EXPERT + DP
MOST = 16
NX, NZH, NC, NY, NZL = 4, 4, 2, 4, 2
NZ = NZH * NZL
BF = jnp.bfloat16
F32 = jnp.float32
GROUPS = ((0, -1, 1), (-2, 2), (-3, 3, 4))


def shift(value, axes, count, step):
    return lax.ppermute(value, axes, [(i, (i + step) % count) for i in range(count)])


def to_plane(value, dx, dc):
    pairs = []
    for x in range(NX):
        for c in range(NC):
            pairs.append((x * NC + c, ((x + dx) % NX) * NC + (c ^ dc)))
    return lax.ppermute(value, PLANE, pairs)


def from_plane(value, dx, dc):
    return to_plane(value, (-dx) % NX, dc)


REL = tuple((dx, dc) for dx in range(NX) for dc in range(NC))


def flip(value, axis, bit):
    count = {"x": NX, "zh": NZH, "c": NC, "zl": NZL}[axis]
    return lax.ppermute(value, axis, [(i, i ^ bit) for i in range(count)])


def after(value, *others):
    return lax.optimization_barrier((value, *others))[0]


def ffn_kernel(splits, place_ref, *refs):
    n_rows = len(splits)
    weight_refs, refs = refs[:6], refs[6:]
    row_refs, refs = refs[:n_rows], refs[n_rows:]
    out_refs, refs = refs[:n_rows], refs[n_rows:]
    gate_v, up_v, down_v, rows_v, res_v, sem_w, sem_r, sem_o = refs
    zl = place_ref[0]
    copies = []
    starts = []
    at = 0
    for i, n in enumerate(splits):
        starts.append(at)
        cp = pltpu.make_async_copy(row_refs[i], rows_v.at[pl.ds(at, n)], sem_r.at[i])
        cp.start()
        copies.append(cp)
        at += n
    total = at
    loads = []
    for half in range(2):
        zl_from = zl if half == 0 else 1 - zl
        for k, dest in enumerate((gate_v, up_v, down_v)):
            src = weight_refs[half * 3 + k]
            piece = src.shape[1]
            for y in range(NY):
                row = pl.multiple_of((y * NZL + zl_from) * piece, piece)
                cp = pltpu.make_async_copy(
                    src.at[y], dest.at[pl.ds(row, piece)], sem_w.at[(half * 3 + k) * NY + y]
                )
                cp.start()
                loads.append(cp)
    for cp in copies:
        cp.wait()
    for cp in loads:
        cp.wait()

    @pl.loop(0, total // 128)
    def _(step):
        at = pl.multiple_of(step * 128, 128)
        block = rows_v[pl.ds(at, 128), :]
        gate = jnp.dot(block, gate_v[...], preferred_element_type=F32)
        up = jnp.dot(block, up_v[...], preferred_element_type=F32)
        hidden = (gate / (1.0 + jnp.exp(-gate)) * up).astype(BF)
        res_v[pl.ds(at, 128), :] = jnp.dot(
            hidden, down_v[...], preferred_element_type=F32
        ).astype(BF)

    outs = []
    for i, n in enumerate(splits):
        cp = pltpu.make_async_copy(res_v.at[pl.ds(starts[i], n)], out_refs[i], sem_o.at[i])
        cp.start()
        outs.append(cp)
    for cp in outs:
        cp.wait()


def ffn(place, weights, rows):
    splits = tuple(r.shape[0] for r in rows)
    total = sum(splits)
    width = rows[0].shape[1]
    hidden = weights[0].shape[2]
    any_spec = pl.BlockSpec(memory_space=pl.ANY)
    flops = 2 * total * width * hidden * 3
    return pl.pallas_call(
        functools.partial(ffn_kernel, splits),
        out_shape=[jax.ShapeDtypeStruct(r.shape, BF) for r in rows],
        in_specs=[pl.BlockSpec(memory_space=pltpu.SMEM)] + [any_spec] * (6 + len(rows)),
        out_specs=[any_spec] * len(rows),
        scratch_shapes=[
            pltpu.VMEM((width, hidden), BF),
            pltpu.VMEM((width, hidden), BF),
            pltpu.VMEM((hidden, width), BF),
            pltpu.VMEM((total, width), BF),
            pltpu.VMEM((total, width), BF),
            pltpu.SemaphoreType.DMA((6 * NY,)),
            pltpu.SemaphoreType.DMA((len(rows),)),
            pltpu.SemaphoreType.DMA((len(rows),)),
        ],
        compiler_params=pltpu.CompilerParams(vmem_limit_bytes=44 << 20),
        cost_estimate=pl.CostEstimate(
            flops=flops, transcendentals=total * hidden, bytes_accessed=18 << 20
        ),
        name="expert_ffn",
    )(place, *weights, *rows)


def own_weights(weights):
    zl = lax.axis_index("zl")
    own = [jnp.where(zl == 0, w[0], w[1]) for w in weights]
    other = [jnp.where(zl == 0, w[1], w[0]) for w in weights]
    swapped = [flip(w, "zl", 1) for w in other]
    order = [own[0], own[1], swapped[0], swapped[1], own[2], swapped[2]]
    full = [lax.all_gather(w, "y", axis=0, tiled=False) for w in order]
    return [full[0], full[1], full[4], full[2], full[3], full[5]]


def held_blocks(weights, pair_list, gate):
    first = [w[0] for w in weights]
    gated = lax.optimization_barrier((*first, gate))[:3]
    me = lax.axis_index(EXPERT)
    want = jnp.sum(jnp.where(jnp.arange(pair_list.shape[0]) == me, pair_list ^ me, 0))
    outs = []
    for own, value in zip(first, gated):
        best = own
        for axis, bit, code in (("c", 1, 1), ("zh", 1, 2), ("zh", 2, 4), ("x", 1, 8), ("x", 2, 16)):
            best = jnp.where(want == code, flip(value, axis, bit), best)
        outs.append(best)
    return outs


def body(
    tokens, norm_gain, expert_ids, route_weights, gate_weight, up_weight, down_weight, pair_list
):
    width = tokens.shape[1]
    rows, top = expert_ids.shape
    x_me, zh_me, c_me = (lax.axis_index(a) for a in EXPERT)
    zl_me = lax.axis_index("zl")
    weights = own_weights((gate_weight, up_weight, down_weight))

    meta = jnp.concatenate([expert_ids.T.astype(BF), route_weights.T.astype(BF)], axis=0)
    metas = lax.all_gather(meta, Z, axis=0, tiled=False)
    values = tokens.astype(F32)
    scale = lax.rsqrt(jnp.mean(values * values, axis=-1, keepdims=True) + 1e-06)
    normed = (values * scale * norm_gain).astype(BF)
    held = {0: normed}
    up_, down_ = normed, normed
    for d in range(1, NZ // 2 + 1):
        up_ = shift(up_, Z, NZ, 1)
        held[-d if d < NZ // 2 else d] = up_
        if d < NZ // 2:
            down_ = shift(down_, Z, NZ, -1)
            held[d] = down_

    far = jnp.arange(len(REL), dtype=jnp.int32)
    holder = ((x_me + far // NC) & (NX - 1)) * (NZH * NC) + zh_me * NC + (c_me ^ (far & (NC - 1)))
    experts = holder * NZL + zl_me
    z_me = zh_me * NZL + zl_me
    slots = jnp.arange(MOST, dtype=jnp.int32)
    metas = jnp.take(metas, (z_me + jnp.arange(NZ, dtype=jnp.int32)) & (NZ - 1), axis=0)

    def choose(d):
        mine = metas[d % NZ]
        ids = mine[:top].astype(jnp.int32)
        named = ids[None, :, :] == experts[:, None, None]
        chosen = jnp.any(named, axis=1)
        factor = jnp.sum(jnp.where(named, mine[None, top:], jnp.zeros((), BF)), axis=1)
        ranks = jnp.cumsum(chosen.astype(jnp.int32), axis=1) - 1
        taken = (ranks[:, None, :] == slots[None, :, None]) & chosen[:, None, :]
        return taken, factor

    received, takens = [], []
    for group in GROUPS:
        n = len(group)
        parts = [choose(d) for d in group]
        taken = jnp.stack([p[0] for p in parts], axis=1)
        eye = jnp.eye(n, dtype=jnp.bool_)[None, :, None, :, None]
        placing = (taken[:, :, :, None, :] & eye).reshape(len(REL) * n * MOST, n * rows)
        factor = jnp.stack([p[1] for p in parts], axis=1)
        spread = jnp.where(
            taken[:, :, :, None, :] & eye, factor[:, :, None, None, :], jnp.zeros((), BF)
        ).reshape(len(REL) * n * MOST, n * rows)
        takens.append(spread)
        source = jnp.concatenate([held[d] for d in group], axis=0)
        out = jnp.dot(placing.astype(BF), source, preferred_element_type=F32).astype(BF)
        out = out.reshape(len(REL), n * MOST, width)
        got = []
        for r, (dx, dc) in enumerate(REL):
            got.append(out[r] if r == 0 else to_plane(out[r], dx, dc))
        received.append(got)

    new = held_blocks((gate_weight, up_weight, down_weight), pair_list, received[-1][-1])

    place = zl_me.astype(jnp.int32).reshape(1)
    partial = {}
    order = [len(GROUPS) - 1, *range(len(GROUPS) - 1)]
    calls = [[len(GROUPS) - 1], list(range(len(GROUPS) - 2, -1, -1))]
    for call in calls:
        flat = [r for g in call for r in received[g]]
        done = ffn(place, weights, flat)
        for k, g in enumerate(call):
            n = len(GROUPS[g])
            mine = done[k * len(REL) : (k + 1) * len(REL)]
            back = []
            for r, (dx, dc) in enumerate(REL):
                back.append(mine[r] if r == 0 else from_plane(mine[r], dx, dc))
            stack = jnp.concatenate(back, axis=0)
            part = lax.dot_general(
                takens[g], stack, (((0,), (0,)), ((), ())), preferred_element_type=F32
            ).reshape(n, rows, width)
            for i, d in enumerate(GROUPS[g]):
                partial[d] = part[i]

    def joined(got, d):
        return (got.astype(F32) + partial[d]).astype(BF)

    forward = shift(partial[4].astype(BF), Z, NZ, 1)
    for d in (3, 2, 1):
        forward = shift(joined(forward, d), Z, NZ, 1)
    backward = shift(partial[-3].astype(BF), Z, NZ, -1)
    for d in (-2, -1):
        backward = shift(joined(backward, d), Z, NZ, -1)
    mixed = (forward.astype(F32) + backward.astype(F32) + partial[0]).astype(BF)
    return (mixed, *(v[None] for v in new))


def solution(mesh):
    split = Mesh(mesh.devices.reshape(NX, NZH, NC, NY, NZL), EXPERT_DP)
    rows = P(EXPERT_DP, None)
    blocks = P(EXPERT, DP, None)
    return jax.shard_map(
        body,
        mesh=split,
        in_specs=(rows, P(), rows, rows, blocks, blocks, blocks, P()),
        out_specs=(rows, blocks, blocks, blocks),
        check_vma=False,
    )
```

```python
import functools

import jax
import jax.numpy as jnp
from jax import lax
from jax.experimental import pallas as pl
from jax.experimental.pallas import tpu as pltpu
from jax.sharding import Mesh
from jax.sharding import PartitionSpec as P

EXPERT = ("x", "zh", "c")
DP = ("y", "zl")
Z = ("zh", "zl")
EXPERT_DP = EXPERT + DP
MOST = 16
NX, NZH, NC, NY, NZL = 4, 4, 2, 4, 2
NZ = NZH * NZL
PLACES = NX * NC
ROWS, TOP, WIDTH, HIDDEN = 96, 8, 2048, 768
META = 8
SHARD, DSHARD = 256, 96
PACK = 384
HALF = PACK // 2
SIDE = 2 * HIDDEN
BF = jnp.bfloat16
F32 = jnp.float32
GROUPS = ((0, -1, 1), (-2, 2), (-3, 3, 4))
VMEM = pl.BlockSpec(memory_space=pltpu.VMEM)
SMEM = pl.BlockSpec(memory_space=pltpu.SMEM)
ANY = pl.BlockSpec(memory_space=pl.ANY)
LIMIT = 48 << 20


def shift(value, axes, count, step):
    return lax.ppermute(value, axes, [(i, (i + step) % count) for i in range(count)])


def along_z(value, step):
    return shift(value, Z, NZ, step)


def along_y(value, step):
    return shift(value, "y", NY, step)


def flip(value, axis):
    return lax.ppermute(value, axis, [(0, 1), (1, 0)])


def across(value, axis):
    return lax.all_to_all(value, axis, split_axis=0, concat_axis=0, tiled=True)


def fence(*values):
    return lax.optimization_barrier(values)


def call(kernel, outs, in_specs, out_specs, name, scratch=(), cost=None):
    return pl.pallas_call(
        kernel,
        out_shape=outs,
        in_specs=in_specs,
        out_specs=out_specs,
        scratch_shapes=scratch,
        compiler_params=pltpu.CompilerParams(vmem_limit_bytes=LIMIT),
        cost_estimate=cost,
        name=name,
    )


def shape(*dims, dtype=BF):
    return jax.ShapeDtypeStruct(dims, dtype)


def prep_kernel(tokens_ref, gain_ref, ids_ref, weights_ref, out_ref):
    values = tokens_ref[...].astype(F32)
    scale = lax.rsqrt(jnp.mean(values * values, axis=-1, keepdims=True) + 1e-06)
    out_ref[pl.ds(0, ROWS), :] = (values * scale * gain_ref[...]).astype(BF)
    out_ref[pl.ds(ROWS, META), 0:128] = ids_ref[...].astype(F32).astype(BF)
    out_ref[pl.ds(ROWS, META), 128:256] = weights_ref[...].astype(BF)
    out_ref[pl.ds(ROWS, META), 256:WIDTH] = jnp.zeros((META, WIDTH - 256), BF)


def pack_kernel(place_ref, gate_ref, up_ref, down_ref, own_ref, other_ref, first_ref):
    zl = place_ref[3]
    for out_ref, e in ((own_ref, zl), (other_ref, 1 - zl), (first_ref, 0)):
        out_ref[0:SHARD, 0:HIDDEN] = gate_ref[e]
        out_ref[0:SHARD, HIDDEN:SIDE] = up_ref[e]
        out_ref[SHARD : SHARD + DSHARD, :] = down_ref[e, :, 0:SIDE]
        for j in range(3):
            out_ref[SHARD + DSHARD : PACK, 512 * j : 512 * (j + 1)] = down_ref[
                e, 32 * j : 32 * (j + 1), SIDE:WIDTH
            ]


def unpack_kernel(kind_ref, z_ref, x_ref, c_ref, gate_ref, up_ref, down_ref):
    for kind, ref in enumerate((z_ref, x_ref, c_ref)):

        @pl.when(kind_ref[0] == kind)
        def _(ref=ref):
            gate_ref[...] = ref[0:SHARD, 0:HIDDEN]
            up_ref[...] = ref[0:SHARD, HIDDEN:SIDE]
            down_ref[:, 0:SIDE] = ref[SHARD : SHARD + DSHARD, :]
            for j in range(3):
                down_ref[32 * j : 32 * (j + 1), SIDE:WIDTH] = ref[
                    SHARD + DSHARD : PACK, 512 * j : 512 * (j + 1)
                ]


def dispatch_kernel(n, place_ref, *refs):
    sources, (same_ref, other_ref, weight_ref) = refs[:n], refs[n:]
    x_me, zh, c, zl = (place_ref[k] for k in range(4))
    before = lax.broadcasted_iota(jnp.int32, (128, 128), 0)
    after = lax.broadcasted_iota(jnp.int32, (128, 128), 1)
    upto = (before <= after).astype(F32).astype(BF)
    slot = (before & (MOST - 1)).astype(F32)
    for i, ref in enumerate(sources):
        ids = ref[ROWS : ROWS + META, 0:128].astype(F32)
        route = ref[ROWS : ROWS + META, 128:256].astype(F32)
        chosen, factor = [], []
        for dc in range(NC):
            for x in range(NX):
                expert = ((x * NZH + zh) * NC + (c ^ dc)) * NZL + zl
                named = jnp.where(ids == expert.astype(F32), 1.0, 0.0)
                chosen.append(jnp.sum(named, axis=0, keepdims=True))
                factor.append(jnp.sum(named * route, axis=0, keepdims=True))
        chosen = jnp.concatenate(chosen, axis=0)
        factor = jnp.concatenate(factor, axis=0)
        ranks = jnp.dot(chosen.astype(BF), upto, preferred_element_type=F32) - 1.0
        ranks = jnp.where(chosen > 0.0, ranks, -1.0)

        def spread(v):
            return jnp.broadcast_to(v[:, None, :], (PLACES, MOST, 128)).reshape(128, 128)

        taken = spread(ranks) == slot
        placing = jnp.where(taken, 1.0, 0.0).astype(BF)
        rows = jnp.dot(placing[:, 0:ROWS], ref[0:ROWS, :], preferred_element_type=F32).astype(BF)
        for x in range(NX):
            at = x * n * MOST + i * MOST
            same_ref[at : at + MOST, :] = rows[x * MOST : (x + 1) * MOST]
            far = (NX + x) * MOST
            other_ref[at : at + MOST, :] = rows[far : far + MOST]
        weight_ref[i] = jnp.where(taken, spread(factor), 0.0).T.astype(BF)


def dispatch(place, sources):
    n = len(sources)
    rows = NX * n * MOST
    return call(
        functools.partial(dispatch_kernel, n),
        [shape(rows, WIDTH), shape(rows, WIDTH), shape(n, 128, 128)],
        [SMEM] + [VMEM] * n,
        [VMEM] * 3,
        "dispatch",
    )(place, *sources)


def ffn_kernel(splits, block, place_ref, *refs):
    pieces, refs = refs[:10], refs[10:]
    n = len(splits)
    row_refs, out_refs = refs[:n], refs[n : 2 * n]
    side_v, down_v, rows_v, res_v, sem_w, sem_r, sem_o = refs[2 * n :]
    zl, y_me = place_ref[3], place_ref[4]
    loads, starts, at = [], [], 0

    def load(src, dst):
        cp = pltpu.make_async_copy(src, dst, sem_w.at[len(loads)])
        cp.start()
        loads.append(cp)

    def down_parts(src, at, base):
        load(src.at[pl.ds(at, DSHARD)], down_v.at[pl.ds(base, DSHARD), 0:SIDE])
        for j in range(3):
            load(
                src.at[pl.ds(at + DSHARD, 32), 512 * j : 512 * (j + 1)],
                down_v.at[pl.ds(base + 32 * j, 32), SIDE:WIDTH],
            )

    gets = []
    for i, rows in enumerate(splits):
        starts.append(at)
        cp = pltpu.make_async_copy(row_refs[i], rows_v.at[pl.ds(at, rows)], sem_r.at[i])
        cp.start()
        gets.append(cp)
        at += rows
    total = at
    for half in range(2):
        from_zl = zl if half == 0 else 1 - zl
        full, (top, low) = pieces[5 * half : 5 * half + 3], pieces[5 * half + 3 : 5 * half + 5]
        for step, src in zip((0, NY - 1, 1), full):
            holder = ((y_me + step) & (NY - 1)) * NZL + from_zl
            base = pl.multiple_of(holder * SHARD, SHARD)
            load(src.at[pl.ds(0, SHARD)], side_v.at[pl.ds(base, SHARD)])
            down_parts(src, SHARD, pl.multiple_of(holder * DSHARD, DSHARD))
        holder = ((y_me + 2) & (NY - 1)) * NZL + from_zl
        base = pl.multiple_of(holder * SHARD, SHARD)
        load(top, side_v.at[pl.ds(base, HALF)])
        load(low.at[pl.ds(0, SHARD - HALF)], side_v.at[pl.ds(base + HALF, SHARD - HALF)])
        down_parts(low, SHARD - HALF, pl.multiple_of(holder * DSHARD, DSHARD))
    for cp in gets:
        cp.wait()
    for cp in loads:
        cp.wait()

    @pl.loop(0, total // block)
    def _(step):
        at = pl.multiple_of(step * block, block)
        both = jnp.dot(rows_v[pl.ds(at, block), :], side_v[...], preferred_element_type=F32)
        gate, up = both[:, 0:HIDDEN], both[:, HIDDEN:SIDE]
        hidden = (gate / (1.0 + jnp.exp(-gate)) * up).astype(BF)
        res_v[pl.ds(at, block), :] = jnp.dot(
            hidden, down_v[...], preferred_element_type=F32
        ).astype(BF)

    puts = []
    for i, rows in enumerate(splits):
        cp = pltpu.make_async_copy(res_v.at[pl.ds(starts[i], rows)], out_refs[i], sem_o.at[i])
        cp.start()
        puts.append(cp)
    for cp in puts:
        cp.wait()


def ffn(place, pieces, rows, block):
    splits = tuple(r.shape[0] for r in rows)
    total = sum(splits)
    return call(
        functools.partial(ffn_kernel, splits, block),
        [shape(s, WIDTH) for s in splits],
        [SMEM] + [ANY] * (10 + len(rows)),
        [ANY] * len(rows),
        "expert_ffn",
        scratch=[
            pltpu.VMEM((WIDTH, SIDE), BF),
            pltpu.VMEM((HIDDEN, WIDTH), BF),
            pltpu.VMEM((total, WIDTH), BF),
            pltpu.VMEM((total, WIDTH), BF),
            pltpu.SemaphoreType.DMA((2 * (3 * 5 + 2 + 4),)),
            pltpu.SemaphoreType.DMA((len(rows),)),
            pltpu.SemaphoreType.DMA((len(rows),)),
        ],
        cost=pl.CostEstimate(
            flops=6 * total * WIDTH * HIDDEN,
            transcendentals=total * HIDDEN,
            bytes_accessed=10 * WIDTH * HIDDEN,
        ),
    )(place, *pieces, *rows)


def combine_kernel(n, weight_ref, same_ref, other_ref, *outs):
    for i, out_ref in enumerate(outs):
        rows = []
        for ref in (same_ref, other_ref):
            for x in range(NX):
                at = x * n * MOST + i * MOST
                rows.append(ref[at : at + MOST, :])
        stack = jnp.concatenate(rows, axis=0)
        out_ref[...] = jnp.dot(
            weight_ref[i, 0:ROWS, :], stack, preferred_element_type=F32
        ).astype(out_ref.dtype)


def combine(weight, same, other, dtypes):
    n = len(dtypes)
    return call(
        functools.partial(combine_kernel, n),
        [shape(ROWS, WIDTH, dtype=t) for t in dtypes],
        [VMEM] * 3,
        [VMEM] * n,
        "combine",
    )(weight, same, other)


def spread_pieces(value):
    return value.reshape(NX, PACK // NX, SIDE)


def body(
    tokens, norm_gain, expert_ids, route_weights, gate_weight, up_weight, down_weight, pair_list
):
    x_me, zh_me, c_me = (lax.axis_index(a) for a in EXPERT)
    zl_me, y_me = lax.axis_index("zl"), lax.axis_index("y")
    place = jnp.stack([x_me, zh_me, c_me, zl_me, y_me]).astype(jnp.int32)

    ids = jnp.pad(expert_ids.T, ((0, 0), (0, 128 - ROWS)), constant_values=-1)
    route = jnp.pad(route_weights.T, ((0, 0), (0, 128 - ROWS)))
    near = call(prep_kernel, shape(ROWS + META, WIDTH), [VMEM] * 4, VMEM, "prep")(
        tokens, norm_gain[None, :], ids, route
    )
    own, other, first = call(
        pack_kernel, [shape(PACK, SIDE)] * 3, [SMEM] + [VMEM] * 3, [VMEM] * 3, "pack"
    )(place, gate_weight, up_weight, down_weight)

    p1, m1 = along_z(near, 1), along_z(near, -1)
    yp, ym = along_y(own, 1), along_y(own, -1)
    swapped = flip(other, "zl")
    s0, o0, w0 = dispatch(place, (near, p1, m1))
    p2, m2 = along_z(p1, 1), along_z(m1, -1)
    o0, s0 = across(o0.reshape(NX, -1, WIDTH), "x"), across(s0.reshape(NX, -1, WIDTH), "x")
    yt, yl = along_y(yp[:HALF], 1), along_y(ym[HALF:], -1)
    hx = across(spread_pieces(first), "x")
    p2, m2, yp, ym, yt, yl, swapped, o0, s0, hx, first = fence(
        p2, m2, yp, ym, yt, yl, swapped, o0, s0, hx, first
    )

    p3, m3 = along_z(p2, 1), along_z(m2, -1)
    vp, vm = along_y(swapped, 1), along_y(swapped, -1)
    o0 = flip(o0, "c")
    s1, o1, w1 = dispatch(place, (p2, m2))
    far = along_z(p3, 1)
    o1, s1 = across(o1.reshape(NX, -1, WIDTH), "x"), across(s1.reshape(NX, -1, WIDTH), "x")
    vt, vl = along_y(vp[:HALF], 1), along_y(vm[HALF:], -1)
    s2, o2, w2 = dispatch(place, (p3, m3, far))
    o2, s2, o1, s1 = fence(o2, s2, o1, s1)
    o2, s2 = across(o2.reshape(NX, -1, WIDTH), "x"), across(s2.reshape(NX, -1, WIDTH), "x")
    o1 = flip(o1, "c")
    o2 = flip(o2, "c")
    o0, s0, o1, s1, o2, s2, vp, vm, vt, vl, hx, first = fence(
        o0, s0, o1, s1, o2, s2, vp, vm, vt, vl, hx, first
    )

    holders = jnp.arange(NX, dtype=jnp.int32)
    x_from = pair_list[(holders * NZH + zh_me) * NC + c_me] >> 3
    z_from = (pair_list[(x_me * NZH + holders) * NC + c_me] >> 1) & (NZH - 1)
    me = (x_me * NZH + zh_me) * NC + c_me
    bits = jnp.sum(jnp.where(jnp.arange(pair_list.shape[0]) == me, pair_list ^ me, 0))
    kind = jnp.where(bits == 1, 2, jnp.where(bits >= 8, 1, 0)).astype(jnp.int32).reshape(1)
    hc = flip(first, "c")
    hz = across(spread_pieces(first), "zh")
    hx = across(jnp.take(hx, x_from, axis=0, mode="clip"), "x").reshape(PACK, SIDE)
    hz = across(jnp.take(hz, z_from, axis=0, mode="clip"), "zh").reshape(PACK, SIDE)
    new = call(
        unpack_kernel,
        [shape(SHARD, HIDDEN), shape(SHARD, HIDDEN), shape(DSHARD, WIDTH)],
        [SMEM] + [VMEM] * 3,
        [VMEM] * 3,
        "unpack",
    )(kind, hz, hx, hc)

    pieces = (own, yp, ym, yt, yl, swapped, vp, vm, vt, vl)

    def flat(v):
        return v.reshape(-1, WIDTH)

    def blocks(v):
        return v.reshape(NX, -1, WIDTH)

    s2, o2 = ffn(place, pieces, (flat(s2), flat(o2)), 384)
    o2, s2, o1, s1, o0, s0 = fence(o2, s2, o1, s1, o0, s0)
    s1, o1, s0, o0 = ffn(place, pieces, (flat(s1), flat(o1), flat(s0), flat(o0)), 320)
    o2 = across(blocks(flip(o2, "c")), "x")
    s2 = across(blocks(s2), "x")
    o1, o0 = flip(o1, "c"), flip(o0, "c")
    o2, s2, o1, s1 = fence(o2, s2, o1, s1)
    c_m3, c_p3, c_4 = combine(w2, flat(s2), flat(o2), (F32, BF, BF))
    o1, s1 = across(blocks(o1), "x"), across(blocks(s1), "x")
    o1, s1, o0, s0 = fence(o1, s1, o0, s0)
    c_m2, c_p2 = combine(w1, flat(s1), flat(o1), (F32, F32))
    o0, s0 = across(blocks(o0), "x"), across(blocks(s0), "x")
    c_0, c_m1, c_p1 = combine(w0, flat(s0), flat(o0), (F32, F32, F32))

    def joined(got, mine):
        return (got.astype(F32) + mine).astype(BF)

    down = along_z(c_4, -1)
    down = along_z(joined(down, c_m3), -1)
    rise = along_z(c_p3, 1)
    down = along_z(joined(down, c_m2), -1)
    rise = along_z(joined(rise, c_p2), 1)
    down = along_z(joined(down, c_m1), -1)
    rise = along_z(joined(rise, c_p1), 1)
    mixed = (down.astype(F32) + rise.astype(F32) + c_0).astype(BF)
    return (mixed, *(v[None] for v in new))


def solution(mesh):
    split = Mesh(mesh.devices.reshape(NX, NZH, NC, NY, NZL), EXPERT_DP)
    rows = P(EXPERT_DP, None)
    blocks = P(EXPERT, DP, None)
    return jax.shard_map(
        body,
        mesh=split,
        in_specs=(rows, P(), rows, rows, blocks, blocks, blocks, P()),
        out_specs=(rows, blocks, blocks, blocks),
        check_vma=False,
    )
```

```python
import functools

import jax
import jax.numpy as jnp
from jax import lax
from jax.experimental import pallas as pl
from jax.experimental.pallas import tpu as pltpu
from jax.sharding import Mesh
from jax.sharding import PartitionSpec as P

EXPERT = ("x", "zh", "c")
DP = ("y", "zl")
Z = ("zh", "zl")
EXPERT_DP = EXPERT + DP
MOST = 16
NX, NZH, NC, NY, NZL = 4, 4, 2, 4, 2
NZ = NZH * NZL
PLACES = NX * NC
ROWS, TOP, WIDTH, HIDDEN = 96, 8, 2048, 768
META = 8
SHARD, DSHARD = 256, 96
PACK = 384
HALF = PACK // 2
SIDE = 2 * HIDDEN
BF = jnp.bfloat16
F32 = jnp.float32
GROUPS = ((0, -1, 1), (-2, 2), (-3, 3, 4))
VMEM = pl.BlockSpec(memory_space=pltpu.VMEM)
SMEM = pl.BlockSpec(memory_space=pltpu.SMEM)
ANY = pl.BlockSpec(memory_space=pl.ANY)
LIMIT = 48 << 20


def shift(value, axes, count, step):
    return lax.ppermute(value, axes, [(i, (i + step) % count) for i in range(count)])


def along_z(value, step):
    return shift(value, Z, NZ, step)


def along_y(value, step):
    return shift(value, "y", NY, step)


def flip(value, axis):
    return lax.ppermute(value, axis, [(0, 1), (1, 0)])


def across(value, axis):
    return lax.all_to_all(value, axis, split_axis=0, concat_axis=0, tiled=True)


def fence(*values):
    return lax.optimization_barrier(values)


def call(kernel, outs, in_specs, out_specs, name, scratch=(), cost=None):
    return pl.pallas_call(
        kernel,
        out_shape=outs,
        in_specs=in_specs,
        out_specs=out_specs,
        scratch_shapes=scratch,
        compiler_params=pltpu.CompilerParams(vmem_limit_bytes=LIMIT),
        cost_estimate=cost,
        name=name,
    )


def shape(*dims, dtype=BF):
    return jax.ShapeDtypeStruct(dims, dtype)


def prep_kernel(tokens_ref, gain_ref, ids_ref, weights_ref, out_ref):
    values = tokens_ref[...].astype(F32)
    scale = lax.rsqrt(jnp.mean(values * values, axis=-1, keepdims=True) + 1e-06)
    out_ref[pl.ds(0, ROWS), :] = (values * scale * gain_ref[...]).astype(BF)
    out_ref[pl.ds(ROWS, META), 0:128] = ids_ref[...].astype(F32).astype(BF)
    out_ref[pl.ds(ROWS, META), 128:256] = weights_ref[...].astype(BF)
    out_ref[pl.ds(ROWS, META), 256:WIDTH] = jnp.zeros((META, WIDTH - 256), BF)


def pack_kernel(place_ref, gate_ref, up_ref, down_ref, *outs):
    zl = place_ref[3]
    for k, e in enumerate((zl, 1 - zl)):
        top_ref, low_ref = outs[2 * k], outs[2 * k + 1]
        rest = SHARD - HALF
        top_ref[:, 0:HIDDEN] = gate_ref[e, 0:HALF, :]
        top_ref[:, HIDDEN:SIDE] = up_ref[e, 0:HALF, :]
        low_ref[0:rest, 0:HIDDEN] = gate_ref[e, HALF:SHARD, :]
        low_ref[0:rest, HIDDEN:SIDE] = up_ref[e, HALF:SHARD, :]
        low_ref[rest : rest + DSHARD, :] = down_ref[e, :, 0:SIDE]
        for j in range(3):
            low_ref[rest + DSHARD : HALF, 512 * j : 512 * (j + 1)] = down_ref[
                e, 32 * j : 32 * (j + 1), SIDE:WIDTH
            ]


def pack_first_kernel(gate_ref, up_ref, down_ref, out_ref):
    out_ref[0:SHARD, 0:HIDDEN] = gate_ref[0]
    out_ref[0:SHARD, HIDDEN:SIDE] = up_ref[0]
    out_ref[SHARD : SHARD + DSHARD, :] = down_ref[0, :, 0:SIDE]
    for j in range(3):
        out_ref[SHARD + DSHARD : PACK, 512 * j : 512 * (j + 1)] = down_ref[
            0, 32 * j : 32 * (j + 1), SIDE:WIDTH
        ]


def unpack_kernel(kind_ref, z_ref, x_ref, c_ref, gate_ref, up_ref, down_ref):
    for kind, ref in enumerate((z_ref, x_ref, c_ref)):

        @pl.when(kind_ref[0] == kind)
        def _(ref=ref):
            gate_ref[...] = ref[0:SHARD, 0:HIDDEN]
            up_ref[...] = ref[0:SHARD, HIDDEN:SIDE]
            down_ref[:, 0:SIDE] = ref[SHARD : SHARD + DSHARD, :]
            for j in range(3):
                down_ref[32 * j : 32 * (j + 1), SIDE:WIDTH] = ref[
                    SHARD + DSHARD : PACK, 512 * j : 512 * (j + 1)
                ]


def dispatch_kernel(n, place_ref, *refs):
    sources, (same_ref, other_ref, weight_ref) = refs[:n], refs[n:]
    x_me, zh, c, zl = (place_ref[k] for k in range(4))
    before = lax.broadcasted_iota(jnp.int32, (128, 128), 0)
    after = lax.broadcasted_iota(jnp.int32, (128, 128), 1)
    upto = (before <= after).astype(F32).astype(BF)
    slot = (before & (MOST - 1)).astype(F32)
    for i, ref in enumerate(sources):
        ids = ref[ROWS : ROWS + META, 0:128].astype(F32)
        route = ref[ROWS : ROWS + META, 128:256].astype(F32)
        chosen, factor = [], []
        for dc in range(NC):
            for x in range(NX):
                expert = ((x * NZH + zh) * NC + (c ^ dc)) * NZL + zl
                named = jnp.where(ids == expert.astype(F32), 1.0, 0.0)
                chosen.append(jnp.sum(named, axis=0, keepdims=True))
                factor.append(jnp.sum(named * route, axis=0, keepdims=True))
        chosen = jnp.concatenate(chosen, axis=0)
        factor = jnp.concatenate(factor, axis=0)
        ranks = jnp.dot(chosen.astype(BF), upto, preferred_element_type=F32) - 1.0
        ranks = jnp.where(chosen > 0.0, ranks, -1.0)

        def spread(v):
            return jnp.broadcast_to(v[:, None, :], (PLACES, MOST, 128)).reshape(128, 128)

        taken = spread(ranks) == slot
        placing = jnp.where(taken, 1.0, 0.0).astype(BF)
        rows = jnp.dot(placing[:, 0:ROWS], ref[0:ROWS, :], preferred_element_type=F32).astype(BF)
        for x in range(NX):
            at = x * n * MOST + i * MOST
            same_ref[at : at + MOST, :] = rows[x * MOST : (x + 1) * MOST]
            far = (NX + x) * MOST
            other_ref[at : at + MOST, :] = rows[far : far + MOST]
        weight_ref[i] = jnp.where(taken, spread(factor), 0.0).T.astype(BF)


def dispatch(place, sources):
    n = len(sources)
    rows = NX * n * MOST
    return call(
        functools.partial(dispatch_kernel, n),
        [shape(rows, WIDTH), shape(rows, WIDTH), shape(n, 128, 128)],
        [SMEM] + [VMEM] * n,
        [VMEM] * 3,
        "dispatch",
    )(place, *sources)


def ffn_kernel(counts, block, place_ref, *refs):
    pieces, refs = refs[:16], refs[16:]
    n = len(counts)
    row_refs, out_refs = refs[:n], refs[n : 3 * n]
    side_v, down_v, rows_v, res_v, sem_w, sem_r, sem_o = refs[3 * n :]
    zl, y_me = place_ref[3], place_ref[4]
    loads, starts, at = [], [], 0
    rest = SHARD - HALF

    def load(src, dst):
        cp = pltpu.make_async_copy(src, dst, sem_w.at[len(loads)])
        cp.start()
        loads.append(cp)

    gets = []
    for i, count in enumerate(counts):
        starts.append(at)
        rows = NX * NC * count * MOST
        cp = pltpu.make_async_copy(row_refs[i], rows_v.at[pl.ds(at, rows)], sem_r.at[i])
        cp.start()
        gets.append(cp)
        at += rows
    total = at
    for half in range(2):
        from_zl = zl if half == 0 else 1 - zl
        for k, step in enumerate((0, NY - 1, 1, 2)):
            top, low = pieces[8 * half + 2 * k], pieces[8 * half + 2 * k + 1]
            holder = ((y_me + step) & (NY - 1)) * NZL + from_zl
            base = pl.multiple_of(holder * SHARD, SHARD)
            load(top, side_v.at[pl.ds(base, HALF)])
            load(low.at[pl.ds(0, rest)], side_v.at[pl.ds(base + HALF, rest)])
            base = pl.multiple_of(holder * DSHARD, DSHARD)
            load(low.at[pl.ds(rest, DSHARD)], down_v.at[pl.ds(base, DSHARD), 0:SIDE])
            for j in range(3):
                load(
                    low.at[pl.ds(rest + DSHARD, 32), 512 * j : 512 * (j + 1)],
                    down_v.at[pl.ds(base + 32 * j, 32), SIDE:WIDTH],
                )
    for cp in gets:
        cp.wait()
    for cp in loads:
        cp.wait()

    @pl.loop(0, total // block)
    def _(step):
        at = pl.multiple_of(step * block, block)
        both = jnp.dot(rows_v[pl.ds(at, block), :], side_v[...], preferred_element_type=F32)
        gate, up = both[:, 0:HIDDEN], both[:, HIDDEN:SIDE]
        hidden = (gate / (1.0 + jnp.exp(-gate)) * up).astype(BF)
        res_v[pl.ds(at, block), :] = jnp.dot(
            hidden, down_v[...], preferred_element_type=F32
        ).astype(BF)

    puts = []
    for i, count in enumerate(counts):
        rows = count * MOST
        for dc in range(NC):
            for x in range(NX):
                cp = pltpu.make_async_copy(
                    res_v.at[pl.ds(starts[i] + (x * NC + dc) * rows, rows)],
                    out_refs[2 * i + dc].at[pl.ds(x * rows, rows)],
                    sem_o.at[len(puts)],
                )
                cp.start()
                puts.append(cp)
    for cp in puts:
        cp.wait()


def ffn(place, pieces, groups, block):
    counts = tuple(g.shape[0] // (NX * NC * MOST) for g in groups)
    total = sum(counts) * NX * NC * MOST
    outs = [shape(NX * c * MOST, WIDTH) for c in counts for _ in range(NC)]
    return call(
        functools.partial(ffn_kernel, counts, block),
        outs,
        [SMEM] + [ANY] * (16 + len(groups)),
        [ANY] * len(outs),
        "expert_ffn",
        scratch=[
            pltpu.VMEM((WIDTH, SIDE), BF),
            pltpu.VMEM((HIDDEN, WIDTH), BF),
            pltpu.VMEM((total, WIDTH), BF),
            pltpu.VMEM((total, WIDTH), BF),
            pltpu.SemaphoreType.DMA((2 * NY * 6,)),
            pltpu.SemaphoreType.DMA((len(groups),)),
            pltpu.SemaphoreType.DMA((len(groups) * PLACES,)),
        ],
        cost=pl.CostEstimate(
            flops=6 * total * WIDTH * HIDDEN,
            transcendentals=total * HIDDEN,
            bytes_accessed=10 * WIDTH * HIDDEN,
        ),
    )(place, *pieces, *groups)


def combine_kernel(n, weight_ref, back_ref, *outs):
    for i, out_ref in enumerate(outs):
        rows = []
        for dc in range(NC):
            for x in range(NX):
                at = (x * NC + dc) * n * MOST + i * MOST
                rows.append(back_ref[at : at + MOST, :])
        stack = jnp.concatenate(rows, axis=0)
        out_ref[...] = jnp.dot(
            weight_ref[i, 0:ROWS, :], stack, preferred_element_type=F32
        ).astype(out_ref.dtype)


def combine(weight, back, dtypes):
    n = len(dtypes)
    return call(
        functools.partial(combine_kernel, n),
        [shape(ROWS, WIDTH, dtype=t) for t in dtypes],
        [VMEM] * 2,
        [VMEM] * n,
        "combine",
    )(weight, back)


def spread_pieces(value):
    return value.reshape(NX, PACK // NX, SIDE)


def over_zh(pieces, zh):
    got = [jnp.take(pieces, zh, axis=0, mode="clip")]
    for step in range(1, NZH):
        mine = jnp.take(pieces, (zh + step) & (NZH - 1), axis=0, mode="clip")
        got.append(shift(mine, "zh", NZH, step))
    return got


def blocks(v):
    return v.reshape(NX, -1, WIDTH)


def flat(v):
    return v.reshape(-1, WIDTH)


def along_x(same, other):
    both = jnp.concatenate([blocks(same), blocks(flip(other, "c"))], axis=1)
    return flat(across(both, "x"))


def body(
    tokens, norm_gain, expert_ids, route_weights, gate_weight, up_weight, down_weight, pair_list
):
    x_me, zh_me, c_me = (lax.axis_index(a) for a in EXPERT)
    zl_me, y_me = lax.axis_index("zl"), lax.axis_index("y")
    place = jnp.stack([x_me, zh_me, c_me, zl_me, y_me]).astype(jnp.int32)

    ids = jnp.pad(expert_ids.T, ((0, 0), (0, 128 - ROWS)), constant_values=-1)
    route = jnp.pad(route_weights.T, ((0, 0), (0, 128 - ROWS)))
    near = call(prep_kernel, shape(ROWS + META, WIDTH), [VMEM] * 4, VMEM, "prep")(
        tokens, norm_gain[None, :], ids, route
    )
    near, place = fence(near, place)
    own_t, own_l, other_t, other_l = call(
        pack_kernel, [shape(HALF, SIDE)] * 4, [SMEM] + [VMEM] * 3, [VMEM] * 4, "pack"
    )(place, gate_weight, up_weight, down_weight)
    first = call(pack_first_kernel, shape(PACK, SIDE), [VMEM] * 3, VMEM, "pack_first")(
        gate_weight, up_weight, down_weight
    )

    p1, m1 = along_z(near, 1), along_z(near, -1)
    yp_t, ym_t = along_y(own_t, 1), along_y(own_t, -1)
    swap_t = flip(other_t, "zl")
    near, p1, m1, yp_t, ym_t, own_l, other_l = fence(near, p1, m1, yp_t, ym_t, own_l, other_l)

    p2, m2 = along_z(p1, 1), along_z(m1, -1)
    s0, o0, w0 = dispatch(place, (near, p1, m1))
    yp_l, ym_l = along_y(own_l, 1), along_y(own_l, -1)
    yo_t = along_y(yp_t, 1)
    r0 = along_x(s0, o0)
    p3, m3 = along_z(p2, 1), along_z(m2, -1)
    swap_l = flip(other_l, "zl")
    p2, m2, p3, m3, r0, yp_l, ym_l, yo_t, swap_t, swap_l, first = fence(
        p2, m2, p3, m3, r0, yp_l, ym_l, yo_t, swap_t, swap_l, first
    )

    far = along_z(p3, 1)
    s1, o1, w1 = dispatch(place, (p2, m2))
    yo_l = along_y(ym_l, -1)
    vp_t, vm_t = along_y(swap_t, 1), along_y(swap_t, -1)
    r1 = along_x(s1, o1)
    p3, m3, far, r1, r0, yo_l, vp_t, vm_t, swap_l, first = fence(
        p3, m3, far, r1, r0, yo_l, vp_t, vm_t, swap_l, first
    )

    s2, o2, w2 = dispatch(place, (p3, m3, far))
    vp_l, vm_l = along_y(swap_l, 1), along_y(swap_l, -1)
    vo_t = along_y(vp_t, 1)
    r2 = along_x(s2, o2)
    vo_l = along_y(vm_l, -1)
    hz = over_zh(spread_pieces(first), zh_me)
    r0, r1, r2, vp_l, vm_l, vo_t, vo_l, first, *hz = fence(
        r0, r1, r2, vp_l, vm_l, vo_t, vo_l, first, *hz
    )
    pieces = (own_t, own_l, yp_t, yp_l, ym_t, ym_l, yo_t, yo_l)
    pieces += (swap_t, swap_l, vp_t, vp_l, vm_t, vm_l, vo_t, vo_l)

    s2, o2 = ffn(place, pieces, (r2,), 384)
    s2, o2, r0, r1, first, *hz = fence(s2, o2, r0, r1, first, *hz)
    b2 = along_x(s2, o2)
    s1, o1, s0, o0 = ffn(place, pieces, (r1, r0), 320)
    z_from = (pair_list[(x_me * NZH + jnp.arange(NZH)) * NC + c_me] >> 1) & (NZH - 1)
    picked = jnp.take(jnp.stack(hz), (zh_me - z_from) & (NZH - 1), axis=0, mode="clip")
    hz = over_zh(picked, zh_me)
    b2, s1, o1, s0, o0, first, *hz = fence(b2, s1, o1, s0, o0, first, *hz)

    c_m3, c_p3, c_4 = combine(w2, b2, (F32, BF, BF))
    b1 = along_x(s1, o1)
    down = along_z(c_4, -1)
    b1, down, c_m3, c_p3, s0, o0, first, *hz = fence(b1, down, c_m3, c_p3, s0, o0, first, *hz)

    def joined(got, mine):
        return (got.astype(F32) + mine).astype(BF)

    b0 = along_x(s0, o0)
    down = along_z(joined(down, c_m3), -1)
    rise = along_z(c_p3, 1)
    c_m2, c_p2 = combine(w1, b1, (F32, F32))
    down = along_z(joined(down, c_m2), -1)
    rise = along_z(joined(rise, c_p2), 1)
    b0, down, rise, first, *hz = fence(b0, down, rise, first, *hz)

    c_0, c_m1, c_p1 = combine(w0, b0, (F32, F32, F32))
    down = along_z(joined(down, c_m1), -1)
    rise = along_z(joined(rise, c_p1), 1)
    mixed = (down.astype(F32) + rise.astype(F32) + c_0).astype(BF)

    x_from = pair_list[(jnp.arange(NX) * NZH + zh_me) * NC + c_me] >> 3
    hx = across(spread_pieces(first), "x")
    hx = across(jnp.take(hx, x_from, axis=0, mode="clip"), "x").reshape(PACK, SIDE)
    hc = flip(first, "c")
    hz = jnp.take(jnp.stack(hz), (zh_me - jnp.arange(NZH)) & (NZH - 1), axis=0, mode="clip")
    me = (x_me * NZH + zh_me) * NC + c_me
    bits = jnp.sum(jnp.where(jnp.arange(pair_list.shape[0]) == me, pair_list ^ me, 0))
    kind = jnp.where(bits == 1, 2, jnp.where(bits >= 8, 1, 0)).astype(jnp.int32).reshape(1)
    new = call(
        unpack_kernel,
        [shape(SHARD, HIDDEN), shape(SHARD, HIDDEN), shape(DSHARD, WIDTH)],
        [SMEM] + [VMEM] * 3,
        [VMEM] * 3,
        "unpack",
    )(kind, hz.reshape(PACK, SIDE), hx, hc)
    return (mixed, *(v[None] for v in new))


def solution(mesh):
    split = Mesh(mesh.devices.reshape(NX, NZH, NC, NY, NZL), EXPERT_DP)
    rows = P(EXPERT_DP, None)
    blocks = P(EXPERT, DP, None)
    return jax.shard_map(
        body,
        mesh=split,
        in_specs=(rows, P(), rows, rows, blocks, blocks, blocks, P()),
        out_specs=(rows, blocks, blocks, blocks),
        check_vma=False,
    )
```

```python
import functools

import jax
import jax.numpy as jnp
from jax import lax
from jax.experimental import pallas as pl
from jax.experimental.pallas import tpu as pltpu
from jax.sharding import Mesh
from jax.sharding import PartitionSpec as P

EXPERT = ("x", "zh", "c")
DP = ("y", "zl")
Z = ("zh", "zl")
EXPERT_DP = EXPERT + DP
MOST = 16
NX, NZH, NC, NY, NZL = 4, 4, 2, 4, 2
NZ = NZH * NZL
PLACES = NX * NC
ROWS, TOP, WIDTH, HIDDEN = 96, 8, 2048, 768
META = 8
SHARD, DSHARD = 256, 96
PACK = 384
HALF = PACK // 2
SIDE = 2 * HIDDEN
BF = jnp.bfloat16
F32 = jnp.float32
GROUPS = ((0, -1, 1), (-2, 2), (-3, 3, 4))
VMEM = pl.BlockSpec(memory_space=pltpu.VMEM)
SMEM = pl.BlockSpec(memory_space=pltpu.SMEM)
ANY = pl.BlockSpec(memory_space=pl.ANY)
LIMIT = 48 << 20


def shift(value, axes, count, step):
    return lax.ppermute(value, axes, [(i, (i + step) % count) for i in range(count)])


def along_z(value, step):
    return shift(value, Z, NZ, step)


def along_y(value, step):
    return shift(value, "y", NY, step)


def flip(value, axis):
    return lax.ppermute(value, axis, [(0, 1), (1, 0)])


def across(value, axis):
    return lax.all_to_all(value, axis, split_axis=0, concat_axis=0, tiled=True)


def fence(*values):
    return lax.optimization_barrier(values)


def call(kernel, outs, in_specs, out_specs, name, scratch=(), cost=None):
    return pl.pallas_call(
        kernel,
        out_shape=outs,
        in_specs=in_specs,
        out_specs=out_specs,
        scratch_shapes=scratch,
        compiler_params=pltpu.CompilerParams(vmem_limit_bytes=LIMIT),
        cost_estimate=cost,
        name=name,
    )


def shape(*dims, dtype=BF):
    return jax.ShapeDtypeStruct(dims, dtype)


def prep_kernel(tokens_ref, gain_ref, ids_ref, weights_ref, out_ref):
    values = tokens_ref[...].astype(F32)
    scale = lax.rsqrt(jnp.mean(values * values, axis=-1, keepdims=True) + 1e-06)
    out_ref[pl.ds(0, ROWS), :] = (values * scale * gain_ref[...]).astype(BF)
    out_ref[pl.ds(ROWS, META), :] = jnp.full((META, WIDTH), -1.0, BF)
    out_ref[pl.ds(ROWS, META), 0:ROWS] = ids_ref[...].astype(F32).astype(BF)
    out_ref[pl.ds(ROWS, META), 128 : 128 + ROWS] = weights_ref[...].astype(BF)


def pack_kernel(place_ref, gate_ref, up_ref, down_ref, own_ref, other_ref, first_ref):
    zl = place_ref[3]
    for out_ref, e in ((own_ref, zl), (other_ref, 1 - zl), (first_ref, 0)):
        out_ref[0:SHARD, 0:HIDDEN] = gate_ref[e]
        out_ref[0:SHARD, HIDDEN:SIDE] = up_ref[e]
        out_ref[SHARD : SHARD + DSHARD, :] = down_ref[e, :, 0:SIDE]
        for j in range(3):
            out_ref[SHARD + DSHARD : PACK, 512 * j : 512 * (j + 1)] = down_ref[
                e, 32 * j : 32 * (j + 1), SIDE:WIDTH
            ]


def unpack_kernel(kind_ref, *refs):
    gate_ref, up_ref, down_ref = refs[-3:]
    for kind, ref in zip((0, 1, 2, 4, 8, 16), refs):

        @pl.when(kind_ref[0] == kind)
        def _(ref=ref):
            gate_ref[...] = ref[0:SHARD, 0:HIDDEN]
            up_ref[...] = ref[0:SHARD, HIDDEN:SIDE]
            down_ref[:, 0:SIDE] = ref[SHARD : SHARD + DSHARD, :]
            for j in range(3):
                down_ref[32 * j : 32 * (j + 1), SIDE:WIDTH] = ref[
                    SHARD + DSHARD : PACK, 512 * j : 512 * (j + 1)
                ]


def dispatch_kernel(n, place_ref, *refs):
    sources, (out_ref, weight_ref) = refs[:n], refs[n:]
    zh, zl = place_ref[1], place_ref[3]
    before = lax.broadcasted_iota(jnp.int32, (128, 128), 0)
    after = lax.broadcasted_iota(jnp.int32, (128, 128), 1)
    upto = (before <= after).astype(F32).astype(BF)
    slot = (before & (MOST - 1)).astype(F32)
    for i, ref in enumerate(sources):
        ids = ref[ROWS : ROWS + META, 0:128].astype(F32)
        route = ref[ROWS : ROWS + META, 128:256].astype(F32)
        chosen, factor = [], []
        for p in range(PLACES):
            expert = ((p // NC * NZH + zh) * NC + p % NC) * NZL + zl
            named = jnp.where(ids == expert.astype(F32), 1.0, 0.0)
            chosen.append(jnp.sum(named, axis=0, keepdims=True))
            factor.append(jnp.sum(named * route, axis=0, keepdims=True))
        chosen = jnp.concatenate(chosen, axis=0)
        factor = jnp.concatenate(factor, axis=0)
        ranks = jnp.dot(chosen.astype(BF), upto, preferred_element_type=F32) - 1.0
        ranks = jnp.where(chosen > 0.0, ranks, -1.0)

        def spread(v):
            return jnp.broadcast_to(v[:, None, :], (PLACES, MOST, 128)).reshape(128, 128)

        taken = spread(ranks) == slot
        placing = jnp.where(taken, 1.0, 0.0).astype(BF)
        rows = jnp.dot(placing[:, 0:ROWS], ref[0:ROWS, :], preferred_element_type=F32).astype(BF)
        for p in range(PLACES):
            at = (p * n + i) * MOST
            out_ref[at : at + MOST, :] = rows[p * MOST : (p + 1) * MOST]
        weight_ref[i] = jnp.where(taken, spread(factor), 0.0).T.astype(BF)


def dispatch(place, sources):
    n = len(sources)
    return call(
        functools.partial(dispatch_kernel, n),
        [shape(PLACES * n * MOST, WIDTH), shape(n, 128, 128)],
        [SMEM] + [VMEM] * n,
        [VMEM] * 2,
        "dispatch",
        cost=pl.CostEstimate(flops=0, transcendentals=0, bytes_accessed=80 << 20),
    )(place, *sources)


def ffn_kernel(splits, block, place_ref, own_ref, swap_ref, *refs):
    n = len(splits)
    row_refs, out_refs = refs[:n], refs[n : 2 * n]
    side_v, down_v, rows_v, res_v, sem_w, sem_r, sem_o = refs[2 * n :]
    zl = place_ref[3]
    loads, gets, puts, starts, at = [], [], [], [], 0

    def load(src, dst):
        cp = pltpu.make_async_copy(src, dst, sem_w.at[len(loads)])
        cp.start()
        loads.append(cp)

    for i, rows in enumerate(splits):
        starts.append(at)
        cp = pltpu.make_async_copy(row_refs[i], rows_v.at[pl.ds(at, rows)], sem_r.at[i])
        cp.start()
        gets.append(cp)
        at += rows
    total = at
    for src, from_zl in ((own_ref, zl), (swap_ref, 1 - zl)):
        for y in range(NY):
            holder = y * NZL + from_zl
            base = pl.multiple_of(holder * SHARD, SHARD)
            load(src.at[y, pl.ds(0, SHARD)], side_v.at[pl.ds(base, SHARD)])
            base = pl.multiple_of(holder * DSHARD, DSHARD)
            load(src.at[y, pl.ds(SHARD, DSHARD)], down_v.at[pl.ds(base, DSHARD), 0:SIDE])
            for j in range(3):
                load(
                    src.at[y, pl.ds(SHARD + DSHARD, 32), 512 * j : 512 * (j + 1)],
                    down_v.at[pl.ds(base + 32 * j, 32), SIDE:WIDTH],
                )
    for cp in gets:
        cp.wait()
    for cp in loads:
        cp.wait()

    @pl.loop(0, total // block)
    def _(step):
        at = pl.multiple_of(step * block, block)
        both = jnp.dot(rows_v[pl.ds(at, block), :], side_v[...], preferred_element_type=F32)
        gate, up = both[:, 0:HIDDEN], both[:, HIDDEN:SIDE]
        hidden = (gate / (1.0 + jnp.exp(-gate)) * up).astype(BF)
        res_v[pl.ds(at, block), :] = jnp.dot(
            hidden, down_v[...], preferred_element_type=F32
        ).astype(BF)

    for i, rows in enumerate(splits):
        cp = pltpu.make_async_copy(res_v.at[pl.ds(starts[i], rows)], out_refs[i], sem_o.at[i])
        cp.start()
        puts.append(cp)
    for cp in puts:
        cp.wait()


def ffn(place, own, swapped, groups, block):
    splits = tuple(g.shape[0] for g in groups)
    total = sum(splits)
    return call(
        functools.partial(ffn_kernel, splits, block),
        [shape(r, WIDTH) for r in splits],
        [SMEM] + [ANY] * (2 + len(groups)),
        [ANY] * len(groups),
        "expert_ffn",
        scratch=[
            pltpu.VMEM((WIDTH, SIDE), BF),
            pltpu.VMEM((HIDDEN, WIDTH), BF),
            pltpu.VMEM((total, WIDTH), BF),
            pltpu.VMEM((total, WIDTH), BF),
            pltpu.SemaphoreType.DMA((2 * NY * 5,)),
            pltpu.SemaphoreType.DMA((len(groups),)),
            pltpu.SemaphoreType.DMA((len(groups),)),
        ],
        cost=pl.CostEstimate(
            flops=6 * total * WIDTH * HIDDEN,
            transcendentals=total * HIDDEN,
            bytes_accessed=10 * WIDTH * HIDDEN,
        ),
    )(place, own, swapped, *groups)


def combine_kernel(n, weight_ref, back_ref, *outs):
    for i, out_ref in enumerate(outs):
        stack = jnp.concatenate(
            [back_ref[(p * n + i) * MOST : (p * n + i + 1) * MOST, :] for p in range(PLACES)],
            axis=0,
        )
        out_ref[...] = jnp.dot(
            weight_ref[i, 0:ROWS, :], stack, preferred_element_type=F32
        ).astype(out_ref.dtype)


def combine(weight, back, dtypes):
    n = len(dtypes)
    return call(
        functools.partial(combine_kernel, n),
        [shape(ROWS, WIDTH, dtype=t) for t in dtypes],
        [VMEM] * 2,
        [VMEM] * n,
        "combine",
    )(weight, back)


PLANE = ("x", "c")


def in_plane(rows):
    blocks = rows.reshape(PLACES, -1, WIDTH)
    return across(blocks, PLANE).reshape(-1, WIDTH)


def partner(value, axis, bit):
    count = {"x": NX, "zh": NZH, "c": NC, "zl": NZL}[axis]
    return lax.ppermute(value, axis, [(i, i ^ bit) for i in range(count)])


def joined(got, mine):
    return (got.astype(F32) + mine).astype(BF)


def body(
    tokens, norm_gain, expert_ids, route_weights, gate_weight, up_weight, down_weight, pair_list
):
    x_me, zh_me, c_me = (lax.axis_index(a) for a in EXPERT)
    zl_me = lax.axis_index("zl")
    place = jnp.stack([x_me, zh_me, c_me, zl_me]).astype(jnp.int32)

    near = call(prep_kernel, shape(ROWS + META, WIDTH), [VMEM] * 4, VMEM, "prep")(
        tokens, norm_gain[None, :], expert_ids.T, route_weights.T
    )
    near, place = fence(near, place)
    own, other, first = call(
        pack_kernel, [shape(PACK, SIDE)] * 3, [SMEM] + [VMEM] * 3, [VMEM] * 3, "pack"
    )(place, gate_weight, up_weight, down_weight)

    own_full = lax.all_gather(own, "y", axis=0, tiled=False)
    swapped = partner(other, "zl", 1)

    p1, m1 = along_z(near, 1), along_z(near, -1)
    p2, m2 = along_z(p1, 1), along_z(m1, -1)
    d0, w0 = dispatch(place, (near, p1, m1))
    r0 = in_plane(d0)
    hx1 = partner(first, "x", 1)
    p3, m3 = along_z(p2, 1), along_z(m2, -1)
    far = along_z(p3, 1)
    d1, w1 = dispatch(place, (p2, m2))
    d1, r0, hx1, p3, m3, first, swapped = fence(d1, r0, hx1, p3, m3, first, swapped)
    swap_full = lax.all_gather(swapped, "y", axis=0, tiled=False)
    r1 = in_plane(d1)
    d2, w2 = dispatch(place, (p3, m3, far))
    d2, r1, first = fence(d2, r1, first)
    r2 = in_plane(d2)
    hz1 = partner(first, "zh", 1)
    r0, r1, r2, first = fence(r0, r1, r2, first)
    hx2 = partner(first, "x", 2)
    r0, r1, r2, first, hz1, hx2, own_full, swap_full = fence(
        r0, r1, r2, first, hz1, hx2, own_full, swap_full
    )

    (s2,) = ffn(place, own_full, swap_full, (r2,), 384)
    hz2 = partner(first, "zh", 2)
    s2, r1, r0 = fence(s2, r1, r0)
    b2 = in_plane(s2)
    s1, s0 = ffn(place, own_full, swap_full, (r1, r0), 320)
    b2, s1, s0 = fence(b2, s1, s0)

    c_m3, c_p3, c_4 = combine(w2, b2, (F32, BF, BF))
    down, rise = along_z(c_4, -1), along_z(c_p3, 1)
    b1 = in_plane(s1)
    down = along_z(joined(down, c_m3), -1)
    b1, s0, rise, hz2, hx1, hz1, hx2, first = fence(b1, s0, rise, hz2, hx1, hz1, hx2, first)
    b0 = in_plane(s0)
    c_m2, c_p2 = combine(w1, b1, (F32, F32))
    down = along_z(joined(down, c_m2), -1)
    rise = along_z(joined(rise, c_p2), 1)

    hc = partner(first, "c", 1)
    me = (x_me * NZH + zh_me) * NC + c_me
    bits = jnp.sum(jnp.where(jnp.arange(pair_list.shape[0]) == me, pair_list ^ me, 0))
    new = call(
        unpack_kernel,
        [shape(SHARD, HIDDEN), shape(SHARD, HIDDEN), shape(DSHARD, WIDTH)],
        [SMEM] + [VMEM] * 6,
        [VMEM] * 3,
        "unpack",
    )(bits.astype(jnp.int32).reshape(1), first, hc, hz1, hz2, hx1, hx2)

    c_0, c_m1, c_p1 = combine(w0, b0, (F32, F32, F32))
    down = along_z(joined(down, c_m1), -1)
    rise = along_z(joined(rise, c_p1), 1)
    mixed = (down.astype(F32) + rise.astype(F32) + c_0).astype(BF)
    return (mixed, *(v[None] for v in new))


def solution(mesh):
    split = Mesh(mesh.devices.reshape(NX, NZH, NC, NY, NZL), EXPERT_DP)
    rows = P(EXPERT_DP, None)
    blocks = P(EXPERT, DP, None)
    return jax.shard_map(
        body,
        mesh=split,
        in_specs=(rows, P(), rows, rows, blocks, blocks, blocks, P()),
        out_specs=(rows, blocks, blocks, blocks),
        check_vma=False,
    )
```

```python
import functools

import jax
import jax.numpy as jnp
from jax import lax
from jax.experimental import pallas as pl
from jax.experimental.pallas import tpu as pltpu
from jax.sharding import Mesh
from jax.sharding import PartitionSpec as P

EXPERT = ("x", "zh", "c")
DP = ("y", "zl")
Z = ("zh", "zl")
EXPERT_DP = EXPERT + DP
MOST = 16
NX, NZH, NC, NY, NZL = 4, 4, 2, 4, 2
NZ = NZH * NZL
PLACES = NX * NC
ROWS, TOP, WIDTH, HIDDEN = 96, 8, 2048, 768
META = 8
SHARD, DSHARD = 256, 96
PACK = 384
HALF = PACK // 2
SIDE = 2 * HIDDEN
PIECE = PACK // NZH
BF = jnp.bfloat16
F32 = jnp.float32
GROUPS = ((0, -1, 1), (-2, 2), (-3, 3, 4))
VMEM = pl.BlockSpec(memory_space=pltpu.VMEM)
SMEM = pl.BlockSpec(memory_space=pltpu.SMEM)
HBM = pl.BlockSpec(memory_space=pltpu.HBM)
LIMIT = 48 << 20


def shift(value, axes, count, step):
    return lax.ppermute(value, axes, [(i, (i + step) % count) for i in range(count)])


def along_z(value, step):
    return shift(value, Z, NZ, step)


def along_y(value, step):
    return shift(value, "y", NY, step)


def flip(value, axis):
    return lax.ppermute(value, axis, [(0, 1), (1, 0)])


def across(value, axis):
    return lax.all_to_all(value, axis, split_axis=0, concat_axis=0, tiled=True)


def fence(*values):
    return lax.optimization_barrier(values)


def call(kernel, outs, in_specs, out_specs, name, scratch=(), cost=None):
    return pl.pallas_call(
        kernel,
        out_shape=outs,
        in_specs=in_specs,
        out_specs=out_specs,
        scratch_shapes=scratch,
        compiler_params=pltpu.CompilerParams(vmem_limit_bytes=LIMIT),
        cost_estimate=cost,
        name=name,
    )


def shape(*dims, dtype=BF):
    return jax.ShapeDtypeStruct(dims, dtype)


def prep_kernel(
    place_ref, tokens_ref, gain_ref, ids_ref, route_ref, gate_ref, up_ref, down_ref,
    out_ref, own_ref, other_ref, first_ref, tokens_v, gain_v, ids_v, route_v, sem_a, sem_b,
):
    zl = place_ref[3]
    reads, moves = [], []
    for src, dst in (
        (tokens_ref, tokens_v), (gain_ref, gain_v), (ids_ref, ids_v), (route_ref, route_v),
    ):
        cp = pltpu.make_async_copy(src, dst, sem_a.at[len(reads)])
        cp.start()
        reads.append(cp)

    def move(src, dst):
        cp = pltpu.make_async_copy(src, dst, sem_b.at[len(moves)])
        cp.start()
        moves.append(cp)

    for pack_ref, e in ((own_ref, zl), (other_ref, 1 - zl), (first_ref, 0)):
        move(gate_ref.at[e], pack_ref.at[pl.ds(0, SHARD), 0:HIDDEN])
        move(up_ref.at[e], pack_ref.at[pl.ds(0, SHARD), HIDDEN:SIDE])
        move(down_ref.at[e, :, 0:SIDE], pack_ref.at[pl.ds(SHARD, DSHARD), :])
        for j in range(3):
            move(
                down_ref.at[e, pl.ds(32 * j, 32), SIDE:WIDTH],
                pack_ref.at[pl.ds(SHARD + DSHARD, 32), 512 * j : 512 * (j + 1)],
            )
    for cp in reads:
        cp.wait()
    values = tokens_v[...].astype(F32)
    scale = lax.rsqrt(jnp.mean(values * values, axis=-1, keepdims=True) + 1e-06)
    out_ref[pl.ds(0, ROWS), :] = (values * scale * gain_v[...]).astype(BF)
    out_ref[pl.ds(ROWS, META), :] = jnp.full((META, WIDTH), -1.0, BF)
    out_ref[pl.ds(ROWS, META), 0:ROWS] = ids_v[...].astype(F32).astype(BF)
    out_ref[pl.ds(ROWS, META), 128 : 128 + ROWS] = route_v[...].astype(BF)
    for cp in moves:
        cp.wait()


def cut_kernel(place_ref, first_ref, *refs):
    outs, sem = refs[:-1], refs[-1]
    copies = []
    for k, out_ref in enumerate(outs):
        at = pl.multiple_of(((place_ref[1] + k) & (NZH - 1)) * PIECE, PIECE)
        cp = pltpu.make_async_copy(first_ref.at[pl.ds(at, PIECE)], out_ref, sem.at[k])
        cp.start()
        copies.append(cp)
    for cp in copies:
        cp.wait()


def pick_kernel(chosen_ref, *refs):
    pieces, outs, sem = refs[:NZH], refs[NZH : 2 * NZH], refs[-1]
    for k, out_ref in enumerate(outs):
        for j, piece in enumerate(pieces):

            @pl.when(chosen_ref[k] == j)
            def _(piece=piece, out_ref=out_ref, k=k):
                pltpu.make_async_copy(piece, out_ref, sem.at[k]).start()

    for k, out_ref in enumerate(outs):
        pltpu.make_async_copy(pieces[0], out_ref, sem.at[k]).wait()


def unpack_kernel(kind_ref, place_ref, *refs):
    whole, pieces, refs = refs[:4], refs[4 : 4 + NZH], refs[4 + NZH :]
    gate_ref, up_ref, down_ref, block, sem = refs
    for kinds, ref in zip(((0,), (1,), (8,), (16,)), whole):

        @pl.when(kind_ref[0] == kinds[0])
        def _(ref=ref):
            cp = pltpu.make_async_copy(ref, block, sem.at[NZH])
            cp.start()
            cp.wait()

    @pl.when((kind_ref[0] == 2) | (kind_ref[0] == 4))
    def _():
        copies = []
        for k, ref in enumerate(pieces):
            at = pl.multiple_of(((place_ref[1] - k) & (NZH - 1)) * PIECE, PIECE)
            cp = pltpu.make_async_copy(ref, block.at[pl.ds(at, PIECE)], sem.at[k])
            cp.start()
            copies.append(cp)
        for cp in copies:
            cp.wait()

    gate_ref[...] = block[0:SHARD, 0:HIDDEN]
    up_ref[...] = block[0:SHARD, HIDDEN:SIDE]
    down_ref[:, 0:SIDE] = block[SHARD : SHARD + DSHARD, :]
    for j in range(3):
        down_ref[32 * j : 32 * (j + 1), SIDE:WIDTH] = block[
            SHARD + DSHARD : PACK, 512 * j : 512 * (j + 1)
        ]


def dispatch_kernel(n, place_ref, *refs):
    sources, (out_ref, weight_ref) = refs[:n], refs[n:]
    zh, zl = place_ref[1], place_ref[3]
    before = lax.broadcasted_iota(jnp.int32, (128, 128), 0)
    after = lax.broadcasted_iota(jnp.int32, (128, 128), 1)
    upto = (before <= after).astype(F32).astype(BF)
    slot = (before & (MOST - 1)).astype(F32)
    for i, ref in enumerate(sources):
        ids = ref[ROWS : ROWS + META, 0:128].astype(F32)
        route = ref[ROWS : ROWS + META, 128:256].astype(F32)
        chosen, factor = [], []
        for p in range(PLACES):
            expert = ((p // NC * NZH + zh) * NC + p % NC) * NZL + zl
            named = jnp.where(ids == expert.astype(F32), 1.0, 0.0)
            chosen.append(jnp.sum(named, axis=0, keepdims=True))
            factor.append(jnp.sum(named * route, axis=0, keepdims=True))
        chosen = jnp.concatenate(chosen, axis=0)
        factor = jnp.concatenate(factor, axis=0)
        ranks = jnp.dot(chosen.astype(BF), upto, preferred_element_type=F32) - 1.0
        ranks = jnp.where(chosen > 0.0, ranks, -1.0)

        def spread(v):
            return jnp.broadcast_to(v[:, None, :], (PLACES, MOST, 128)).reshape(128, 128)

        taken = spread(ranks) == slot
        placing = jnp.where(taken, 1.0, 0.0).astype(BF)
        rows = jnp.dot(placing[:, 0:ROWS], ref[0:ROWS, :], preferred_element_type=F32).astype(BF)
        for p in range(PLACES):
            at = (p * n + i) * MOST
            out_ref[at : at + MOST, :] = rows[p * MOST : (p + 1) * MOST]
        weight_ref[i] = jnp.where(taken, spread(factor), 0.0).T.astype(BF)


def dispatch(place, sources):
    n = len(sources)
    return call(
        functools.partial(dispatch_kernel, n),
        [shape(PLACES * n * MOST, WIDTH), shape(n, 128, 128)],
        [SMEM] + [VMEM] * n,
        [VMEM] * 2,
        "dispatch",
        cost=pl.CostEstimate(flops=0, transcendentals=0, bytes_accessed=80 << 20),
    )(place, *sources)


def ffn_kernel(splits, block, place_ref, own_ref, swap_ref, *refs):
    n = len(splits)
    row_refs, out_refs = refs[:n], refs[n : 2 * n]
    side_v, down_v, rows_v, res_v, sem_w, sem_r, sem_o = refs[2 * n :]
    zl = place_ref[3]
    loads, gets, puts, starts, at = [], [], [], [], 0

    def load(src, dst):
        cp = pltpu.make_async_copy(src, dst, sem_w.at[len(loads)])
        cp.start()
        loads.append(cp)

    for i, rows in enumerate(splits):
        starts.append(at)
        cp = pltpu.make_async_copy(row_refs[i], rows_v.at[pl.ds(at, rows)], sem_r.at[i])
        cp.start()
        gets.append(cp)
        at += rows
    total = at
    for src, from_zl in ((own_ref, zl), (swap_ref, 1 - zl)):
        for y in range(NY):
            holder = y * NZL + from_zl
            base = pl.multiple_of(holder * SHARD, SHARD)
            load(src.at[y, pl.ds(0, SHARD)], side_v.at[pl.ds(base, SHARD)])
            base = pl.multiple_of(holder * DSHARD, DSHARD)
            load(src.at[y, pl.ds(SHARD, DSHARD)], down_v.at[pl.ds(base, DSHARD), 0:SIDE])
            for j in range(3):
                load(
                    src.at[y, pl.ds(SHARD + DSHARD, 32), 512 * j : 512 * (j + 1)],
                    down_v.at[pl.ds(base + 32 * j, 32), SIDE:WIDTH],
                )
    for cp in gets:
        cp.wait()
    for cp in loads:
        cp.wait()

    @pl.loop(0, total // block)
    def _(step):
        at = pl.multiple_of(step * block, block)
        both = jnp.dot(rows_v[pl.ds(at, block), :], side_v[...], preferred_element_type=F32)
        gate, up = both[:, 0:HIDDEN], both[:, HIDDEN:SIDE]
        hidden = (gate / (1.0 + jnp.exp(-gate)) * up).astype(BF)
        res_v[pl.ds(at, block), :] = jnp.dot(
            hidden, down_v[...], preferred_element_type=F32
        ).astype(BF)

    for i, rows in enumerate(splits):
        cp = pltpu.make_async_copy(res_v.at[pl.ds(starts[i], rows)], out_refs[i], sem_o.at[i])
        cp.start()
        puts.append(cp)
    for cp in puts:
        cp.wait()


def ffn(place, own, swapped, groups, block):
    splits = tuple(g.shape[0] for g in groups)
    total = sum(splits)
    return call(
        functools.partial(ffn_kernel, splits, block),
        [shape(r, WIDTH) for r in splits],
        [SMEM] + [HBM] * (2 + len(groups)),
        [HBM] * len(groups),
        "expert_ffn",
        scratch=[
            pltpu.VMEM((WIDTH, SIDE), BF),
            pltpu.VMEM((HIDDEN, WIDTH), BF),
            pltpu.VMEM((total, WIDTH), BF),
            pltpu.VMEM((total, WIDTH), BF),
            pltpu.SemaphoreType.DMA((2 * NY * 5,)),
            pltpu.SemaphoreType.DMA((len(groups),)),
            pltpu.SemaphoreType.DMA((len(groups),)),
        ],
        cost=pl.CostEstimate(
            flops=6 * total * WIDTH * HIDDEN,
            transcendentals=total * HIDDEN,
            bytes_accessed=10 * WIDTH * HIDDEN,
        ),
    )(place, own, swapped, *groups)


def combine_kernel(n, weight_ref, back_ref, *outs):
    for i, out_ref in enumerate(outs):
        stack = jnp.concatenate(
            [back_ref[(p * n + i) * MOST : (p * n + i + 1) * MOST, :] for p in range(PLACES)],
            axis=0,
        )
        out_ref[...] = jnp.dot(
            weight_ref[i, 0:ROWS, :], stack, preferred_element_type=F32
        ).astype(out_ref.dtype)


def combine(weight, back, dtypes):
    n = len(dtypes)
    return call(
        functools.partial(combine_kernel, n),
        [shape(ROWS, WIDTH, dtype=t) for t in dtypes],
        [VMEM] * 2,
        [VMEM] * n,
        "combine",
    )(weight, back)


PLANE = ("x", "c")


def in_plane(rows):
    blocks = rows.reshape(PLACES, -1, WIDTH)
    return across(blocks, PLANE).reshape(-1, WIDTH)


def partner(value, axis, bit):
    count = {"x": NX, "zh": NZH, "c": NC, "zl": NZL}[axis]
    return lax.ppermute(value, axis, [(i, i ^ bit) for i in range(count)])


def joined(got, mine):
    return (got.astype(F32) + mine).astype(BF)


def body(
    tokens, norm_gain, expert_ids, route_weights, gate_weight, up_weight, down_weight, pair_list
):
    x_me, zh_me, c_me = (lax.axis_index(a) for a in EXPERT)
    zl_me = lax.axis_index("zl")
    place = jnp.stack([x_me, zh_me, c_me, zl_me]).astype(jnp.int32)

    near, own, other, first = call(
        prep_kernel,
        [shape(ROWS + META, WIDTH)] + [shape(PACK, SIDE)] * 3,
        [SMEM] + [HBM] * 7,
        [VMEM] + [HBM] * 3,
        "prep",
        scratch=[
            pltpu.VMEM((ROWS, WIDTH), BF),
            pltpu.VMEM((1, WIDTH), F32),
            pltpu.VMEM((TOP, ROWS), jnp.int32),
            pltpu.VMEM((TOP, ROWS), F32),
            pltpu.SemaphoreType.DMA((4,)),
            pltpu.SemaphoreType.DMA((18,)),
        ],
    )(
        place, tokens, norm_gain[None, :], expert_ids.T, route_weights.T,
        gate_weight, up_weight, down_weight,
    )

    own_full = lax.all_gather(own, "y", axis=0, tiled=False)
    swapped = partner(other, "zl", 1)

    p1, m1 = along_z(near, 1), along_z(near, -1)
    p2, m2 = along_z(p1, 1), along_z(m1, -1)
    d0, w0 = dispatch(place, (near, p1, m1))
    hx1 = partner(first, "x", 1)
    d0, hx1, swapped = fence(d0, hx1, swapped)
    swap_full = lax.all_gather(swapped, "y", axis=0, tiled=False)
    r0 = in_plane(d0)
    p3, m3 = along_z(p2, 1), along_z(m2, -1)
    d1, w1 = dispatch(place, (p2, m2))
    d1, r0, p3, m3 = fence(d1, r0, p3, m3)
    r1 = in_plane(d1)
    far = along_z(p3, 1)
    far, first = fence(far, first)
    cut = call(
        cut_kernel, [shape(PIECE, SIDE)] * NZH, [SMEM, HBM], [HBM] * NZH, "cut",
        scratch=[pltpu.SemaphoreType.DMA((NZH,))],
    )(place, first)
    held = [cut[0]] + [shift(cut[k], "zh", NZH, k) for k in range(1, NZH)]
    d2, w2 = dispatch(place, (p3, m3, far))
    d2, r1 = fence(d2, r1)
    r2 = in_plane(d2)
    r0, r1, r2, first, *held = fence(r0, r1, r2, first, *held)

    (s2,) = ffn(place, own_full, swap_full, (r2,), 384)
    s2, r1, r0, *held = fence(s2, r1, r0, *held)
    b2 = in_plane(s2)
    s1, s0 = ffn(place, own_full, swap_full, (r1, r0), 320)
    turn = (zh_me + jnp.arange(NZH, dtype=jnp.int32)) & (NZH - 1)
    matched = jnp.take(pair_list, (x_me * NZH + turn) * NC + c_me, mode="clip")
    chosen = (zh_me - (matched >> 1)) & (NZH - 1)
    picked = call(
        pick_kernel, [shape(PIECE, SIDE)] * NZH, [SMEM] + [HBM] * NZH, [HBM] * NZH, "pick",
        scratch=[pltpu.SemaphoreType.DMA((NZH,))],
    )(chosen.astype(jnp.int32), *held)
    held = [picked[0]] + [shift(picked[k], "zh", NZH, k) for k in range(1, NZH)]
    b2, s1, s0, *held = fence(b2, s1, s0, *held)

    c_m3, c_p3, c_4 = combine(w2, b2, (F32, BF, BF))
    down, rise = along_z(c_4, -1), along_z(c_p3, 1)
    b1 = in_plane(s1)
    down = along_z(joined(down, c_m3), -1)
    b1, s0, rise = fence(b1, s0, rise)
    b0 = in_plane(s0)
    c_m2, c_p2 = combine(w1, b1, (F32, F32))
    down = along_z(joined(down, c_m2), -1)
    rise = along_z(joined(rise, c_p2), 1)
    b0, first, hx1, *held = fence(b0, first, hx1, *held)

    hx2 = partner(first, "x", 2)
    hc = partner(first, "c", 1)
    me = (x_me * NZH + zh_me) * NC + c_me
    bits = jnp.sum(jnp.where(jnp.arange(pair_list.shape[0]) == me, pair_list ^ me, 0))
    new = call(
        unpack_kernel,
        [shape(SHARD, HIDDEN), shape(SHARD, HIDDEN), shape(DSHARD, WIDTH)],
        [SMEM] * 2 + [HBM] * 8,
        [VMEM] * 3,
        "unpack",
        scratch=[pltpu.VMEM((PACK, SIDE), BF), pltpu.SemaphoreType.DMA((NZH + 1,))],
    )(bits.astype(jnp.int32).reshape(1), place, first, hc, hx1, hx2, *held)

    c_0, c_m1, c_p1 = combine(w0, b0, (F32, F32, F32))
    down = along_z(joined(down, c_m1), -1)
    rise = along_z(joined(rise, c_p1), 1)
    mixed = (down.astype(F32) + rise.astype(F32) + c_0).astype(BF)
    return (mixed, *(v[None] for v in new))


def solution(mesh):
    split = Mesh(mesh.devices.reshape(NX, NZH, NC, NY, NZL), EXPERT_DP)
    rows = P(EXPERT_DP, None)
    blocks = P(EXPERT, DP, None)
    return jax.shard_map(
        body,
        mesh=split,
        in_specs=(rows, P(), rows, rows, blocks, blocks, blocks, P()),
        out_specs=(rows, blocks, blocks, blocks),
        check_vma=False,
    )
```

```python
import functools

import jax
import jax.numpy as jnp
from jax import lax
from jax.experimental import pallas as pl
from jax.experimental.pallas import tpu as pltpu
from jax.sharding import Mesh
from jax.sharding import PartitionSpec as P

EXPERT = ("x", "zh", "c")
DP = ("y", "zl")
Z = ("zh", "zl")
EXPERT_DP = EXPERT + DP
MOST = 16
NX, NZH, NC, NY, NZL = 4, 4, 2, 4, 2
NZ = NZH * NZL
PLACES = NX * NC
ROWS, TOP, WIDTH, HIDDEN = 96, 8, 2048, 768
META = 8
SHARD, DSHARD = 256, 96
PACK = 384
HALF = PACK // 2
SIDE = 2 * HIDDEN
PIECE = PACK // NZH
BF = jnp.bfloat16
F32 = jnp.float32
GROUPS = ((0, -1, 1), (-2, 2), (-3, 3, 4))
VMEM = pl.BlockSpec(memory_space=pltpu.VMEM)
SMEM = pl.BlockSpec(memory_space=pltpu.SMEM)
HBM = pl.BlockSpec(memory_space=pltpu.HBM)
LIMIT = 48 << 20


def shift(value, axes, count, step):
    return lax.ppermute(value, axes, [(i, (i + step) % count) for i in range(count)])


def along_z(value, step):
    return shift(value, Z, NZ, step)


def along_y(value, step):
    return shift(value, "y", NY, step)


def flip(value, axis):
    return lax.ppermute(value, axis, [(0, 1), (1, 0)])


def across(value, axis):
    return lax.all_to_all(value, axis, split_axis=0, concat_axis=0, tiled=True)


def fence(*values):
    return lax.optimization_barrier(values)


def call(kernel, outs, in_specs, out_specs, name, scratch=(), cost=None):
    return pl.pallas_call(
        kernel,
        out_shape=outs,
        in_specs=in_specs,
        out_specs=out_specs,
        scratch_shapes=scratch,
        compiler_params=pltpu.CompilerParams(vmem_limit_bytes=LIMIT),
        cost_estimate=cost,
        name=name,
    )


def shape(*dims, dtype=BF):
    return jax.ShapeDtypeStruct(dims, dtype)


def prep_kernel(
    place_ref, tokens_ref, gain_ref, ids_ref, route_ref, gate_ref, up_ref, down_ref,
    out_ref, own_ref, other_ref, first_ref, tokens_v, gain_v, ids_v, route_v, sem_a, sem_b,
):
    zl = place_ref[3]
    reads, moves = [], []
    for src, dst in (
        (tokens_ref, tokens_v), (gain_ref, gain_v), (ids_ref, ids_v), (route_ref, route_v),
    ):
        cp = pltpu.make_async_copy(src, dst, sem_a.at[len(reads)])
        cp.start()
        reads.append(cp)

    def move(src, dst):
        cp = pltpu.make_async_copy(src, dst, sem_b.at[len(moves)])
        cp.start()
        moves.append(cp)

    for pack_ref, e in ((own_ref, zl), (other_ref, 1 - zl), (first_ref, 0)):
        move(gate_ref.at[e], pack_ref.at[pl.ds(0, SHARD), 0:HIDDEN])
        move(up_ref.at[e], pack_ref.at[pl.ds(0, SHARD), HIDDEN:SIDE])
        move(down_ref.at[e, :, 0:SIDE], pack_ref.at[pl.ds(SHARD, DSHARD), :])
        for j in range(3):
            move(
                down_ref.at[e, pl.ds(32 * j, 32), SIDE:WIDTH],
                pack_ref.at[pl.ds(SHARD + DSHARD, 32), 512 * j : 512 * (j + 1)],
            )
    for cp in reads:
        cp.wait()
    values = tokens_v[...].astype(F32)
    scale = lax.rsqrt(jnp.mean(values * values, axis=-1, keepdims=True) + 1e-06)
    out_ref[pl.ds(0, ROWS), :] = (values * scale * gain_v[...]).astype(BF)
    out_ref[pl.ds(ROWS, META), :] = jnp.full((META, WIDTH), -1.0, BF)
    out_ref[pl.ds(ROWS, META), 0:ROWS] = ids_v[...].astype(F32).astype(BF)
    out_ref[pl.ds(ROWS, META), 128 : 128 + ROWS] = route_v[...].astype(BF)
    for cp in moves:
        cp.wait()


def cut_kernel(place_ref, first_ref, *refs):
    outs, sem = refs[:-1], refs[-1]
    copies = []
    for k, out_ref in enumerate(outs):
        at = pl.multiple_of(((place_ref[1] + k) & (NZH - 1)) * PIECE, PIECE)
        cp = pltpu.make_async_copy(first_ref.at[pl.ds(at, PIECE)], out_ref, sem.at[k])
        cp.start()
        copies.append(cp)
    for cp in copies:
        cp.wait()


def pick_kernel(chosen_ref, *refs):
    pieces, outs, sem = refs[:NZH], refs[NZH : 2 * NZH], refs[-1]
    for k, out_ref in enumerate(outs):
        for j, piece in enumerate(pieces):

            @pl.when(chosen_ref[k] == j)
            def _(piece=piece, out_ref=out_ref, k=k):
                pltpu.make_async_copy(piece, out_ref, sem.at[k]).start()

    for k, out_ref in enumerate(outs):
        pltpu.make_async_copy(pieces[0], out_ref, sem.at[k]).wait()


def unpack_kernel(kind_ref, place_ref, *refs):
    whole, pieces, refs = refs[:4], refs[4 : 4 + NZH], refs[4 + NZH :]
    gate_ref, up_ref, down_ref, block, sem = refs
    for kinds, ref in zip(((0,), (1,), (8,), (16,)), whole):

        @pl.when(kind_ref[0] == kinds[0])
        def _(ref=ref):
            cp = pltpu.make_async_copy(ref, block, sem.at[NZH])
            cp.start()
            cp.wait()

    @pl.when((kind_ref[0] == 2) | (kind_ref[0] == 4))
    def _():
        copies = []
        for k, ref in enumerate(pieces):
            at = pl.multiple_of(((place_ref[1] - k) & (NZH - 1)) * PIECE, PIECE)
            cp = pltpu.make_async_copy(ref, block.at[pl.ds(at, PIECE)], sem.at[k])
            cp.start()
            copies.append(cp)
        for cp in copies:
            cp.wait()

    gate_ref[...] = block[0:SHARD, 0:HIDDEN]
    up_ref[...] = block[0:SHARD, HIDDEN:SIDE]
    down_ref[:, 0:SIDE] = block[SHARD : SHARD + DSHARD, :]
    for j in range(3):
        down_ref[32 * j : 32 * (j + 1), SIDE:WIDTH] = block[
            SHARD + DSHARD : PACK, 512 * j : 512 * (j + 1)
        ]


def dispatch_kernel(n, place_ref, *refs):
    sources, (out_ref, weight_ref) = refs[:n], refs[n:]
    zh, zl = place_ref[1], place_ref[3]
    before = lax.broadcasted_iota(jnp.int32, (128, 128), 0)
    after = lax.broadcasted_iota(jnp.int32, (128, 128), 1)
    upto = (before <= after).astype(F32).astype(BF)
    slot = (before & (MOST - 1)).astype(F32)
    for i, ref in enumerate(sources):
        ids = ref[ROWS : ROWS + META, 0:128].astype(F32)
        route = ref[ROWS : ROWS + META, 128:256].astype(F32)
        chosen, factor = [], []
        for p in range(PLACES):
            expert = ((p // NC * NZH + zh) * NC + p % NC) * NZL + zl
            named = jnp.where(ids == expert.astype(F32), 1.0, 0.0)
            chosen.append(jnp.sum(named, axis=0, keepdims=True))
            factor.append(jnp.sum(named * route, axis=0, keepdims=True))
        chosen = jnp.concatenate(chosen, axis=0)
        factor = jnp.concatenate(factor, axis=0)
        ranks = jnp.dot(chosen.astype(BF), upto, preferred_element_type=F32) - 1.0
        ranks = jnp.where(chosen > 0.0, ranks, -1.0)

        def spread(v):
            return jnp.broadcast_to(v[:, None, :], (PLACES, MOST, 128)).reshape(128, 128)

        taken = spread(ranks) == slot
        placing = jnp.where(taken, 1.0, 0.0).astype(BF)
        rows = jnp.dot(placing[:, 0:ROWS], ref[0:ROWS, :], preferred_element_type=F32).astype(BF)
        for p in range(PLACES):
            at = (p * n + i) * MOST
            out_ref[at : at + MOST, :] = rows[p * MOST : (p + 1) * MOST]
        weight_ref[i] = jnp.where(taken, spread(factor), 0.0).T.astype(BF)


def dispatch(place, sources):
    n = len(sources)
    return call(
        functools.partial(dispatch_kernel, n),
        [shape(PLACES * n * MOST, WIDTH), shape(n, 128, 128)],
        [SMEM] + [VMEM] * n,
        [VMEM] * 2,
        "dispatch",
        cost=pl.CostEstimate(flops=0, transcendentals=0, bytes_accessed=80 << 20),
    )(place, *sources)


def ffn_kernel(splits, block, place_ref, own_ref, swap_ref, *refs):
    n = len(splits)
    row_refs, out_refs = refs[:n], refs[n : 2 * n]
    side_v, down_v, rows_v, res_v, sem_w, sem_r, sem_o = refs[2 * n :]
    zl = place_ref[3]
    loads, gets, puts, starts, at = [], [], [], [], 0

    def load(src, dst):
        cp = pltpu.make_async_copy(src, dst, sem_w.at[len(loads)])
        cp.start()
        loads.append(cp)

    for i, rows in enumerate(splits):
        starts.append(at)
        cp = pltpu.make_async_copy(row_refs[i], rows_v.at[pl.ds(at, rows)], sem_r.at[i])
        cp.start()
        gets.append(cp)
        at += rows
    total = at
    for src, from_zl in ((own_ref, zl), (swap_ref, 1 - zl)):
        for y in range(NY):
            holder = y * NZL + from_zl
            base = pl.multiple_of(holder * SHARD, SHARD)
            load(src.at[y, pl.ds(0, SHARD)], side_v.at[pl.ds(base, SHARD)])
            base = pl.multiple_of(holder * DSHARD, DSHARD)
            load(src.at[y, pl.ds(SHARD, DSHARD)], down_v.at[pl.ds(base, DSHARD), 0:SIDE])
            for j in range(3):
                load(
                    src.at[y, pl.ds(SHARD + DSHARD, 32), 512 * j : 512 * (j + 1)],
                    down_v.at[pl.ds(base + 32 * j, 32), SIDE:WIDTH],
                )
    for cp in gets:
        cp.wait()
    for cp in loads:
        cp.wait()

    @pl.loop(0, total // block)
    def _(step):
        at = pl.multiple_of(step * block, block)
        both = jnp.dot(rows_v[pl.ds(at, block), :], side_v[...], preferred_element_type=F32)
        gate, up = both[:, 0:HIDDEN], both[:, HIDDEN:SIDE]
        hidden = (gate / (1.0 + jnp.exp(-gate)) * up).astype(BF)
        res_v[pl.ds(at, block), :] = jnp.dot(
            hidden, down_v[...], preferred_element_type=F32
        ).astype(BF)

    for i, rows in enumerate(splits):
        cp = pltpu.make_async_copy(res_v.at[pl.ds(starts[i], rows)], out_refs[i], sem_o.at[i])
        cp.start()
        puts.append(cp)
    for cp in puts:
        cp.wait()


def ffn(place, own, swapped, groups, block):
    splits = tuple(g.shape[0] for g in groups)
    total = sum(splits)
    return call(
        functools.partial(ffn_kernel, splits, block),
        [pltpu.HBM((r, WIDTH), BF) for r in splits],
        [SMEM] + [HBM] * (2 + len(groups)),
        [HBM] * len(groups),
        "expert_ffn",
        scratch=[
            pltpu.VMEM((WIDTH, SIDE), BF),
            pltpu.VMEM((HIDDEN, WIDTH), BF),
            pltpu.VMEM((total, WIDTH), BF),
            pltpu.VMEM((total, WIDTH), BF),
            pltpu.SemaphoreType.DMA((2 * NY * 5,)),
            pltpu.SemaphoreType.DMA((len(groups),)),
            pltpu.SemaphoreType.DMA((len(groups),)),
        ],
        cost=pl.CostEstimate(
            flops=6 * total * WIDTH * HIDDEN,
            transcendentals=total * HIDDEN,
            bytes_accessed=10 * WIDTH * HIDDEN,
        ),
    )(place, own, swapped, *groups)


def combine_kernel(n, weight_ref, back_ref, *outs):
    for i, out_ref in enumerate(outs):
        stack = jnp.concatenate(
            [back_ref[(p * n + i) * MOST : (p * n + i + 1) * MOST, :] for p in range(PLACES)],
            axis=0,
        )
        out_ref[...] = jnp.dot(
            weight_ref[i, 0:ROWS, :], stack, preferred_element_type=F32
        ).astype(out_ref.dtype)


def combine(weight, back, dtypes):
    n = len(dtypes)
    return call(
        functools.partial(combine_kernel, n),
        [shape(ROWS, WIDTH, dtype=t) for t in dtypes],
        [VMEM] * 2,
        [VMEM] * n,
        "combine",
    )(weight, back)


PLANE = ("x", "c")


def in_plane(rows):
    blocks = rows.reshape(PLACES, -1, WIDTH)
    return across(blocks, PLANE).reshape(-1, WIDTH)


def partner(value, axis, bit):
    count = {"x": NX, "zh": NZH, "c": NC, "zl": NZL}[axis]
    return lax.ppermute(value, axis, [(i, i ^ bit) for i in range(count)])


def joined(got, mine):
    return (got.astype(F32) + mine).astype(BF)


def body(
    tokens, norm_gain, expert_ids, route_weights, gate_weight, up_weight, down_weight, pair_list
):
    x_me, zh_me, c_me = (lax.axis_index(a) for a in EXPERT)
    zl_me = lax.axis_index("zl")
    place = jnp.stack([x_me, zh_me, c_me, zl_me]).astype(jnp.int32)

    near, own, other, first = call(
        prep_kernel,
        [shape(ROWS + META, WIDTH)] + [shape(PACK, SIDE)] * 3,
        [SMEM] + [HBM] * 7,
        [VMEM] + [HBM] * 3,
        "prep",
        scratch=[
            pltpu.VMEM((ROWS, WIDTH), BF),
            pltpu.VMEM((1, WIDTH), F32),
            pltpu.VMEM((TOP, ROWS), jnp.int32),
            pltpu.VMEM((TOP, ROWS), F32),
            pltpu.SemaphoreType.DMA((4,)),
            pltpu.SemaphoreType.DMA((18,)),
        ],
    )(
        place, *(
            pltpu.with_memory_space_constraint(v, pltpu.HBM)
            for v in (
                tokens, norm_gain[None, :], expert_ids.T, route_weights.T,
                gate_weight, up_weight, down_weight,
            )
        )
    )

    own_full = lax.all_gather(own, "y", axis=0, tiled=False)

    p1, m1 = along_z(near, 1), along_z(near, -1)
    p1, m1, other = fence(p1, m1, other)
    swapped = partner(other, "zl", 1)
    p2, m2 = along_z(p1, 1), along_z(m1, -1)
    d0, w0 = dispatch(place, (near, p1, m1))
    hx1 = partner(first, "x", 1)
    d0, hx1 = fence(d0, hx1)
    r0 = in_plane(d0)
    p2, m2, swapped = fence(p2, m2, swapped)
    p3, m3 = along_z(p2, 1), along_z(m2, -1)
    d1, w1 = dispatch(place, (p2, m2))
    d1, r0, p3, m3, swapped = fence(d1, r0, p3, m3, swapped)
    swap_full = lax.all_gather(swapped, "y", axis=0, tiled=False)
    r1 = in_plane(d1)
    far = along_z(p3, 1)
    far, first = fence(far, first)
    cut = call(
        cut_kernel, [shape(PIECE, SIDE)] * NZH, [SMEM, HBM], [HBM] * NZH, "cut",
        scratch=[pltpu.SemaphoreType.DMA((NZH,))],
    )(place, first)
    held = [cut[0]] + [shift(cut[k], "zh", NZH, k) for k in range(1, NZH)]
    d2, w2 = dispatch(place, (p3, m3, far))
    d2, r1 = fence(d2, r1)
    r2 = in_plane(d2)
    r0, r1, r2, first, *held = fence(r0, r1, r2, first, *held)

    hx2 = partner(first, "x", 2)
    (s2,) = ffn(place, own_full, swap_full, (r2,), 384)
    s2, r1, r0, hx2, *held = fence(s2, r1, r0, hx2, *held)
    b2 = in_plane(s2)
    s1, s0 = ffn(place, own_full, swap_full, (r1, r0), 320)
    b2, s1, s0, *held = fence(b2, s1, s0, *held)
    turn = (zh_me + jnp.arange(NZH, dtype=jnp.int32)) & (NZH - 1)
    matched = jnp.take(pair_list, (x_me * NZH + turn) * NC + c_me, mode="clip")
    chosen = (zh_me - (matched >> 1)) & (NZH - 1)
    picked = call(
        pick_kernel, [shape(PIECE, SIDE)] * NZH, [SMEM] + [HBM] * NZH, [HBM] * NZH, "pick",
        scratch=[pltpu.SemaphoreType.DMA((NZH,))],
    )(chosen.astype(jnp.int32), *held)
    held = [picked[0]] + [shift(picked[k], "zh", NZH, k) for k in range(1, NZH)]

    c_m3, c_p3, c_4 = combine(w2, b2, (F32, BF, BF))
    down, rise = along_z(c_4, -1), along_z(c_p3, 1)
    b1 = in_plane(s1)
    down = along_z(joined(down, c_m3), -1)
    b1, s0, rise = fence(b1, s0, rise)
    b0 = in_plane(s0)
    c_m2, c_p2 = combine(w1, b1, (F32, F32))
    down = along_z(joined(down, c_m2), -1)
    rise = along_z(joined(rise, c_p2), 1)
    b0, first, hx1, *held = fence(b0, first, hx1, *held)

    hc = partner(first, "c", 1)
    me = (x_me * NZH + zh_me) * NC + c_me
    bits = jnp.sum(jnp.where(jnp.arange(pair_list.shape[0]) == me, pair_list ^ me, 0))
    new = call(
        unpack_kernel,
        [shape(SHARD, HIDDEN), shape(SHARD, HIDDEN), shape(DSHARD, WIDTH)],
        [SMEM] * 2 + [HBM] * 8,
        [VMEM] * 3,
        "unpack",
        scratch=[pltpu.VMEM((PACK, SIDE), BF), pltpu.SemaphoreType.DMA((NZH + 1,))],
    )(bits.astype(jnp.int32).reshape(1), place, first, hc, hx1, hx2, *held)

    c_0, c_m1, c_p1 = combine(w0, b0, (F32, F32, F32))
    down = along_z(joined(down, c_m1), -1)
    rise = along_z(joined(rise, c_p1), 1)
    mixed = (down.astype(F32) + rise.astype(F32) + c_0).astype(BF)
    return (mixed, *(v[None] for v in new))


def solution(mesh):
    split = Mesh(mesh.devices.reshape(NX, NZH, NC, NY, NZL), EXPERT_DP)
    rows = P(EXPERT_DP, None)
    blocks = P(EXPERT, DP, None)
    return jax.shard_map(
        body,
        mesh=split,
        in_specs=(rows, P(), rows, rows, blocks, blocks, blocks, P()),
        out_specs=(rows, blocks, blocks, blocks),
        check_vma=False,
    )
```

```python
import functools

import jax
import jax.numpy as jnp
from jax import lax
from jax.experimental import pallas as pl
from jax.experimental.pallas import tpu as pltpu
from jax.sharding import Mesh
from jax.sharding import PartitionSpec as P

EXPERT = ("x", "zh", "c")
DP = ("y", "zl")
Z = ("zh", "zl")
EXPERT_DP = EXPERT + DP
MOST = 16
NX, NZH, NC, NY, NZL = 4, 4, 2, 4, 2
NZ = NZH * NZL
PLACES = NX * NC
ROWS, TOP, WIDTH, HIDDEN = 96, 8, 2048, 768
META = 8
SHARD, DSHARD = 256, 96
PACK = 384
HALF = PACK // 2
SIDE = 2 * HIDDEN
PIECE = PACK // NZH
BF = jnp.bfloat16
F32 = jnp.float32
GROUPS = ((0, -1, 1), (-2, 2), (-3, 3, 4))
VMEM = pl.BlockSpec(memory_space=pltpu.VMEM)
SMEM = pl.BlockSpec(memory_space=pltpu.SMEM)
HBM = pl.BlockSpec(memory_space=pltpu.HBM)
LIMIT = 48 << 20


def shift(value, axes, count, step):
    return lax.ppermute(value, axes, [(i, (i + step) % count) for i in range(count)])


def along_z(value, step):
    return shift(value, Z, NZ, step)


def along_y(value, step):
    return shift(value, "y", NY, step)


def flip(value, axis):
    return lax.ppermute(value, axis, [(0, 1), (1, 0)])


def across(value, axis):
    return lax.all_to_all(value, axis, split_axis=0, concat_axis=0, tiled=True)


def fence(*values):
    return lax.optimization_barrier(values)


def call(kernel, outs, in_specs, out_specs, name, scratch=(), cost=None):
    return pl.pallas_call(
        kernel,
        out_shape=outs,
        in_specs=in_specs,
        out_specs=out_specs,
        scratch_shapes=scratch,
        compiler_params=pltpu.CompilerParams(vmem_limit_bytes=LIMIT),
        cost_estimate=cost,
        name=name,
    )


def shape(*dims, dtype=BF):
    return jax.ShapeDtypeStruct(dims, dtype)


def prep_kernel(
    place_ref, tokens_ref, gain_ref, ids_ref, route_ref, gate_ref, up_ref, down_ref,
    out_ref, own_ref, other_ref, first_ref, tokens_v, gain_v, ids_v, route_v, sem_a, sem_b,
):
    zl = place_ref[3]
    reads, moves = [], []
    for src, dst in (
        (tokens_ref, tokens_v), (gain_ref, gain_v), (ids_ref, ids_v), (route_ref, route_v),
    ):
        cp = pltpu.make_async_copy(src, dst, sem_a.at[len(reads)])
        cp.start()
        reads.append(cp)

    def move(src, dst):
        cp = pltpu.make_async_copy(src, dst, sem_b.at[len(moves)])
        cp.start()
        moves.append(cp)

    for pack_ref, e in ((own_ref, zl), (other_ref, 1 - zl), (first_ref, 0)):
        move(gate_ref.at[e], pack_ref.at[pl.ds(0, SHARD), 0:HIDDEN])
        move(up_ref.at[e], pack_ref.at[pl.ds(0, SHARD), HIDDEN:SIDE])
        move(down_ref.at[e, :, 0:SIDE], pack_ref.at[pl.ds(SHARD, DSHARD), :])
        for j in range(3):
            move(
                down_ref.at[e, pl.ds(32 * j, 32), SIDE:WIDTH],
                pack_ref.at[pl.ds(SHARD + DSHARD, 32), 512 * j : 512 * (j + 1)],
            )
    for cp in reads:
        cp.wait()
    values = tokens_v[...].astype(F32)
    scale = lax.rsqrt(jnp.mean(values * values, axis=-1, keepdims=True) + 1e-06)
    out_ref[pl.ds(0, ROWS), :] = (values * scale * gain_v[...]).astype(BF)
    out_ref[pl.ds(ROWS, META), :] = jnp.full((META, WIDTH), -1.0, BF)
    out_ref[pl.ds(ROWS, META), 0:ROWS] = ids_v[...].astype(F32).astype(BF)
    out_ref[pl.ds(ROWS, META), 128 : 128 + ROWS] = route_v[...].astype(BF)
    for cp in moves:
        cp.wait()


def cut_kernel(place_ref, first_ref, *refs):
    outs, sem = refs[:-1], refs[-1]
    copies = []
    for k, out_ref in enumerate(outs):
        at = pl.multiple_of(((place_ref[1] + k) & (NZH - 1)) * PIECE, PIECE)
        cp = pltpu.make_async_copy(first_ref.at[pl.ds(at, PIECE)], out_ref, sem.at[k])
        cp.start()
        copies.append(cp)
    for cp in copies:
        cp.wait()


def pick_kernel(chosen_ref, *refs):
    pieces, outs, sem = refs[:NZH], refs[NZH : 2 * NZH], refs[-1]
    for k, out_ref in enumerate(outs):
        for j, piece in enumerate(pieces):

            @pl.when(chosen_ref[k] == j)
            def _(piece=piece, out_ref=out_ref, k=k):
                pltpu.make_async_copy(piece, out_ref, sem.at[k]).start()

    for k, out_ref in enumerate(outs):
        pltpu.make_async_copy(pieces[0], out_ref, sem.at[k]).wait()


def unpack_kernel(kind_ref, place_ref, *refs):
    whole, pieces, refs = refs[:3], refs[3 : 3 + NZH], refs[3 + NZH :]
    gate_ref, up_ref, down_ref, block, sem = refs
    kind = kind_ref[0]
    for chosen, ref in zip((kind == 0, kind == 1, kind >= 8), whole):

        @pl.when(chosen)
        def _(ref=ref):
            cp = pltpu.make_async_copy(ref, block, sem.at[NZH])
            cp.start()
            cp.wait()

    @pl.when((kind == 2) | (kind == 4))
    def _():
        copies = []
        for k, ref in enumerate(pieces):
            at = pl.multiple_of(((place_ref[1] - k) & (NZH - 1)) * PIECE, PIECE)
            cp = pltpu.make_async_copy(ref, block.at[pl.ds(at, PIECE)], sem.at[k])
            cp.start()
            copies.append(cp)
        for cp in copies:
            cp.wait()

    gate_ref[...] = block[0:SHARD, 0:HIDDEN]
    up_ref[...] = block[0:SHARD, HIDDEN:SIDE]
    down_ref[:, 0:SIDE] = block[SHARD : SHARD + DSHARD, :]
    for j in range(3):
        down_ref[32 * j : 32 * (j + 1), SIDE:WIDTH] = block[
            SHARD + DSHARD : PACK, 512 * j : 512 * (j + 1)
        ]


def dispatch_kernel(n, place_ref, *refs):
    sources, (out_ref, weight_ref) = refs[:n], refs[n:]
    zh, zl = place_ref[1], place_ref[3]
    before = lax.broadcasted_iota(jnp.int32, (128, 128), 0)
    after = lax.broadcasted_iota(jnp.int32, (128, 128), 1)
    upto = (before <= after).astype(F32).astype(BF)
    slot = (before & (MOST - 1)).astype(F32)
    for i, ref in enumerate(sources):
        ids = ref[ROWS : ROWS + META, 0:128].astype(F32)
        route = ref[ROWS : ROWS + META, 128:256].astype(F32)
        chosen, factor = [], []
        for p in range(PLACES):
            expert = ((p // NC * NZH + zh) * NC + p % NC) * NZL + zl
            named = jnp.where(ids == expert.astype(F32), 1.0, 0.0)
            chosen.append(jnp.sum(named, axis=0, keepdims=True))
            factor.append(jnp.sum(named * route, axis=0, keepdims=True))
        chosen = jnp.concatenate(chosen, axis=0)
        factor = jnp.concatenate(factor, axis=0)
        ranks = jnp.dot(chosen.astype(BF), upto, preferred_element_type=F32) - 1.0
        ranks = jnp.where(chosen > 0.0, ranks, -1.0)

        def spread(v):
            return jnp.broadcast_to(v[:, None, :], (PLACES, MOST, 128)).reshape(128, 128)

        taken = spread(ranks) == slot
        placing = jnp.where(taken, 1.0, 0.0).astype(BF)
        rows = jnp.dot(placing[:, 0:ROWS], ref[0:ROWS, :], preferred_element_type=F32).astype(BF)
        for p in range(PLACES):
            at = (p * n + i) * MOST
            out_ref[at : at + MOST, :] = rows[p * MOST : (p + 1) * MOST]
        weight_ref[i] = jnp.where(taken, spread(factor), 0.0).T.astype(BF)


def dispatch(place, sources):
    n = len(sources)
    return call(
        functools.partial(dispatch_kernel, n),
        [shape(PLACES * n * MOST, WIDTH), shape(n, 128, 128)],
        [SMEM] + [VMEM] * n,
        [VMEM] * 2,
        "dispatch",
        cost=pl.CostEstimate(flops=0, transcendentals=0, bytes_accessed=80 << 20),
    )(place, *sources)


def ffn_kernel(splits, block, place_ref, own_ref, swap_ref, *refs):
    n = len(splits)
    row_refs, out_refs = refs[:n], refs[n : 2 * n]
    side_v, down_v, rows_v, res_v, sem_w, sem_r, sem_o = refs[2 * n :]
    zl = place_ref[3]
    loads, gets, puts, starts, at = [], [], [], [], 0

    def load(src, dst):
        cp = pltpu.make_async_copy(src, dst, sem_w.at[len(loads)])
        cp.start()
        loads.append(cp)

    for i, rows in enumerate(splits):
        starts.append(at)
        cp = pltpu.make_async_copy(row_refs[i], rows_v.at[pl.ds(at, rows)], sem_r.at[i])
        cp.start()
        gets.append(cp)
        at += rows
    total = at
    for src, from_zl in ((own_ref, zl), (swap_ref, 1 - zl)):
        for y in range(NY):
            holder = y * NZL + from_zl
            base = pl.multiple_of(holder * SHARD, SHARD)
            load(src.at[y, pl.ds(0, SHARD)], side_v.at[pl.ds(base, SHARD)])
            base = pl.multiple_of(holder * DSHARD, DSHARD)
            load(src.at[y, pl.ds(SHARD, DSHARD)], down_v.at[pl.ds(base, DSHARD), 0:SIDE])
            for j in range(3):
                load(
                    src.at[y, pl.ds(SHARD + DSHARD, 32), 512 * j : 512 * (j + 1)],
                    down_v.at[pl.ds(base + 32 * j, 32), SIDE:WIDTH],
                )
    for cp in gets:
        cp.wait()
    for cp in loads:
        cp.wait()

    @pl.loop(0, total // block)
    def _(step):
        at = pl.multiple_of(step * block, block)
        both = jnp.dot(rows_v[pl.ds(at, block), :], side_v[...], preferred_element_type=F32)
        gate, up = both[:, 0:HIDDEN], both[:, HIDDEN:SIDE]
        hidden = (gate / (1.0 + jnp.exp(-gate)) * up).astype(BF)
        res_v[pl.ds(at, block), :] = jnp.dot(
            hidden, down_v[...], preferred_element_type=F32
        ).astype(BF)

    for i, rows in enumerate(splits):
        cp = pltpu.make_async_copy(res_v.at[pl.ds(starts[i], rows)], out_refs[i], sem_o.at[i])
        cp.start()
        puts.append(cp)
    for cp in puts:
        cp.wait()


def ffn(place, own, swapped, groups, block):
    splits = tuple(g.shape[0] for g in groups)
    total = sum(splits)
    return call(
        functools.partial(ffn_kernel, splits, block),
        [pltpu.HBM((r, WIDTH), BF) for r in splits],
        [SMEM] + [HBM] * (2 + len(groups)),
        [HBM] * len(groups),
        "expert_ffn",
        scratch=[
            pltpu.VMEM((WIDTH, SIDE), BF),
            pltpu.VMEM((HIDDEN, WIDTH), BF),
            pltpu.VMEM((total, WIDTH), BF),
            pltpu.VMEM((total, WIDTH), BF),
            pltpu.SemaphoreType.DMA((2 * NY * 5,)),
            pltpu.SemaphoreType.DMA((len(groups),)),
            pltpu.SemaphoreType.DMA((len(groups),)),
        ],
        cost=pl.CostEstimate(
            flops=6 * total * WIDTH * HIDDEN,
            transcendentals=total * HIDDEN,
            bytes_accessed=10 * WIDTH * HIDDEN,
        ),
    )(place, own, swapped, *groups)


def combine_kernel(n, weight_ref, back_ref, *outs):
    for i, out_ref in enumerate(outs):
        stack = jnp.concatenate(
            [back_ref[(p * n + i) * MOST : (p * n + i + 1) * MOST, :] for p in range(PLACES)],
            axis=0,
        )
        out_ref[...] = jnp.dot(
            weight_ref[i, 0:ROWS, :], stack, preferred_element_type=F32
        ).astype(out_ref.dtype)


def combine(weight, back, dtypes):
    n = len(dtypes)
    return call(
        functools.partial(combine_kernel, n),
        [shape(ROWS, WIDTH, dtype=t) for t in dtypes],
        [VMEM] * 2,
        [VMEM] * n,
        "combine",
    )(weight, back)


PLANE = ("x", "c")


def in_plane(rows):
    blocks = rows.reshape(PLACES, -1, WIDTH)
    return across(blocks, PLANE).reshape(-1, WIDTH)


def partner(value, axis, bit):
    count = {"x": NX, "zh": NZH, "c": NC, "zl": NZL}[axis]
    return lax.ppermute(value, axis, [(i, i ^ bit) for i in range(count)])


def joined(got, mine):
    return (got.astype(F32) + mine).astype(BF)


def body(
    tokens, norm_gain, expert_ids, route_weights, gate_weight, up_weight, down_weight, pair_list
):
    x_me, zh_me, c_me = (lax.axis_index(a) for a in EXPERT)
    zl_me = lax.axis_index("zl")
    place = jnp.stack([x_me, zh_me, c_me, zl_me]).astype(jnp.int32)

    near, own, other, first = call(
        prep_kernel,
        [shape(ROWS + META, WIDTH)] + [shape(PACK, SIDE)] * 3,
        [SMEM] + [HBM] * 7,
        [VMEM] * 4,
        "prep",
        scratch=[
            pltpu.VMEM((ROWS, WIDTH), BF),
            pltpu.VMEM((1, WIDTH), F32),
            pltpu.VMEM((TOP, ROWS), jnp.int32),
            pltpu.VMEM((TOP, ROWS), F32),
            pltpu.SemaphoreType.DMA((4,)),
            pltpu.SemaphoreType.DMA((18,)),
        ],
    )(
        place, *(
            pltpu.with_memory_space_constraint(v, pltpu.HBM)
            for v in (
                tokens, norm_gain[None, :], expert_ids.T, route_weights.T,
                gate_weight, up_weight, down_weight,
            )
        )
    )

    own_full = lax.all_gather(own, "y", axis=0, tiled=False)

    p1, m1 = along_z(near, 1), along_z(near, -1)
    p1, m1, other = fence(p1, m1, other)
    swapped = partner(other, "zl", 1)
    p2, m2 = along_z(p1, 1), along_z(m1, -1)
    d0, w0 = dispatch(place, (near, p1, m1))
    hx = across(first.reshape(NX, PACK // NX, SIDE), "x")
    hc = partner(first, "c", 1)
    d0, hx, hc = fence(d0, hx, hc)
    r0 = in_plane(d0)
    p2, m2, swapped = fence(p2, m2, swapped)
    p3, m3 = along_z(p2, 1), along_z(m2, -1)
    d1, w1 = dispatch(place, (p2, m2))
    d1, r0, p3, m3, swapped = fence(d1, r0, p3, m3, swapped)
    swap_full = lax.all_gather(swapped, "y", axis=0, tiled=False)
    r1 = in_plane(d1)
    far = along_z(p3, 1)
    far, first = fence(far, first)
    cut = call(
        cut_kernel, [shape(PIECE, SIDE)] * NZH, [SMEM, HBM], [HBM] * NZH, "cut",
        scratch=[pltpu.SemaphoreType.DMA((NZH,))],
    )(place, first)
    held = [cut[0]] + [shift(cut[k], "zh", NZH, k) for k in range(1, NZH)]
    d2, w2 = dispatch(place, (p3, m3, far))
    d2, r1 = fence(d2, r1)
    r2 = in_plane(d2)
    r0, r1, r2, first, hx, *held = fence(r0, r1, r2, first, hx, *held)
    x_turn = jnp.arange(NX, dtype=jnp.int32)
    x_from = jnp.take(pair_list, (x_turn * NZH + zh_me) * NC + c_me, mode="clip") >> 3
    hx = across(jnp.take(hx, x_from, axis=0, mode="clip"), "x").reshape(PACK, SIDE)

    turn = (zh_me + jnp.arange(NZH, dtype=jnp.int32)) & (NZH - 1)
    matched = jnp.take(pair_list, (x_me * NZH + turn) * NC + c_me, mode="clip")
    chosen = (zh_me - (matched >> 1)) & (NZH - 1)
    picked = call(
        pick_kernel, [shape(PIECE, SIDE)] * NZH, [SMEM] + [HBM] * NZH, [HBM] * NZH, "pick",
        scratch=[pltpu.SemaphoreType.DMA((NZH,))],
    )(chosen.astype(jnp.int32), *held)
    held = [picked[0]] + [shift(picked[k], "zh", NZH, k) for k in range(1, NZH)]

    (s2,) = ffn(place, own_full, swap_full, (r2,), 384)
    s2, r1, r0, hx, *held = fence(s2, r1, r0, hx, *held)
    b2 = in_plane(s2)
    s1, s0 = ffn(place, own_full, swap_full, (r1, r0), 320)
    b2, s1, s0 = fence(b2, s1, s0)
    c_m3, c_p3, c_4 = combine(w2, b2, (F32, BF, BF))
    down, rise = along_z(c_4, -1), along_z(c_p3, 1)
    b1 = in_plane(s1)
    down = along_z(joined(down, c_m3), -1)
    b1, s0, rise, *held = fence(b1, s0, rise, *held)
    b0 = in_plane(s0)
    c_m2, c_p2 = combine(w1, b1, (F32, F32))
    down = along_z(joined(down, c_m2), -1)
    rise = along_z(joined(rise, c_p2), 1)

    me = (x_me * NZH + zh_me) * NC + c_me
    bits = jnp.sum(jnp.where(jnp.arange(pair_list.shape[0]) == me, pair_list ^ me, 0))
    new = call(
        unpack_kernel,
        [shape(SHARD, HIDDEN), shape(SHARD, HIDDEN), shape(DSHARD, WIDTH)],
        [SMEM] * 2 + [HBM] * 7,
        [VMEM] * 3,
        "unpack",
        scratch=[pltpu.VMEM((PACK, SIDE), BF), pltpu.SemaphoreType.DMA((NZH + 1,))],
    )(bits.astype(jnp.int32).reshape(1), place, first, hc, hx, *held)

    c_0, c_m1, c_p1 = combine(w0, b0, (F32, F32, F32))
    down = along_z(joined(down, c_m1), -1)
    rise = along_z(joined(rise, c_p1), 1)
    mixed = (down.astype(F32) + rise.astype(F32) + c_0).astype(BF)
    return (mixed, *(v[None] for v in new))


def solution(mesh):
    split = Mesh(mesh.devices.reshape(NX, NZH, NC, NY, NZL), EXPERT_DP)
    rows = P(EXPERT_DP, None)
    blocks = P(EXPERT, DP, None)
    return jax.shard_map(
        body,
        mesh=split,
        in_specs=(rows, P(), rows, rows, blocks, blocks, blocks, P()),
        out_specs=(rows, blocks, blocks, blocks),
        check_vma=False,
    )
```

```python
import functools

import jax
import jax.numpy as jnp
from jax import lax
from jax.experimental import pallas as pl
from jax.experimental.pallas import tpu as pltpu
from jax.sharding import Mesh
from jax.sharding import PartitionSpec as P

EXPERT = ("x", "zh", "c")
DP = ("y", "zl")
Z = ("zh", "zl")
EXPERT_DP = EXPERT + DP
MOST = 16
NX, NZH, NC, NY, NZL = 4, 4, 2, 4, 2
NZ = NZH * NZL
PLACES = NX * NC
ROWS, TOP, WIDTH, HIDDEN = 96, 8, 2048, 768
META = 8
SHARD, DSHARD = 256, 96
PACK = 384
HALF = PACK // 2
SIDE = 2 * HIDDEN
PIECE = PACK // NZH
BF = jnp.bfloat16
F32 = jnp.float32
GROUPS = ((0, -1, 1), (-2, 2), (-3, 3, 4))
VMEM = pl.BlockSpec(memory_space=pltpu.VMEM)
SMEM = pl.BlockSpec(memory_space=pltpu.SMEM)
HBM = pl.BlockSpec(memory_space=pltpu.HBM)
LIMIT = 48 << 20


def shift(value, axes, count, step):
    return lax.ppermute(value, axes, [(i, (i + step) % count) for i in range(count)])


def along_z(value, step):
    return shift(value, Z, NZ, step)


def along_y(value, step):
    return shift(value, "y", NY, step)


def flip(value, axis):
    return lax.ppermute(value, axis, [(0, 1), (1, 0)])


def across(value, axis):
    return lax.all_to_all(value, axis, split_axis=0, concat_axis=0, tiled=True)


def fence(*values):
    return lax.optimization_barrier(values)


def call(kernel, outs, in_specs, out_specs, name, scratch=(), cost=None):
    return pl.pallas_call(
        kernel,
        out_shape=outs,
        in_specs=in_specs,
        out_specs=out_specs,
        scratch_shapes=scratch,
        compiler_params=pltpu.CompilerParams(vmem_limit_bytes=LIMIT),
        cost_estimate=cost,
        name=name,
    )


def shape(*dims, dtype=BF):
    return jax.ShapeDtypeStruct(dims, dtype)


def prep_kernel(
    place_ref, tokens_ref, gain_ref, ids_ref, route_ref, gate_ref, up_ref, down_ref,
    out_ref, own_ref, other_ref, first_ref, tokens_v, gain_v, ids_v, route_v, sem_a, sem_b,
):
    zl = place_ref[3]
    reads, moves = [], []
    for src, dst in (
        (tokens_ref, tokens_v), (gain_ref, gain_v), (ids_ref, ids_v), (route_ref, route_v),
    ):
        cp = pltpu.make_async_copy(src, dst, sem_a.at[len(reads)])
        cp.start()
        reads.append(cp)

    def move(src, dst):
        cp = pltpu.make_async_copy(src, dst, sem_b.at[len(moves)])
        cp.start()
        moves.append(cp)

    for pack_ref, e in ((own_ref, zl), (other_ref, 1 - zl), (first_ref, 0)):
        move(gate_ref.at[e], pack_ref.at[pl.ds(0, SHARD), 0:HIDDEN])
        move(up_ref.at[e], pack_ref.at[pl.ds(0, SHARD), HIDDEN:SIDE])
        move(down_ref.at[e, :, 0:SIDE], pack_ref.at[pl.ds(SHARD, DSHARD), :])
        for j in range(3):
            move(
                down_ref.at[e, pl.ds(32 * j, 32), SIDE:WIDTH],
                pack_ref.at[pl.ds(SHARD + DSHARD, 32), 512 * j : 512 * (j + 1)],
            )
    for cp in reads:
        cp.wait()
    values = tokens_v[...].astype(F32)
    scale = lax.rsqrt(jnp.mean(values * values, axis=-1, keepdims=True) + 1e-06)
    out_ref[pl.ds(0, ROWS), :] = (values * scale * gain_v[...]).astype(BF)
    out_ref[pl.ds(ROWS, META), :] = jnp.full((META, WIDTH), -1.0, BF)
    out_ref[pl.ds(ROWS, META), 0:ROWS] = ids_v[...].astype(F32).astype(BF)
    out_ref[pl.ds(ROWS, META), 128 : 128 + ROWS] = route_v[...].astype(BF)
    for cp in moves:
        cp.wait()


def cut_kernel(place_ref, first_ref, *refs):
    outs, sem = refs[:-1], refs[-1]
    copies = []
    for k, out_ref in enumerate(outs):
        at = pl.multiple_of(((place_ref[1] + k) & (NZH - 1)) * PIECE, PIECE)
        cp = pltpu.make_async_copy(first_ref.at[pl.ds(at, PIECE)], out_ref, sem.at[k])
        cp.start()
        copies.append(cp)
    for cp in copies:
        cp.wait()


def pick_kernel(chosen_ref, *refs):
    pieces, outs, sem = refs[:NZH], refs[NZH : 2 * NZH], refs[-1]
    for k, out_ref in enumerate(outs):
        for j, piece in enumerate(pieces):

            @pl.when(chosen_ref[k] == j)
            def _(piece=piece, out_ref=out_ref, k=k):
                pltpu.make_async_copy(piece, out_ref, sem.at[k]).start()

    for k, out_ref in enumerate(outs):
        pltpu.make_async_copy(pieces[0], out_ref, sem.at[k]).wait()


def unpack_kernel(kind_ref, place_ref, *refs):
    whole, pieces, refs = refs[:3], refs[3 : 3 + NZH], refs[3 + NZH :]
    gate_ref, up_ref, down_ref, block, sem = refs
    kind = kind_ref[0]
    for chosen, ref in zip((kind == 0, kind == 1, kind >= 8), whole):

        @pl.when(chosen)
        def _(ref=ref):
            cp = pltpu.make_async_copy(ref, block, sem.at[NZH])
            cp.start()
            cp.wait()

    @pl.when((kind == 2) | (kind == 4))
    def _():
        copies = []
        for k, ref in enumerate(pieces):
            at = pl.multiple_of(((place_ref[1] - k) & (NZH - 1)) * PIECE, PIECE)
            cp = pltpu.make_async_copy(ref, block.at[pl.ds(at, PIECE)], sem.at[k])
            cp.start()
            copies.append(cp)
        for cp in copies:
            cp.wait()

    gate_ref[...] = block[0:SHARD, 0:HIDDEN]
    up_ref[...] = block[0:SHARD, HIDDEN:SIDE]
    down_ref[:, 0:SIDE] = block[SHARD : SHARD + DSHARD, :]
    for j in range(3):
        down_ref[32 * j : 32 * (j + 1), SIDE:WIDTH] = block[
            SHARD + DSHARD : PACK, 512 * j : 512 * (j + 1)
        ]


def dispatch_kernel(n, place_ref, *refs):
    sources, (out_ref, weight_ref) = refs[:n], refs[n:]
    zh, zl = place_ref[1], place_ref[3]
    before = lax.broadcasted_iota(jnp.int32, (128, 128), 0)
    after = lax.broadcasted_iota(jnp.int32, (128, 128), 1)
    upto = (before <= after).astype(F32).astype(BF)
    slot = (before & (MOST - 1)).astype(F32)
    for i, ref in enumerate(sources):
        ids = ref[ROWS : ROWS + META, 0:128].astype(F32)
        route = ref[ROWS : ROWS + META, 128:256].astype(F32)
        chosen, factor = [], []
        for p in range(PLACES):
            expert = ((p // NC * NZH + zh) * NC + p % NC) * NZL + zl
            named = jnp.where(ids == expert.astype(F32), 1.0, 0.0)
            chosen.append(jnp.sum(named, axis=0, keepdims=True))
            factor.append(jnp.sum(named * route, axis=0, keepdims=True))
        chosen = jnp.concatenate(chosen, axis=0)
        factor = jnp.concatenate(factor, axis=0)
        ranks = jnp.dot(chosen.astype(BF), upto, preferred_element_type=F32) - 1.0
        ranks = jnp.where(chosen > 0.0, ranks, -1.0)

        def spread(v):
            return jnp.broadcast_to(v[:, None, :], (PLACES, MOST, 128)).reshape(128, 128)

        taken = spread(ranks) == slot
        placing = jnp.where(taken, 1.0, 0.0).astype(BF)
        rows = jnp.dot(placing[:, 0:ROWS], ref[0:ROWS, :], preferred_element_type=F32).astype(BF)
        for p in range(PLACES):
            at = (p * n + i) * MOST
            out_ref[at : at + MOST, :] = rows[p * MOST : (p + 1) * MOST]
        weight_ref[i] = jnp.where(taken, spread(factor), 0.0).T.astype(BF)


def dispatch(place, sources):
    n = len(sources)
    return call(
        functools.partial(dispatch_kernel, n),
        [shape(PLACES * n * MOST, WIDTH), shape(n, 128, 128)],
        [SMEM] + [VMEM] * n,
        [VMEM] * 2,
        "dispatch",
        cost=pl.CostEstimate(flops=0, transcendentals=0, bytes_accessed=80 << 20),
    )(place, *sources)


def ffn_kernel(splits, block, place_ref, own_ref, swap_ref, *refs):
    n = len(splits)
    row_refs, out_refs = refs[:n], refs[n : 2 * n]
    side_v, down_v, rows_v, res_v, sem_w, sem_r, sem_o = refs[2 * n :]
    zl = place_ref[3]
    loads, gets, puts, starts, at = [], [], [], [], 0

    def load(src, dst):
        cp = pltpu.make_async_copy(src, dst, sem_w.at[len(loads)])
        cp.start()
        loads.append(cp)

    for i, rows in enumerate(splits):
        starts.append(at)
        cp = pltpu.make_async_copy(row_refs[i], rows_v.at[pl.ds(at, rows)], sem_r.at[i])
        cp.start()
        gets.append(cp)
        at += rows
    total = at
    for src, from_zl in ((own_ref, zl), (swap_ref, 1 - zl)):
        for y in range(NY):
            holder = y * NZL + from_zl
            base = pl.multiple_of(holder * SHARD, SHARD)
            load(src.at[y, pl.ds(0, SHARD)], side_v.at[pl.ds(base, SHARD)])
            base = pl.multiple_of(holder * DSHARD, DSHARD)
            load(src.at[y, pl.ds(SHARD, DSHARD)], down_v.at[pl.ds(base, DSHARD), 0:SIDE])
            for j in range(3):
                load(
                    src.at[y, pl.ds(SHARD + DSHARD, 32), 512 * j : 512 * (j + 1)],
                    down_v.at[pl.ds(base + 32 * j, 32), SIDE:WIDTH],
                )
    for cp in gets:
        cp.wait()
    for cp in loads:
        cp.wait()

    @pl.loop(0, total // block)
    def _(step):
        at = pl.multiple_of(step * block, block)
        both = jnp.dot(rows_v[pl.ds(at, block), :], side_v[...], preferred_element_type=F32)
        gate, up = both[:, 0:HIDDEN], both[:, HIDDEN:SIDE]
        hidden = (gate / (1.0 + jnp.exp(-gate)) * up).astype(BF)
        res_v[pl.ds(at, block), :] = jnp.dot(
            hidden, down_v[...], preferred_element_type=F32
        ).astype(BF)

    for i, rows in enumerate(splits):
        cp = pltpu.make_async_copy(res_v.at[pl.ds(starts[i], rows)], out_refs[i], sem_o.at[i])
        cp.start()
        puts.append(cp)
    for cp in puts:
        cp.wait()


def ffn(place, own, swapped, groups, block):
    splits = tuple(g.shape[0] for g in groups)
    total = sum(splits)
    return call(
        functools.partial(ffn_kernel, splits, block),
        [pltpu.HBM((r, WIDTH), BF) for r in splits],
        [SMEM] + [HBM] * (2 + len(groups)),
        [HBM] * len(groups),
        "expert_ffn",
        scratch=[
            pltpu.VMEM((WIDTH, SIDE), BF),
            pltpu.VMEM((HIDDEN, WIDTH), BF),
            pltpu.VMEM((total, WIDTH), BF),
            pltpu.VMEM((total, WIDTH), BF),
            pltpu.SemaphoreType.DMA((2 * NY * 5,)),
            pltpu.SemaphoreType.DMA((len(groups),)),
            pltpu.SemaphoreType.DMA((len(groups),)),
        ],
        cost=pl.CostEstimate(
            flops=6 * total * WIDTH * HIDDEN,
            transcendentals=total * HIDDEN,
            bytes_accessed=10 * WIDTH * HIDDEN,
        ),
    )(place, own, swapped, *groups)


def combine_kernel(n, weight_ref, back_ref, *outs):
    for i, out_ref in enumerate(outs):
        stack = jnp.concatenate(
            [back_ref[(p * n + i) * MOST : (p * n + i + 1) * MOST, :] for p in range(PLACES)],
            axis=0,
        )
        out_ref[...] = jnp.dot(
            weight_ref[i, 0:ROWS, :], stack, preferred_element_type=F32
        ).astype(out_ref.dtype)


def combine(weight, back, dtypes):
    n = len(dtypes)
    return call(
        functools.partial(combine_kernel, n),
        [shape(ROWS, WIDTH, dtype=t) for t in dtypes],
        [VMEM] * 2,
        [VMEM] * n,
        "combine",
    )(weight, back)


PLANE = ("x", "c")


def in_plane(rows):
    blocks = rows.reshape(PLACES, -1, WIDTH)
    return across(blocks, PLANE).reshape(-1, WIDTH)


def partner(value, axis, bit):
    count = {"x": NX, "zh": NZH, "c": NC, "zl": NZL}[axis]
    return lax.ppermute(value, axis, [(i, i ^ bit) for i in range(count)])


def joined(got, mine):
    return (got.astype(F32) + mine).astype(BF)


def body(
    tokens, norm_gain, expert_ids, route_weights, gate_weight, up_weight, down_weight, pair_list
):
    x_me, zh_me, c_me = (lax.axis_index(a) for a in EXPERT)
    zl_me = lax.axis_index("zl")
    place = jnp.stack([x_me, zh_me, c_me, zl_me]).astype(jnp.int32)

    near, own, other, first = call(
        prep_kernel,
        [shape(ROWS + META, WIDTH)] + [shape(PACK, SIDE)] * 3,
        [SMEM] + [HBM] * 7,
        [VMEM] * 4,
        "prep",
        scratch=[
            pltpu.VMEM((ROWS, WIDTH), BF),
            pltpu.VMEM((1, WIDTH), F32),
            pltpu.VMEM((TOP, ROWS), jnp.int32),
            pltpu.VMEM((TOP, ROWS), F32),
            pltpu.SemaphoreType.DMA((4,)),
            pltpu.SemaphoreType.DMA((18,)),
        ],
    )(
        place, *(
            pltpu.with_memory_space_constraint(v, pltpu.HBM)
            for v in (
                tokens, norm_gain[None, :], expert_ids.T, route_weights.T,
                gate_weight, up_weight, down_weight,
            )
        )
    )

    own_full = lax.all_gather(own, "y", axis=0, tiled=False)

    p1, m1 = along_z(near, 1), along_z(near, -1)
    p1, m1, other = fence(p1, m1, other)
    swapped = partner(other, "zl", 1)
    p2, m2 = along_z(p1, 1), along_z(m1, -1)
    d0, w0 = dispatch(place, (near, p1, m1))
    hx = across(first.reshape(NX, PACK // NX, SIDE), "x")
    hc = partner(first, "c", 1)
    d0, hx, hc = fence(d0, hx, hc)
    r0 = in_plane(d0)
    p2, m2, swapped = fence(p2, m2, swapped)
    p3, m3 = along_z(p2, 1), along_z(m2, -1)
    cut = call(
        cut_kernel, [shape(PIECE, SIDE)] * NZH, [SMEM, HBM], [HBM] * NZH, "cut",
        scratch=[pltpu.SemaphoreType.DMA((NZH,))],
    )(place, first)
    d1, w1 = dispatch(place, (p2, m2))
    d1, r0, p3, m3, swapped, *cut = fence(d1, r0, p3, m3, swapped, *cut)
    swap_full = lax.all_gather(swapped, "y", axis=0, tiled=False)
    r1 = in_plane(d1)
    far = along_z(p3, 1)
    held = [cut[0]] + [shift(cut[k], "zh", NZH, k) for k in range(1, NZH)]
    d2, w2 = dispatch(place, (p3, m3, far))
    d2, r1, *held = fence(d2, r1, *held)
    r2 = in_plane(d2)
    x_turn = jnp.arange(NX, dtype=jnp.int32)
    x_from = jnp.take(pair_list, (x_turn * NZH + zh_me) * NC + c_me, mode="clip") >> 3
    hx = jnp.take(hx, x_from, axis=0, mode="clip")
    turn = (zh_me + jnp.arange(NZH, dtype=jnp.int32)) & (NZH - 1)
    matched = jnp.take(pair_list, (x_me * NZH + turn) * NC + c_me, mode="clip")
    chosen = (zh_me - (matched >> 1)) & (NZH - 1)
    picked = call(
        pick_kernel, [shape(PIECE, SIDE)] * NZH, [SMEM] + [HBM] * NZH, [HBM] * NZH, "pick",
        scratch=[pltpu.SemaphoreType.DMA((NZH,))],
    )(chosen.astype(jnp.int32), *held)
    held = [picked[0]] + [shift(picked[k], "zh", NZH, k) for k in range(1, NZH)]
    r0, r1, r2, hx, *held = fence(r0, r1, r2, hx, *held)
    hx = across(hx, "x").reshape(PACK, SIDE)
    (s2,) = ffn(place, own_full, swap_full, (r2,), 384)
    s2, r1, r0, hx = fence(s2, r1, r0, hx)
    b2 = in_plane(s2)
    s1, s0 = ffn(place, own_full, swap_full, (r1, r0), 320)
    b2, s1, s0 = fence(b2, s1, s0)
    c_m3, c_p3, c_4 = combine(w2, b2, (F32, BF, BF))
    down, rise = along_z(c_4, -1), along_z(c_p3, 1)
    b1 = in_plane(s1)
    down = along_z(joined(down, c_m3), -1)
    b1, s0, rise = fence(b1, s0, rise)
    b0 = in_plane(s0)
    c_m2, c_p2 = combine(w1, b1, (F32, F32))
    down = along_z(joined(down, c_m2), -1)
    rise = along_z(joined(rise, c_p2), 1)

    me = (x_me * NZH + zh_me) * NC + c_me
    bits = jnp.sum(jnp.where(jnp.arange(pair_list.shape[0]) == me, pair_list ^ me, 0))
    new = call(
        unpack_kernel,
        [shape(SHARD, HIDDEN), shape(SHARD, HIDDEN), shape(DSHARD, WIDTH)],
        [SMEM] * 2 + [HBM] * 7,
        [VMEM] * 3,
        "unpack",
        scratch=[pltpu.VMEM((PACK, SIDE), BF), pltpu.SemaphoreType.DMA((NZH + 1,))],
    )(bits.astype(jnp.int32).reshape(1), place, first, hc, hx, *held)

    c_0, c_m1, c_p1 = combine(w0, b0, (F32, F32, F32))
    down = along_z(joined(down, c_m1), -1)
    rise = along_z(joined(rise, c_p1), 1)
    mixed = (down.astype(F32) + rise.astype(F32) + c_0).astype(BF)
    return (mixed, *(v[None] for v in new))


def solution(mesh):
    split = Mesh(mesh.devices.reshape(NX, NZH, NC, NY, NZL), EXPERT_DP)
    rows = P(EXPERT_DP, None)
    blocks = P(EXPERT, DP, None)
    return jax.shard_map(
        body,
        mesh=split,
        in_specs=(rows, P(), rows, rows, blocks, blocks, blocks, P()),
        out_specs=(rows, blocks, blocks, blocks),
        check_vma=False,
    )
```

```python
import functools

import jax
import jax.numpy as jnp
from jax import lax
from jax.experimental import pallas as pl
from jax.experimental.pallas import tpu as pltpu
from jax.sharding import Mesh
from jax.sharding import PartitionSpec as P

EXPERT = ("x", "zh", "c")
DP = ("y", "zl")
Z = ("zh", "zl")
EXPERT_DP = EXPERT + DP
MOST = 16
NX, NZH, NC, NY, NZL = 4, 4, 2, 4, 2
NZ = NZH * NZL
PLACES = NX * NC
ROWS, TOP, WIDTH, HIDDEN = 96, 8, 2048, 768
META = 8
SHARD, DSHARD = 256, 96
PACK = 384
HALF = PACK // 2
SIDE = 2 * HIDDEN
PIECE = PACK // NZH
BF = jnp.bfloat16
F32 = jnp.float32
GROUPS = ((0, -1, 1), (-2, 2), (-3, 3, 4))
VMEM = pl.BlockSpec(memory_space=pltpu.VMEM)
SMEM = pl.BlockSpec(memory_space=pltpu.SMEM)
HBM = pl.BlockSpec(memory_space=pltpu.HBM)
LIMIT = 48 << 20


def shift(value, axes, count, step):
    return lax.ppermute(value, axes, [(i, (i + step) % count) for i in range(count)])


def along_z(value, step):
    return shift(value, Z, NZ, step)


def along_y(value, step):
    return shift(value, "y", NY, step)


def flip(value, axis):
    return lax.ppermute(value, axis, [(0, 1), (1, 0)])


def across(value, axis):
    return lax.all_to_all(value, axis, split_axis=0, concat_axis=0, tiled=True)


def fence(*values):
    return lax.optimization_barrier(values)


def call(kernel, outs, in_specs, out_specs, name, scratch=(), cost=None):
    return pl.pallas_call(
        kernel,
        out_shape=outs,
        in_specs=in_specs,
        out_specs=out_specs,
        scratch_shapes=scratch,
        compiler_params=pltpu.CompilerParams(vmem_limit_bytes=LIMIT),
        cost_estimate=cost,
        name=name,
    )


def shape(*dims, dtype=BF):
    return jax.ShapeDtypeStruct(dims, dtype)


def prep_kernel(
    place_ref, tokens_ref, gain_ref, ids_ref, route_ref, gate_ref, up_ref, down_ref,
    out_ref, own_ref, other_ref, first_ref, tokens_v, gain_v, ids_v, route_v, sem_a, sem_b,
):
    zl = place_ref[3]
    reads, moves = [], []
    for src, dst in (
        (tokens_ref, tokens_v), (gain_ref, gain_v), (ids_ref, ids_v), (route_ref, route_v),
    ):
        cp = pltpu.make_async_copy(src, dst, sem_a.at[len(reads)])
        cp.start()
        reads.append(cp)

    def move(src, dst):
        cp = pltpu.make_async_copy(src, dst, sem_b.at[len(moves)])
        cp.start()
        moves.append(cp)

    for pack_ref, e in ((own_ref, zl), (other_ref, 1 - zl), (first_ref, 0)):
        move(gate_ref.at[e], pack_ref.at[pl.ds(0, SHARD), 0:HIDDEN])
        move(up_ref.at[e], pack_ref.at[pl.ds(0, SHARD), HIDDEN:SIDE])
        move(down_ref.at[e, :, 0:SIDE], pack_ref.at[pl.ds(SHARD, DSHARD), :])
        for j in range(3):
            move(
                down_ref.at[e, pl.ds(32 * j, 32), SIDE:WIDTH],
                pack_ref.at[pl.ds(SHARD + DSHARD, 32), 512 * j : 512 * (j + 1)],
            )
    for cp in reads:
        cp.wait()
    values = tokens_v[...].astype(F32)
    scale = lax.rsqrt(jnp.mean(values * values, axis=-1, keepdims=True) + 1e-06)
    out_ref[pl.ds(0, ROWS), :] = (values * scale * gain_v[...]).astype(BF)
    out_ref[pl.ds(ROWS, META), :] = jnp.full((META, WIDTH), -1.0, BF)
    out_ref[pl.ds(ROWS, META), 0:ROWS] = ids_v[...].astype(F32).astype(BF)
    out_ref[pl.ds(ROWS, META), 128 : 128 + ROWS] = route_v[...].astype(BF)
    for cp in moves:
        cp.wait()


def cut_kernel(place_ref, first_ref, *refs):
    outs, sem = refs[:-1], refs[-1]
    copies = []
    for k, out_ref in enumerate(outs):
        at = pl.multiple_of(((place_ref[1] + k) & (NZH - 1)) * PIECE, PIECE)
        cp = pltpu.make_async_copy(first_ref.at[pl.ds(at, PIECE)], out_ref, sem.at[k])
        cp.start()
        copies.append(cp)
    for cp in copies:
        cp.wait()


def pick_kernel(chosen_ref, *refs):
    pieces, outs, sem = refs[:NZH], refs[NZH : 2 * NZH], refs[-1]
    for k, out_ref in enumerate(outs):
        for j, piece in enumerate(pieces):

            @pl.when(chosen_ref[k] == j)
            def _(piece=piece, out_ref=out_ref, k=k):
                pltpu.make_async_copy(piece, out_ref, sem.at[k]).start()

    for k, out_ref in enumerate(outs):
        pltpu.make_async_copy(pieces[0], out_ref, sem.at[k]).wait()


def unpack_kernel(kind_ref, place_ref, *refs):
    whole, pieces, refs = refs[:3], refs[3 : 3 + NZH], refs[3 + NZH :]
    gate_ref, up_ref, down_ref, block, sem = refs
    kind = kind_ref[0]
    for chosen, ref in zip((kind == 0, kind == 1, kind >= 8), whole):

        @pl.when(chosen)
        def _(ref=ref):
            cp = pltpu.make_async_copy(ref, block, sem.at[NZH])
            cp.start()
            cp.wait()

    @pl.when((kind == 2) | (kind == 4))
    def _():
        copies = []
        for k, ref in enumerate(pieces):
            at = pl.multiple_of(((place_ref[1] - k) & (NZH - 1)) * PIECE, PIECE)
            cp = pltpu.make_async_copy(ref, block.at[pl.ds(at, PIECE)], sem.at[k])
            cp.start()
            copies.append(cp)
        for cp in copies:
            cp.wait()

    gate_ref[...] = block[0:SHARD, 0:HIDDEN]
    up_ref[...] = block[0:SHARD, HIDDEN:SIDE]
    down_ref[:, 0:SIDE] = block[SHARD : SHARD + DSHARD, :]
    for j in range(3):
        down_ref[32 * j : 32 * (j + 1), SIDE:WIDTH] = block[
            SHARD + DSHARD : PACK, 512 * j : 512 * (j + 1)
        ]


def dispatch_kernel(n, place_ref, *refs):
    sources, (out_ref, weight_ref) = refs[:n], refs[n:]
    zh, zl = place_ref[1], place_ref[3]
    before = lax.broadcasted_iota(jnp.int32, (128, 128), 0)
    after = lax.broadcasted_iota(jnp.int32, (128, 128), 1)
    upto = (before <= after).astype(F32).astype(BF)
    slot = (before & (MOST - 1)).astype(F32)
    for i, ref in enumerate(sources):
        ids = ref[ROWS : ROWS + META, 0:128].astype(F32)
        route = ref[ROWS : ROWS + META, 128:256].astype(F32)
        chosen, factor = [], []
        for p in range(PLACES):
            expert = ((p // NC * NZH + zh) * NC + p % NC) * NZL + zl
            named = jnp.where(ids == expert.astype(F32), 1.0, 0.0)
            chosen.append(jnp.sum(named, axis=0, keepdims=True))
            factor.append(jnp.sum(named * route, axis=0, keepdims=True))
        chosen = jnp.concatenate(chosen, axis=0)
        factor = jnp.concatenate(factor, axis=0)
        ranks = jnp.dot(chosen.astype(BF), upto, preferred_element_type=F32) - 1.0
        ranks = jnp.where(chosen > 0.0, ranks, -1.0)

        def spread(v):
            return jnp.broadcast_to(v[:, None, :], (PLACES, MOST, 128)).reshape(128, 128)

        taken = spread(ranks) == slot
        placing = jnp.where(taken, 1.0, 0.0).astype(BF)
        rows = jnp.dot(placing[:, 0:ROWS], ref[0:ROWS, :], preferred_element_type=F32).astype(BF)
        for p in range(PLACES):
            at = (p * n + i) * MOST
            out_ref[at : at + MOST, :] = rows[p * MOST : (p + 1) * MOST]
        weight_ref[i] = jnp.where(taken, spread(factor), 0.0).T.astype(BF)


def dispatch(place, sources):
    n = len(sources)
    return call(
        functools.partial(dispatch_kernel, n),
        [shape(PLACES * n * MOST, WIDTH), shape(n, 128, 128)],
        [SMEM] + [VMEM] * n,
        [VMEM] * 2,
        "dispatch",
        cost=pl.CostEstimate(flops=0, transcendentals=0, bytes_accessed=80 << 20),
    )(place, *sources)


def ffn_kernel(splits, block, place_ref, own_ref, swap_ref, *refs):
    n = len(splits)
    row_refs, out_refs = refs[:n], refs[n : 2 * n]
    side_v, down_v, rows_v, res_v, sem_w, sem_r, sem_o = refs[2 * n :]
    zl = place_ref[3]
    loads, gets, puts, starts, at = [], [], [], [], 0

    def load(src, dst):
        cp = pltpu.make_async_copy(src, dst, sem_w.at[len(loads)])
        cp.start()
        loads.append(cp)

    for i, rows in enumerate(splits):
        starts.append(at)
        cp = pltpu.make_async_copy(row_refs[i], rows_v.at[pl.ds(at, rows)], sem_r.at[i])
        cp.start()
        gets.append(cp)
        at += rows
    total = at
    for src, from_zl in ((own_ref, zl), (swap_ref, 1 - zl)):
        for y in range(NY):
            holder = y * NZL + from_zl
            base = pl.multiple_of(holder * SHARD, SHARD)
            load(src.at[y, pl.ds(0, SHARD)], side_v.at[pl.ds(base, SHARD)])
            base = pl.multiple_of(holder * DSHARD, DSHARD)
            load(src.at[y, pl.ds(SHARD, DSHARD)], down_v.at[pl.ds(base, DSHARD), 0:SIDE])
            for j in range(3):
                load(
                    src.at[y, pl.ds(SHARD + DSHARD, 32), 512 * j : 512 * (j + 1)],
                    down_v.at[pl.ds(base + 32 * j, 32), SIDE:WIDTH],
                )
    for cp in gets:
        cp.wait()
    for cp in loads:
        cp.wait()

    @pl.loop(0, total // block)
    def _(step):
        at = pl.multiple_of(step * block, block)
        both = jnp.dot(rows_v[pl.ds(at, block), :], side_v[...], preferred_element_type=F32)
        gate, up = both[:, 0:HIDDEN], both[:, HIDDEN:SIDE]
        hidden = (gate / (1.0 + jnp.exp(-gate)) * up).astype(BF)
        res_v[pl.ds(at, block), :] = jnp.dot(
            hidden, down_v[...], preferred_element_type=F32
        ).astype(BF)

    for i, rows in enumerate(splits):
        cp = pltpu.make_async_copy(res_v.at[pl.ds(starts[i], rows)], out_refs[i], sem_o.at[i])
        cp.start()
        puts.append(cp)
    for cp in puts:
        cp.wait()


def ffn(place, own, swapped, groups, block):
    splits = tuple(g.shape[0] for g in groups)
    total = sum(splits)
    return call(
        functools.partial(ffn_kernel, splits, block),
        [pltpu.HBM((r, WIDTH), BF) for r in splits],
        [SMEM] + [HBM] * (2 + len(groups)),
        [HBM] * len(groups),
        "expert_ffn",
        scratch=[
            pltpu.VMEM((WIDTH, SIDE), BF),
            pltpu.VMEM((HIDDEN, WIDTH), BF),
            pltpu.VMEM((total, WIDTH), BF),
            pltpu.VMEM((total, WIDTH), BF),
            pltpu.SemaphoreType.DMA((2 * NY * 5,)),
            pltpu.SemaphoreType.DMA((len(groups),)),
            pltpu.SemaphoreType.DMA((len(groups),)),
        ],
        cost=pl.CostEstimate(
            flops=6 * total * WIDTH * HIDDEN,
            transcendentals=total * HIDDEN,
            bytes_accessed=10 * WIDTH * HIDDEN,
        ),
    )(place, own, swapped, *groups)


def combine_kernel(n, weight_ref, back_ref, *outs):
    for i, out_ref in enumerate(outs):
        stack = jnp.concatenate(
            [back_ref[(p * n + i) * MOST : (p * n + i + 1) * MOST, :] for p in range(PLACES)],
            axis=0,
        )
        out_ref[...] = jnp.dot(
            weight_ref[i, 0:ROWS, :], stack, preferred_element_type=F32
        ).astype(out_ref.dtype)


def combine(weight, back, dtypes):
    n = len(dtypes)
    return call(
        functools.partial(combine_kernel, n),
        [shape(ROWS, WIDTH, dtype=t) for t in dtypes],
        [VMEM] * 2,
        [VMEM] * n,
        "combine",
    )(weight, back)


PLANE = ("x", "c")


def in_plane(rows):
    blocks = rows.reshape(PLACES, -1, WIDTH)
    return across(blocks, PLANE).reshape(-1, WIDTH)


def partner(value, axis, bit):
    count = {"x": NX, "zh": NZH, "c": NC, "zl": NZL}[axis]
    return lax.ppermute(value, axis, [(i, i ^ bit) for i in range(count)])


def joined(got, mine):
    return (got.astype(F32) + mine).astype(BF)


def body(
    tokens, norm_gain, expert_ids, route_weights, gate_weight, up_weight, down_weight, pair_list
):
    x_me, zh_me, c_me = (lax.axis_index(a) for a in EXPERT)
    zl_me = lax.axis_index("zl")
    place = jnp.stack([x_me, zh_me, c_me, zl_me]).astype(jnp.int32)

    near, own, other, first = call(
        prep_kernel,
        [shape(ROWS + META, WIDTH)] + [shape(PACK, SIDE)] * 3,
        [SMEM] + [HBM] * 7,
        [VMEM] * 4,
        "prep",
        scratch=[
            pltpu.VMEM((ROWS, WIDTH), BF),
            pltpu.VMEM((1, WIDTH), F32),
            pltpu.VMEM((TOP, ROWS), jnp.int32),
            pltpu.VMEM((TOP, ROWS), F32),
            pltpu.SemaphoreType.DMA((4,)),
            pltpu.SemaphoreType.DMA((18,)),
        ],
    )(
        place, *(
            pltpu.with_memory_space_constraint(v, pltpu.HBM)
            for v in (
                tokens, norm_gain[None, :], expert_ids.T, route_weights.T,
                gate_weight, up_weight, down_weight,
            )
        )
    )

    own_full = lax.all_gather(own, "y", axis=0, tiled=False)

    p1, m1 = along_z(near, 1), along_z(near, -1)
    p1, m1, other = fence(p1, m1, other)
    swapped = partner(other, "zl", 1)
    p2, m2 = along_z(p1, 1), along_z(m1, -1)
    d0, w0 = dispatch(place, (near, p1, m1))
    hx = across(first.reshape(NX, PACK // NX, SIDE), "x")
    hc = partner(first, "c", 1)
    d0, hx, hc = fence(d0, hx, hc)
    r0 = in_plane(d0)
    p2, m2, swapped = fence(p2, m2, swapped)
    p3, m3 = along_z(p2, 1), along_z(m2, -1)
    cut = call(
        cut_kernel, [shape(PIECE, SIDE)] * NZH, [SMEM, HBM], [HBM] * NZH, "cut",
        scratch=[pltpu.SemaphoreType.DMA((NZH,))],
    )(place, first)
    d1, w1 = dispatch(place, (p2, m2))
    r0, hx, swapped = fence(r0, hx, swapped)
    swap_full = lax.all_gather(swapped, "y", axis=0, tiled=False)
    x_turn = jnp.arange(NX, dtype=jnp.int32)
    x_from = jnp.take(pair_list, (x_turn * NZH + zh_me) * NC + c_me, mode="clip") >> 3
    hx = across(jnp.take(hx, x_from, axis=0, mode="clip"), "x").reshape(PACK, SIDE)
    d1, r0, p3, m3, hx, *cut = fence(d1, r0, p3, m3, hx, *cut)
    r1 = in_plane(d1)
    far = along_z(p3, 1)
    held = [cut[0]] + [shift(cut[k], "zh", NZH, k) for k in range(1, NZH)]
    d2, w2 = dispatch(place, (p3, m3, far))
    d2, r1, held[1] = fence(d2, r1, held[1])
    r2 = in_plane(d2)
    r0, r1, r2, hx, *held = fence(r0, r1, r2, hx, *held)
    (s2,) = ffn(place, own_full, swap_full, (r2,), 384)
    s2, r1, r0, hx, *held = fence(s2, r1, r0, hx, *held)
    b2 = in_plane(s2)
    s1, s0 = ffn(place, own_full, swap_full, (r1, r0), 320)
    turn = (zh_me + jnp.arange(NZH, dtype=jnp.int32)) & (NZH - 1)
    matched = jnp.take(pair_list, (x_me * NZH + turn) * NC + c_me, mode="clip")
    chosen = (zh_me - (matched >> 1)) & (NZH - 1)
    picked = call(
        pick_kernel, [shape(PIECE, SIDE)] * NZH, [SMEM] + [HBM] * NZH, [HBM] * NZH, "pick",
        scratch=[pltpu.SemaphoreType.DMA((NZH,))],
    )(chosen.astype(jnp.int32), *held)
    held = [picked[0]] + [shift(picked[k], "zh", NZH, k) for k in range(1, NZH)]
    b2, s1, s0, *held = fence(b2, s1, s0, *held)
    c_m3, c_p3, c_4 = combine(w2, b2, (F32, BF, BF))
    down, rise = along_z(c_4, -1), along_z(c_p3, 1)
    b1 = in_plane(s1)
    down = along_z(joined(down, c_m3), -1)
    b1, s0, rise = fence(b1, s0, rise)
    b0 = in_plane(s0)
    c_m2, c_p2 = combine(w1, b1, (F32, F32))
    down = along_z(joined(down, c_m2), -1)
    rise = along_z(joined(rise, c_p2), 1)

    me = (x_me * NZH + zh_me) * NC + c_me
    bits = jnp.sum(jnp.where(jnp.arange(pair_list.shape[0]) == me, pair_list ^ me, 0))
    new = call(
        unpack_kernel,
        [shape(SHARD, HIDDEN), shape(SHARD, HIDDEN), shape(DSHARD, WIDTH)],
        [SMEM] * 2 + [HBM] * 7,
        [VMEM] * 3,
        "unpack",
        scratch=[pltpu.VMEM((PACK, SIDE), BF), pltpu.SemaphoreType.DMA((NZH + 1,))],
    )(bits.astype(jnp.int32).reshape(1), place, first, hc, hx, *held)

    c_0, c_m1, c_p1 = combine(w0, b0, (F32, F32, F32))
    down = along_z(joined(down, c_m1), -1)
    rise = along_z(joined(rise, c_p1), 1)
    mixed = (down.astype(F32) + rise.astype(F32) + c_0).astype(BF)
    return (mixed, *(v[None] for v in new))


def solution(mesh):
    split = Mesh(mesh.devices.reshape(NX, NZH, NC, NY, NZL), EXPERT_DP)
    rows = P(EXPERT_DP, None)
    blocks = P(EXPERT, DP, None)
    return jax.shard_map(
        body,
        mesh=split,
        in_specs=(rows, P(), rows, rows, blocks, blocks, blocks, P()),
        out_specs=(rows, blocks, blocks, blocks),
        check_vma=False,
    )
```

```python
import functools

import jax
import jax.numpy as jnp
from jax import lax
from jax.experimental import pallas as pl
from jax.experimental.pallas import tpu as pltpu
from jax.sharding import Mesh
from jax.sharding import PartitionSpec as P

EXPERT = ("x", "zh", "c")
DP = ("y", "zl")
Z = ("zh", "zl")
EXPERT_DP = EXPERT + DP
MOST = 16
NX, NZH, NC, NY, NZL = 4, 4, 2, 4, 2
NZ = NZH * NZL
PLACES = NX * NC
ROWS, TOP, WIDTH, HIDDEN = 96, 8, 2048, 768
META = 8
SHARD, DSHARD = 256, 96
PACK = 384
HALF = PACK // 2
SIDE = 2 * HIDDEN
PIECE = PACK // NZH
BF = jnp.bfloat16
F32 = jnp.float32
GROUPS = ((0, -1, 1), (-2, 2), (-3, 3, 4))
VMEM = pl.BlockSpec(memory_space=pltpu.VMEM)
SMEM = pl.BlockSpec(memory_space=pltpu.SMEM)
HBM = pl.BlockSpec(memory_space=pltpu.HBM)
LIMIT = 48 << 20


def shift(value, axes, count, step):
    return lax.ppermute(value, axes, [(i, (i + step) % count) for i in range(count)])


def along_z(value, step):
    return shift(value, Z, NZ, step)


def along_y(value, step):
    return shift(value, "y", NY, step)


def flip(value, axis):
    return lax.ppermute(value, axis, [(0, 1), (1, 0)])


def across(value, axis):
    return lax.all_to_all(value, axis, split_axis=0, concat_axis=0, tiled=True)


def fence(*values):
    return lax.optimization_barrier(values)


def call(kernel, outs, in_specs, out_specs, name, scratch=(), cost=None):
    return pl.pallas_call(
        kernel,
        out_shape=outs,
        in_specs=in_specs,
        out_specs=out_specs,
        scratch_shapes=scratch,
        compiler_params=pltpu.CompilerParams(vmem_limit_bytes=LIMIT),
        cost_estimate=cost,
        name=name,
    )


def shape(*dims, dtype=BF):
    return jax.ShapeDtypeStruct(dims, dtype)


def prep_kernel(
    place_ref, tokens_ref, gain_ref, ids_ref, route_ref, gate_ref, up_ref, down_ref,
    out_ref, own_ref, other_ref, first_ref, tokens_v, gain_v, ids_v, route_v, sem_a, sem_b,
):
    zl = place_ref[3]
    reads, moves = [], []
    for src, dst in (
        (tokens_ref, tokens_v), (gain_ref, gain_v), (ids_ref, ids_v), (route_ref, route_v),
    ):
        cp = pltpu.make_async_copy(src, dst, sem_a.at[len(reads)])
        cp.start()
        reads.append(cp)

    def move(src, dst):
        cp = pltpu.make_async_copy(src, dst, sem_b.at[len(moves)])
        cp.start()
        moves.append(cp)

    for pack_ref, e in ((own_ref, zl), (other_ref, 1 - zl), (first_ref, 0)):
        move(gate_ref.at[e], pack_ref.at[pl.ds(0, SHARD), 0:HIDDEN])
        move(up_ref.at[e], pack_ref.at[pl.ds(0, SHARD), HIDDEN:SIDE])
        move(down_ref.at[e, :, 0:SIDE], pack_ref.at[pl.ds(SHARD, DSHARD), :])
        for j in range(3):
            move(
                down_ref.at[e, pl.ds(32 * j, 32), SIDE:WIDTH],
                pack_ref.at[pl.ds(SHARD + DSHARD, 32), 512 * j : 512 * (j + 1)],
            )
    for cp in reads:
        cp.wait()
    values = tokens_v[...].astype(F32)
    scale = lax.rsqrt(jnp.mean(values * values, axis=-1, keepdims=True) + 1e-06)
    out_ref[pl.ds(0, ROWS), :] = (values * scale * gain_v[...]).astype(BF)
    out_ref[pl.ds(ROWS, META), :] = jnp.full((META, WIDTH), -1.0, BF)
    out_ref[pl.ds(ROWS, META), 0:ROWS] = ids_v[...].astype(F32).astype(BF)
    out_ref[pl.ds(ROWS, META), 128 : 128 + ROWS] = route_v[...].astype(BF)
    for cp in moves:
        cp.wait()


def cut_kernel(place_ref, first_ref, *refs):
    outs, sem = refs[:-1], refs[-1]
    copies = []
    for k, out_ref in enumerate(outs):
        at = pl.multiple_of(((place_ref[1] + k) & (NZH - 1)) * PIECE, PIECE)
        cp = pltpu.make_async_copy(first_ref.at[pl.ds(at, PIECE)], out_ref, sem.at[k])
        cp.start()
        copies.append(cp)
    for cp in copies:
        cp.wait()


def pick_kernel(chosen_ref, *refs):
    pieces, outs, sem = refs[:NZH], refs[NZH : 2 * NZH], refs[-1]
    for k, out_ref in enumerate(outs):
        for j, piece in enumerate(pieces):

            @pl.when(chosen_ref[k] == j)
            def _(piece=piece, out_ref=out_ref, k=k):
                pltpu.make_async_copy(piece, out_ref, sem.at[k]).start()

    for k, out_ref in enumerate(outs):
        pltpu.make_async_copy(pieces[0], out_ref, sem.at[k]).wait()


def unpack_kernel(kind_ref, place_ref, *refs):
    whole, pieces, refs = refs[:3], refs[3 : 3 + NZH], refs[3 + NZH :]
    gate_ref, up_ref, down_ref, block, sem = refs
    kind = kind_ref[0]
    for chosen, ref in zip((kind == 0, kind == 1, kind >= 8), whole):

        @pl.when(chosen)
        def _(ref=ref):
            cp = pltpu.make_async_copy(ref, block, sem.at[NZH])
            cp.start()
            cp.wait()

    @pl.when((kind == 2) | (kind == 4))
    def _():
        copies = []
        for k, ref in enumerate(pieces):
            at = pl.multiple_of(((place_ref[1] - k) & (NZH - 1)) * PIECE, PIECE)
            cp = pltpu.make_async_copy(ref, block.at[pl.ds(at, PIECE)], sem.at[k])
            cp.start()
            copies.append(cp)
        for cp in copies:
            cp.wait()

    gate_ref[...] = block[0:SHARD, 0:HIDDEN]
    up_ref[...] = block[0:SHARD, HIDDEN:SIDE]
    down_ref[:, 0:SIDE] = block[SHARD : SHARD + DSHARD, :]
    for j in range(3):
        down_ref[32 * j : 32 * (j + 1), SIDE:WIDTH] = block[
            SHARD + DSHARD : PACK, 512 * j : 512 * (j + 1)
        ]


def dispatch_kernel(n, place_ref, *refs):
    sources, (out_ref, weight_ref) = refs[:n], refs[n:]
    zh, zl = place_ref[1], place_ref[3]
    before = lax.broadcasted_iota(jnp.int32, (128, 128), 0)
    after = lax.broadcasted_iota(jnp.int32, (128, 128), 1)
    upto = (before <= after).astype(F32).astype(BF)
    slot = (before & (MOST - 1)).astype(F32)
    for i, ref in enumerate(sources):
        ids = ref[ROWS : ROWS + META, 0:128].astype(F32)
        route = ref[ROWS : ROWS + META, 128:256].astype(F32)
        chosen, factor = [], []
        for p in range(PLACES):
            expert = ((p // NC * NZH + zh) * NC + p % NC) * NZL + zl
            named = jnp.where(ids == expert.astype(F32), 1.0, 0.0)
            chosen.append(jnp.sum(named, axis=0, keepdims=True))
            factor.append(jnp.sum(named * route, axis=0, keepdims=True))
        chosen = jnp.concatenate(chosen, axis=0)
        factor = jnp.concatenate(factor, axis=0)
        ranks = jnp.dot(chosen.astype(BF), upto, preferred_element_type=F32) - 1.0
        ranks = jnp.where(chosen > 0.0, ranks, -1.0)

        def spread(v):
            return jnp.broadcast_to(v[:, None, :], (PLACES, MOST, 128)).reshape(128, 128)

        taken = spread(ranks) == slot
        placing = jnp.where(taken, 1.0, 0.0).astype(BF)
        rows = jnp.dot(placing[:, 0:ROWS], ref[0:ROWS, :], preferred_element_type=F32).astype(BF)
        for p in range(PLACES):
            at = (p * n + i) * MOST
            out_ref[at : at + MOST, :] = rows[p * MOST : (p + 1) * MOST]
        weight_ref[i] = jnp.where(taken, spread(factor), 0.0).T.astype(BF)


def dispatch(place, sources):
    n = len(sources)
    return call(
        functools.partial(dispatch_kernel, n),
        [shape(PLACES * n * MOST, WIDTH), shape(n, 128, 128)],
        [SMEM] + [VMEM] * n,
        [VMEM] * 2,
        "dispatch",
        cost=pl.CostEstimate(flops=0, transcendentals=0, bytes_accessed=80 << 20),
    )(place, *sources)


def ffn_kernel(splits, block, place_ref, own_ref, swap_ref, *refs):
    n = len(splits)
    row_refs, out_refs = refs[:n], refs[n : 2 * n]
    side_v, down_v, rows_v, res_v, sem_w, sem_r, sem_o = refs[2 * n :]
    zl = place_ref[3]
    loads, gets, puts, starts, at = [], [], [], [], 0

    def load(src, dst):
        cp = pltpu.make_async_copy(src, dst, sem_w.at[len(loads)])
        cp.start()
        loads.append(cp)

    for i, rows in enumerate(splits):
        starts.append(at)
        cp = pltpu.make_async_copy(row_refs[i], rows_v.at[pl.ds(at, rows)], sem_r.at[i])
        cp.start()
        gets.append(cp)
        at += rows
    total = at
    for src, from_zl in ((own_ref, zl), (swap_ref, 1 - zl)):
        for y in range(NY):
            holder = y * NZL + from_zl
            base = pl.multiple_of(holder * SHARD, SHARD)
            load(src.at[y, pl.ds(0, SHARD)], side_v.at[pl.ds(base, SHARD)])
            base = pl.multiple_of(holder * DSHARD, DSHARD)
            load(src.at[y, pl.ds(SHARD, DSHARD)], down_v.at[pl.ds(base, DSHARD), 0:SIDE])
            for j in range(3):
                load(
                    src.at[y, pl.ds(SHARD + DSHARD, 32), 512 * j : 512 * (j + 1)],
                    down_v.at[pl.ds(base + 32 * j, 32), SIDE:WIDTH],
                )
    for cp in gets:
        cp.wait()
    for cp in loads:
        cp.wait()

    @pl.loop(0, total // block)
    def _(step):
        at = pl.multiple_of(step * block, block)
        both = jnp.dot(rows_v[pl.ds(at, block), :], side_v[...], preferred_element_type=F32)
        gate, up = both[:, 0:HIDDEN], both[:, HIDDEN:SIDE]
        hidden = (gate / (1.0 + jnp.exp(-gate)) * up).astype(BF)
        res_v[pl.ds(at, block), :] = jnp.dot(
            hidden, down_v[...], preferred_element_type=F32
        ).astype(BF)

    for i, rows in enumerate(splits):
        cp = pltpu.make_async_copy(res_v.at[pl.ds(starts[i], rows)], out_refs[i], sem_o.at[i])
        cp.start()
        puts.append(cp)
    for cp in puts:
        cp.wait()


def ffn(place, own, swapped, groups, block):
    splits = tuple(g.shape[0] for g in groups)
    total = sum(splits)
    return call(
        functools.partial(ffn_kernel, splits, block),
        [pltpu.HBM((r, WIDTH), BF) for r in splits],
        [SMEM] + [HBM] * (2 + len(groups)),
        [HBM] * len(groups),
        "expert_ffn",
        scratch=[
            pltpu.VMEM((WIDTH, SIDE), BF),
            pltpu.VMEM((HIDDEN, WIDTH), BF),
            pltpu.VMEM((total, WIDTH), BF),
            pltpu.VMEM((total, WIDTH), BF),
            pltpu.SemaphoreType.DMA((2 * NY * 5,)),
            pltpu.SemaphoreType.DMA((len(groups),)),
            pltpu.SemaphoreType.DMA((len(groups),)),
        ],
        cost=pl.CostEstimate(
            flops=6 * total * WIDTH * HIDDEN,
            transcendentals=total * HIDDEN,
            bytes_accessed=10 * WIDTH * HIDDEN,
        ),
    )(place, own, swapped, *groups)


def combine_kernel(n, weight_ref, back_ref, *outs):
    for i, out_ref in enumerate(outs):
        stack = jnp.concatenate(
            [back_ref[(p * n + i) * MOST : (p * n + i + 1) * MOST, :] for p in range(PLACES)],
            axis=0,
        )
        out_ref[...] = jnp.dot(
            weight_ref[i, 0:ROWS, :], stack, preferred_element_type=F32
        ).astype(out_ref.dtype)


def combine(weight, back, dtypes):
    n = len(dtypes)
    return call(
        functools.partial(combine_kernel, n),
        [shape(ROWS, WIDTH, dtype=t) for t in dtypes],
        [VMEM] * 2,
        [VMEM] * n,
        "combine",
    )(weight, back)


PLANE = ("x", "c")


def in_plane(rows):
    blocks = rows.reshape(PLACES, -1, WIDTH)
    return across(blocks, PLANE).reshape(-1, WIDTH)


def partner(value, axis, bit):
    count = {"x": NX, "zh": NZH, "c": NC, "zl": NZL}[axis]
    return lax.ppermute(value, axis, [(i, i ^ bit) for i in range(count)])


def joined(got, mine):
    return (got.astype(F32) + mine).astype(BF)


def body(
    tokens, norm_gain, expert_ids, route_weights, gate_weight, up_weight, down_weight, pair_list
):
    x_me, zh_me, c_me = (lax.axis_index(a) for a in EXPERT)
    zl_me = lax.axis_index("zl")
    place = jnp.stack([x_me, zh_me, c_me, zl_me]).astype(jnp.int32)

    near, own, other, first = call(
        prep_kernel,
        [shape(ROWS + META, WIDTH)] + [shape(PACK, SIDE)] * 3,
        [SMEM] + [HBM] * 7,
        [VMEM] * 4,
        "prep",
        scratch=[
            pltpu.VMEM((ROWS, WIDTH), BF),
            pltpu.VMEM((1, WIDTH), F32),
            pltpu.VMEM((TOP, ROWS), jnp.int32),
            pltpu.VMEM((TOP, ROWS), F32),
            pltpu.SemaphoreType.DMA((4,)),
            pltpu.SemaphoreType.DMA((18,)),
        ],
    )(
        place, *(
            pltpu.with_memory_space_constraint(v, pltpu.HBM)
            for v in (
                tokens, norm_gain[None, :], expert_ids.T, route_weights.T,
                gate_weight, up_weight, down_weight,
            )
        )
    )

    own_full = lax.all_gather(own, "y", axis=0, tiled=False)

    p1, m1 = along_z(near, 1), along_z(near, -1)
    p1, m1, other = fence(p1, m1, other)
    swapped = partner(other, "zl", 1)
    p2, m2 = along_z(p1, 1), along_z(m1, -1)
    d0, w0 = dispatch(place, (near, p1, m1))
    hx = across(first.reshape(NX, PACK // NX, SIDE), "x")
    hc = partner(first, "c", 1)
    d0, hx, hc = fence(d0, hx, hc)
    r0 = in_plane(d0)
    p2, m2, swapped = fence(p2, m2, swapped)
    p3, m3 = along_z(p2, 1), along_z(m2, -1)
    cut = call(
        cut_kernel, [shape(PIECE, SIDE)] * NZH, [SMEM, HBM], [HBM] * NZH, "cut",
        scratch=[pltpu.SemaphoreType.DMA((NZH,))],
    )(place, first)
    d1, w1 = dispatch(place, (p2, m2))
    d1, r0, p3, m3, swapped, *cut = fence(d1, r0, p3, m3, swapped, *cut)
    swap_full = lax.all_gather(swapped, "y", axis=0, tiled=False)
    r1 = in_plane(d1)
    far = along_z(p3, 1)
    held = [cut[0]] + [shift(cut[k], "zh", NZH, k) for k in range(1, NZH)]
    d2, w2 = dispatch(place, (p3, m3, far))
    d2, r1, held[1] = fence(d2, r1, held[1])
    r2 = in_plane(d2)
    x_turn = jnp.arange(NX, dtype=jnp.int32)
    x_from = jnp.take(pair_list, (x_turn * NZH + zh_me) * NC + c_me, mode="clip") >> 3
    hx = jnp.take(hx, x_from, axis=0, mode="clip")
    r0, r1, r2, hx, *held = fence(r0, r1, r2, hx, *held)
    hx = across(hx, "x").reshape(PACK, SIDE)
    (s2,) = ffn(place, own_full, swap_full, (r2,), 384)
    s2, r1, r0, hx, *held = fence(s2, r1, r0, hx, *held)
    b2 = in_plane(s2)
    s1, s0 = ffn(place, own_full, swap_full, (r1, r0), 320)
    turn = (zh_me + jnp.arange(NZH, dtype=jnp.int32)) & (NZH - 1)
    matched = jnp.take(pair_list, (x_me * NZH + turn) * NC + c_me, mode="clip")
    chosen = (zh_me - (matched >> 1)) & (NZH - 1)
    picked = call(
        pick_kernel, [shape(PIECE, SIDE)] * NZH, [SMEM] + [HBM] * NZH, [HBM] * NZH, "pick",
        scratch=[pltpu.SemaphoreType.DMA((NZH,))],
    )(chosen.astype(jnp.int32), *held)
    held = [picked[0]] + [shift(picked[k], "zh", NZH, k) for k in range(1, NZH)]
    b2, s1, s0, *held = fence(b2, s1, s0, *held)
    c_m3, c_p3, c_4 = combine(w2, b2, (F32, BF, BF))
    down, rise = along_z(c_4, -1), along_z(c_p3, 1)
    b1 = in_plane(s1)
    down = along_z(joined(down, c_m3), -1)
    b1, s0, rise = fence(b1, s0, rise)
    b0 = in_plane(s0)
    c_m2, c_p2 = combine(w1, b1, (F32, F32))
    down = along_z(joined(down, c_m2), -1)
    rise = along_z(joined(rise, c_p2), 1)

    me = (x_me * NZH + zh_me) * NC + c_me
    bits = jnp.sum(jnp.where(jnp.arange(pair_list.shape[0]) == me, pair_list ^ me, 0))
    new = call(
        unpack_kernel,
        [shape(SHARD, HIDDEN), shape(SHARD, HIDDEN), shape(DSHARD, WIDTH)],
        [SMEM] * 2 + [HBM] * 7,
        [VMEM] * 3,
        "unpack",
        scratch=[pltpu.VMEM((PACK, SIDE), BF), pltpu.SemaphoreType.DMA((NZH + 1,))],
    )(bits.astype(jnp.int32).reshape(1), place, first, hc, hx, *held)

    c_0, c_m1, c_p1 = combine(w0, b0, (F32, F32, F32))
    down = along_z(joined(down, c_m1), -1)
    rise = along_z(joined(rise, c_p1), 1)
    mixed = (down.astype(F32) + rise.astype(F32) + c_0).astype(BF)
    return (mixed, *(v[None] for v in new))


def solution(mesh):
    split = Mesh(mesh.devices.reshape(NX, NZH, NC, NY, NZL), EXPERT_DP)
    rows = P(EXPERT_DP, None)
    blocks = P(EXPERT, DP, None)
    return jax.shard_map(
        body,
        mesh=split,
        in_specs=(rows, P(), rows, rows, blocks, blocks, blocks, P()),
        out_specs=(rows, blocks, blocks, blocks),
        check_vma=False,
    )
```

```python
import functools

import jax
import jax.numpy as jnp
from jax import lax
from jax.experimental import pallas as pl
from jax.experimental.pallas import tpu as pltpu
from jax.sharding import Mesh
from jax.sharding import PartitionSpec as P

EXPERT = ("x", "zh", "c")
DP = ("y", "zl")
Z = ("zh", "zl")
EXPERT_DP = EXPERT + DP
MOST = 16
NX, NZH, NC, NY, NZL = 4, 4, 2, 4, 2
NZ = NZH * NZL
PLACES = NX * NC
ROWS, TOP, WIDTH, HIDDEN = 96, 8, 2048, 768
META = 8
SHARD, DSHARD = 256, 96
PACK = 384
HALF = PACK // 2
SIDE = 2 * HIDDEN
PIECE = PACK // NZH
BF = jnp.bfloat16
F32 = jnp.float32
GROUPS = ((0, -1, 1), (-2, 2), (-3, 3, 4))
VMEM = pl.BlockSpec(memory_space=pltpu.VMEM)
SMEM = pl.BlockSpec(memory_space=pltpu.SMEM)
HBM = pl.BlockSpec(memory_space=pltpu.HBM)
LIMIT = 48 << 20


def shift(value, axes, count, step):
    return lax.ppermute(value, axes, [(i, (i + step) % count) for i in range(count)])


def along_z(value, step):
    return shift(value, Z, NZ, step)


def along_y(value, step):
    return shift(value, "y", NY, step)


def flip(value, axis):
    return lax.ppermute(value, axis, [(0, 1), (1, 0)])


def across(value, axis):
    return lax.all_to_all(value, axis, split_axis=0, concat_axis=0, tiled=True)


def fence(*values):
    return lax.optimization_barrier(values)


def call(kernel, outs, in_specs, out_specs, name, scratch=(), cost=None):
    return pl.pallas_call(
        kernel,
        out_shape=outs,
        in_specs=in_specs,
        out_specs=out_specs,
        scratch_shapes=scratch,
        compiler_params=pltpu.CompilerParams(vmem_limit_bytes=LIMIT),
        cost_estimate=cost,
        name=name,
    )


def shape(*dims, dtype=BF):
    return jax.ShapeDtypeStruct(dims, dtype)


def prep_kernel(
    place_ref, tokens_ref, gain_ref, ids_ref, route_ref, gate_ref, up_ref, down_ref,
    out_ref, own_ref, other_ref, first_ref, tokens_v, gain_v, ids_v, route_v, sem_a, sem_b,
):
    zl = place_ref[3]
    reads, moves = [], []
    for src, dst in (
        (tokens_ref, tokens_v), (gain_ref, gain_v), (ids_ref, ids_v), (route_ref, route_v),
    ):
        cp = pltpu.make_async_copy(src, dst, sem_a.at[len(reads)])
        cp.start()
        reads.append(cp)

    def move(src, dst):
        cp = pltpu.make_async_copy(src, dst, sem_b.at[len(moves)])
        cp.start()
        moves.append(cp)

    for pack_ref, e in ((own_ref, zl), (other_ref, 1 - zl), (first_ref, 0)):
        move(gate_ref.at[e], pack_ref.at[pl.ds(0, SHARD), 0:HIDDEN])
        move(up_ref.at[e], pack_ref.at[pl.ds(0, SHARD), HIDDEN:SIDE])
        move(down_ref.at[e, :, 0:SIDE], pack_ref.at[pl.ds(SHARD, DSHARD), :])
        for j in range(3):
            move(
                down_ref.at[e, pl.ds(32 * j, 32), SIDE:WIDTH],
                pack_ref.at[pl.ds(SHARD + DSHARD, 32), 512 * j : 512 * (j + 1)],
            )
    for cp in reads:
        cp.wait()
    values = tokens_v[...].astype(F32)
    scale = lax.rsqrt(jnp.mean(values * values, axis=-1, keepdims=True) + 1e-06)
    out_ref[pl.ds(0, ROWS), :] = (values * scale * gain_v[...]).astype(BF)
    out_ref[pl.ds(ROWS, META), :] = jnp.full((META, WIDTH), -1.0, BF)
    out_ref[pl.ds(ROWS, META), 0:ROWS] = ids_v[...].astype(F32).astype(BF)
    out_ref[pl.ds(ROWS, META), 128 : 128 + ROWS] = route_v[...].astype(BF)
    for cp in moves:
        cp.wait()


def cut_kernel(place_ref, first_ref, *refs):
    outs, sem = refs[:-1], refs[-1]
    copies = []
    for k, out_ref in enumerate(outs):
        at = pl.multiple_of(((place_ref[1] + k) & (NZH - 1)) * PIECE, PIECE)
        cp = pltpu.make_async_copy(first_ref.at[pl.ds(at, PIECE)], out_ref, sem.at[k])
        cp.start()
        copies.append(cp)
    for cp in copies:
        cp.wait()


def pick_kernel(chosen_ref, *refs):
    pieces, outs, sem = refs[:NZH], refs[NZH : 2 * NZH], refs[-1]
    for k, out_ref in enumerate(outs):
        for j, piece in enumerate(pieces):

            @pl.when(chosen_ref[k] == j)
            def _(piece=piece, out_ref=out_ref, k=k):
                pltpu.make_async_copy(piece, out_ref, sem.at[k]).start()

    for k, out_ref in enumerate(outs):
        pltpu.make_async_copy(pieces[0], out_ref, sem.at[k]).wait()


def unpack_kernel(kind_ref, place_ref, *refs):
    whole, pieces, refs = refs[:3], refs[3 : 3 + NZH], refs[3 + NZH :]
    gate_ref, up_ref, down_ref, block, sem = refs
    kind = kind_ref[0]
    for chosen, ref in zip((kind == 0, kind == 1, kind >= 8), whole):

        @pl.when(chosen)
        def _(ref=ref):
            cp = pltpu.make_async_copy(ref, block, sem.at[NZH])
            cp.start()
            cp.wait()

    @pl.when((kind == 2) | (kind == 4))
    def _():
        copies = []
        for k, ref in enumerate(pieces):
            at = pl.multiple_of(((place_ref[1] - k) & (NZH - 1)) * PIECE, PIECE)
            cp = pltpu.make_async_copy(ref, block.at[pl.ds(at, PIECE)], sem.at[k])
            cp.start()
            copies.append(cp)
        for cp in copies:
            cp.wait()

    gate_ref[...] = block[0:SHARD, 0:HIDDEN]
    up_ref[...] = block[0:SHARD, HIDDEN:SIDE]
    down_ref[:, 0:SIDE] = block[SHARD : SHARD + DSHARD, :]
    for j in range(3):
        down_ref[32 * j : 32 * (j + 1), SIDE:WIDTH] = block[
            SHARD + DSHARD : PACK, 512 * j : 512 * (j + 1)
        ]


def dispatch_kernel(n, place_ref, *refs):
    sources, (out_ref, weight_ref) = refs[:n], refs[n:]
    zh, zl = place_ref[1], place_ref[3]
    before = lax.broadcasted_iota(jnp.int32, (128, 128), 0)
    after = lax.broadcasted_iota(jnp.int32, (128, 128), 1)
    upto = (before <= after).astype(F32).astype(BF)
    slot = (before & (MOST - 1)).astype(F32)
    for i, ref in enumerate(sources):
        ids = ref[ROWS : ROWS + META, 0:128].astype(F32)
        route = ref[ROWS : ROWS + META, 128:256].astype(F32)
        chosen, factor = [], []
        for p in range(PLACES):
            expert = ((p // NC * NZH + zh) * NC + p % NC) * NZL + zl
            named = jnp.where(ids == expert.astype(F32), 1.0, 0.0)
            chosen.append(jnp.sum(named, axis=0, keepdims=True))
            factor.append(jnp.sum(named * route, axis=0, keepdims=True))
        chosen = jnp.concatenate(chosen, axis=0)
        factor = jnp.concatenate(factor, axis=0)
        ranks = jnp.dot(chosen.astype(BF), upto, preferred_element_type=F32) - 1.0
        ranks = jnp.where(chosen > 0.0, ranks, -1.0)

        def spread(v):
            return jnp.broadcast_to(v[:, None, :], (PLACES, MOST, 128)).reshape(128, 128)

        taken = spread(ranks) == slot
        placing = jnp.where(taken, 1.0, 0.0).astype(BF)
        rows = jnp.dot(placing[:, 0:ROWS], ref[0:ROWS, :], preferred_element_type=F32).astype(BF)
        for p in range(PLACES):
            at = (p * n + i) * MOST
            out_ref[at : at + MOST, :] = rows[p * MOST : (p + 1) * MOST]
        weight_ref[i] = jnp.where(taken, spread(factor), 0.0).T.astype(BF)


def dispatch(place, sources):
    n = len(sources)
    return call(
        functools.partial(dispatch_kernel, n),
        [shape(PLACES * n * MOST, WIDTH), shape(n, 128, 128)],
        [SMEM] + [VMEM] * n,
        [VMEM] * 2,
        "dispatch",
        cost=pl.CostEstimate(flops=0, transcendentals=0, bytes_accessed=80 << 20),
    )(place, *sources)


def ffn_kernel(splits, block, place_ref, own_ref, swap_ref, *refs):
    n = len(splits)
    row_refs, out_refs = refs[:n], refs[n : 2 * n]
    side_v, down_v, rows_v, res_v, sem_w, sem_r, sem_o = refs[2 * n :]
    zl = place_ref[3]
    loads, gets, puts, starts, at = [], [], [], [], 0

    def load(src, dst):
        cp = pltpu.make_async_copy(src, dst, sem_w.at[len(loads)])
        cp.start()
        loads.append(cp)

    for i, rows in enumerate(splits):
        starts.append(at)
        cp = pltpu.make_async_copy(row_refs[i], rows_v.at[pl.ds(at, rows)], sem_r.at[i])
        cp.start()
        gets.append(cp)
        at += rows
    total = at
    for src, from_zl in ((own_ref, zl), (swap_ref, 1 - zl)):
        for y in range(NY):
            holder = y * NZL + from_zl
            base = pl.multiple_of(holder * SHARD, SHARD)
            load(src.at[y, pl.ds(0, SHARD)], side_v.at[pl.ds(base, SHARD)])
            base = pl.multiple_of(holder * DSHARD, DSHARD)
            load(src.at[y, pl.ds(SHARD, DSHARD)], down_v.at[pl.ds(base, DSHARD), 0:SIDE])
            for j in range(3):
                load(
                    src.at[y, pl.ds(SHARD + DSHARD, 32), 512 * j : 512 * (j + 1)],
                    down_v.at[pl.ds(base + 32 * j, 32), SIDE:WIDTH],
                )
    for cp in gets:
        cp.wait()
    for cp in loads:
        cp.wait()

    @pl.loop(0, total // block)
    def _(step):
        at = pl.multiple_of(step * block, block)
        both = jnp.dot(rows_v[pl.ds(at, block), :], side_v[...], preferred_element_type=F32)
        gate, up = both[:, 0:HIDDEN], both[:, HIDDEN:SIDE]
        hidden = (gate / (1.0 + jnp.exp(-gate)) * up).astype(BF)
        res_v[pl.ds(at, block), :] = jnp.dot(
            hidden, down_v[...], preferred_element_type=F32
        ).astype(BF)

    for i, rows in enumerate(splits):
        cp = pltpu.make_async_copy(res_v.at[pl.ds(starts[i], rows)], out_refs[i], sem_o.at[i])
        cp.start()
        puts.append(cp)
    for cp in puts:
        cp.wait()


def ffn(place, own, swapped, groups, block):
    splits = tuple(g.shape[0] for g in groups)
    total = sum(splits)
    return call(
        functools.partial(ffn_kernel, splits, block),
        [pltpu.HBM((r, WIDTH), BF) for r in splits],
        [SMEM] + [HBM] * (2 + len(groups)),
        [HBM] * len(groups),
        "expert_ffn",
        scratch=[
            pltpu.VMEM((WIDTH, SIDE), BF),
            pltpu.VMEM((HIDDEN, WIDTH), BF),
            pltpu.VMEM((total, WIDTH), BF),
            pltpu.VMEM((total, WIDTH), BF),
            pltpu.SemaphoreType.DMA((2 * NY * 5,)),
            pltpu.SemaphoreType.DMA((len(groups),)),
            pltpu.SemaphoreType.DMA((len(groups),)),
        ],
        cost=pl.CostEstimate(
            flops=6 * total * WIDTH * HIDDEN,
            transcendentals=total * HIDDEN,
            bytes_accessed=10 * WIDTH * HIDDEN,
        ),
    )(place, own, swapped, *groups)


def combine_kernel(n, weight_ref, back_ref, *outs):
    for i, out_ref in enumerate(outs):
        stack = jnp.concatenate(
            [back_ref[(p * n + i) * MOST : (p * n + i + 1) * MOST, :] for p in range(PLACES)],
            axis=0,
        )
        out_ref[...] = jnp.dot(
            weight_ref[i, 0:ROWS, :], stack, preferred_element_type=F32
        ).astype(out_ref.dtype)


def combine(weight, back, dtypes):
    n = len(dtypes)
    return call(
        functools.partial(combine_kernel, n),
        [shape(ROWS, WIDTH, dtype=t) for t in dtypes],
        [VMEM] * 2,
        [VMEM] * n,
        "combine",
    )(weight, back)


PLANE = ("x", "c")


def in_plane(rows):
    blocks = rows.reshape(PLACES, -1, WIDTH)
    return across(blocks, PLANE).reshape(-1, WIDTH)


def partner(value, axis, bit):
    count = {"x": NX, "zh": NZH, "c": NC, "zl": NZL}[axis]
    return lax.ppermute(value, axis, [(i, i ^ bit) for i in range(count)])


def joined(got, mine):
    return (got.astype(F32) + mine).astype(BF)


def body(
    tokens, norm_gain, expert_ids, route_weights, gate_weight, up_weight, down_weight, pair_list
):
    x_me, zh_me, c_me = (lax.axis_index(a) for a in EXPERT)
    zl_me = lax.axis_index("zl")
    place = jnp.stack([x_me, zh_me, c_me, zl_me]).astype(jnp.int32)

    near, own, other, first = call(
        prep_kernel,
        [shape(ROWS + META, WIDTH)] + [shape(PACK, SIDE)] * 3,
        [SMEM] + [HBM] * 7,
        [VMEM] * 4,
        "prep",
        scratch=[
            pltpu.VMEM((ROWS, WIDTH), BF),
            pltpu.VMEM((1, WIDTH), F32),
            pltpu.VMEM((TOP, ROWS), jnp.int32),
            pltpu.VMEM((TOP, ROWS), F32),
            pltpu.SemaphoreType.DMA((4,)),
            pltpu.SemaphoreType.DMA((18,)),
        ],
    )(
        place, *(
            pltpu.with_memory_space_constraint(v, pltpu.HBM)
            for v in (
                tokens, norm_gain[None, :], expert_ids.T, route_weights.T,
                gate_weight, up_weight, down_weight,
            )
        )
    )

    own_full = lax.all_gather(own, "y", axis=0, tiled=False)

    p1, m1 = along_z(near, 1), along_z(near, -1)
    p1, m1, other = fence(p1, m1, other)
    swapped = partner(other, "zl", 1)
    p2, m2 = along_z(p1, 1), along_z(m1, -1)
    d0, w0 = dispatch(place, (near, p1, m1))
    hx = across(first.reshape(NX, PACK // NX, SIDE), "x")
    hc = partner(first, "c", 1)
    d0, hx, hc = fence(d0, hx, hc)
    r0 = in_plane(d0)
    p2, m2, swapped = fence(p2, m2, swapped)
    p3, m3 = along_z(p2, 1), along_z(m2, -1)
    d1, w1 = dispatch(place, (p2, m2))
    d1, r0, p3, m3, swapped = fence(d1, r0, p3, m3, swapped)
    swap_full = lax.all_gather(swapped, "y", axis=0, tiled=False)
    r1 = in_plane(d1)
    far = along_z(p3, 1)
    far, first = fence(far, first)
    cut = call(
        cut_kernel, [shape(PIECE, SIDE)] * NZH, [SMEM, HBM], [HBM] * NZH, "cut",
        scratch=[pltpu.SemaphoreType.DMA((NZH,))],
    )(place, first)
    held = [cut[0]] + [shift(cut[k], "zh", NZH, k) for k in range(1, NZH)]
    d2, w2 = dispatch(place, (p3, m3, far))
    d2, r1 = fence(d2, r1)
    r2 = in_plane(d2)
    x_turn = jnp.arange(NX, dtype=jnp.int32)
    x_from = jnp.take(pair_list, (x_turn * NZH + zh_me) * NC + c_me, mode="clip") >> 3
    hx = jnp.take(hx, x_from, axis=0, mode="clip")
    turn = (zh_me + jnp.arange(NZH, dtype=jnp.int32)) & (NZH - 1)
    matched = jnp.take(pair_list, (x_me * NZH + turn) * NC + c_me, mode="clip")
    chosen = ((zh_me - (matched >> 1)) & (NZH - 1)).astype(jnp.int32)
    r0, r1, r2, first, hx, chosen, *held = fence(r0, r1, r2, first, hx, chosen, *held)
    hx = across(hx, "x").reshape(PACK, SIDE)
    (s2,) = ffn(place, own_full, swap_full, (r2,), 384)
    s2, r1, r0, hx, *held = fence(s2, r1, r0, hx, *held)
    b2 = in_plane(s2)
    s1, s0 = ffn(place, own_full, swap_full, (r1, r0), 320)
    picked = call(
        pick_kernel, [shape(PIECE, SIDE)] * NZH, [SMEM] + [HBM] * NZH, [HBM] * NZH, "pick",
        scratch=[pltpu.SemaphoreType.DMA((NZH,))],
    )(chosen, *held)
    held = [picked[0]] + [shift(picked[k], "zh", NZH, k) for k in range(1, NZH)]
    b2, s1, s0, *held = fence(b2, s1, s0, *held)
    c_m3, c_p3, c_4 = combine(w2, b2, (F32, BF, BF))
    down, rise = along_z(c_4, -1), along_z(c_p3, 1)
    b1 = in_plane(s1)
    down = along_z(joined(down, c_m3), -1)
    b1, s0, rise = fence(b1, s0, rise)
    b0 = in_plane(s0)
    c_m2, c_p2 = combine(w1, b1, (F32, F32))
    down = along_z(joined(down, c_m2), -1)
    rise = along_z(joined(rise, c_p2), 1)

    me = (x_me * NZH + zh_me) * NC + c_me
    bits = jnp.sum(jnp.where(jnp.arange(pair_list.shape[0]) == me, pair_list ^ me, 0))
    new = call(
        unpack_kernel,
        [shape(SHARD, HIDDEN), shape(SHARD, HIDDEN), shape(DSHARD, WIDTH)],
        [SMEM] * 2 + [HBM] * 7,
        [VMEM] * 3,
        "unpack",
        scratch=[pltpu.VMEM((PACK, SIDE), BF), pltpu.SemaphoreType.DMA((NZH + 1,))],
    )(bits.astype(jnp.int32).reshape(1), place, first, hc, hx, *held)

    c_0, c_m1, c_p1 = combine(w0, b0, (F32, F32, F32))
    down = along_z(joined(down, c_m1), -1)
    rise = along_z(joined(rise, c_p1), 1)
    mixed = (down.astype(F32) + rise.astype(F32) + c_0).astype(BF)
    return (mixed, *(v[None] for v in new))


def solution(mesh):
    split = Mesh(mesh.devices.reshape(NX, NZH, NC, NY, NZL), EXPERT_DP)
    rows = P(EXPERT_DP, None)
    blocks = P(EXPERT, DP, None)
    return jax.shard_map(
        body,
        mesh=split,
        in_specs=(rows, P(), rows, rows, blocks, blocks, blocks, P()),
        out_specs=(rows, blocks, blocks, blocks),
        check_vma=False,
    )
```

```python
import functools

import jax
import jax.numpy as jnp
from jax import lax
from jax.experimental import pallas as pl
from jax.experimental.pallas import tpu as pltpu
from jax.sharding import Mesh
from jax.sharding import PartitionSpec as P

EXPERT = ("x", "zh", "c")
DP = ("y", "zl")
Z = ("zh", "zl")
EXPERT_DP = EXPERT + DP
MOST = 16
NX, NZH, NC, NY, NZL = 4, 4, 2, 4, 2
NZ = NZH * NZL
PLACES = NX * NC
ROWS, TOP, WIDTH, HIDDEN = 96, 8, 2048, 768
META = 8
SHARD, DSHARD = 256, 96
PACK = 384
HALF = PACK // 2
SIDE = 2 * HIDDEN
PIECE = PACK // NZH
BF = jnp.bfloat16
F32 = jnp.float32
GROUPS = ((0, -1, 1), (-2, 2), (-3, 3, 4))
VMEM = pl.BlockSpec(memory_space=pltpu.VMEM)
SMEM = pl.BlockSpec(memory_space=pltpu.SMEM)
HBM = pl.BlockSpec(memory_space=pltpu.HBM)
LIMIT = 48 << 20


def shift(value, axes, count, step):
    return lax.ppermute(value, axes, [(i, (i + step) % count) for i in range(count)])


def along_z(value, step):
    return shift(value, Z, NZ, step)


def along_y(value, step):
    return shift(value, "y", NY, step)


def flip(value, axis):
    return lax.ppermute(value, axis, [(0, 1), (1, 0)])


def across(value, axis):
    return lax.all_to_all(value, axis, split_axis=0, concat_axis=0, tiled=True)


def fence(*values):
    return lax.optimization_barrier(values)


def call(kernel, outs, in_specs, out_specs, name, scratch=(), cost=None):
    return pl.pallas_call(
        kernel,
        out_shape=outs,
        in_specs=in_specs,
        out_specs=out_specs,
        scratch_shapes=scratch,
        compiler_params=pltpu.CompilerParams(vmem_limit_bytes=LIMIT),
        cost_estimate=cost,
        name=name,
    )


def shape(*dims, dtype=BF):
    return jax.ShapeDtypeStruct(dims, dtype)


def prep_kernel(
    place_ref, tokens_ref, gain_ref, ids_ref, route_ref, gate_ref, up_ref, down_ref,
    out_ref, own_ref, other_ref, first_ref, tokens_v, gain_v, ids_v, route_v, sem_a, sem_b,
):
    zl = place_ref[3]
    reads, moves = [], []
    for src, dst in (
        (tokens_ref, tokens_v), (gain_ref, gain_v), (ids_ref, ids_v), (route_ref, route_v),
    ):
        cp = pltpu.make_async_copy(src, dst, sem_a.at[len(reads)])
        cp.start()
        reads.append(cp)

    def move(src, dst):
        cp = pltpu.make_async_copy(src, dst, sem_b.at[len(moves)])
        cp.start()
        moves.append(cp)

    for pack_ref, e in ((own_ref, zl), (other_ref, 1 - zl), (first_ref, 0)):
        move(gate_ref.at[e], pack_ref.at[pl.ds(0, SHARD), 0:HIDDEN])
        move(up_ref.at[e], pack_ref.at[pl.ds(0, SHARD), HIDDEN:SIDE])
        move(down_ref.at[e, :, 0:SIDE], pack_ref.at[pl.ds(SHARD, DSHARD), :])
        for j in range(3):
            move(
                down_ref.at[e, pl.ds(32 * j, 32), SIDE:WIDTH],
                pack_ref.at[pl.ds(SHARD + DSHARD, 32), 512 * j : 512 * (j + 1)],
            )
    for cp in reads:
        cp.wait()
    values = tokens_v[...].astype(F32)
    scale = lax.rsqrt(jnp.mean(values * values, axis=-1, keepdims=True) + 1e-06)
    out_ref[pl.ds(0, ROWS), :] = (values * scale * gain_v[...]).astype(BF)
    out_ref[pl.ds(ROWS, META), :] = jnp.full((META, WIDTH), -1.0, BF)
    out_ref[pl.ds(ROWS, META), 0:ROWS] = ids_v[...].astype(F32).astype(BF)
    out_ref[pl.ds(ROWS, META), 128 : 128 + ROWS] = route_v[...].astype(BF)
    for cp in moves:
        cp.wait()


def cut_kernel(place_ref, first_ref, *refs):
    outs, sem = refs[:-1], refs[-1]
    copies = []
    for k, out_ref in enumerate(outs):
        at = pl.multiple_of(((place_ref[1] + k) & (NZH - 1)) * PIECE, PIECE)
        cp = pltpu.make_async_copy(first_ref.at[pl.ds(at, PIECE)], out_ref, sem.at[k])
        cp.start()
        copies.append(cp)
    for cp in copies:
        cp.wait()


def pick_kernel(chosen_ref, *refs):
    pieces, outs, sem = refs[:NZH], refs[NZH : 2 * NZH], refs[-1]
    for k, out_ref in enumerate(outs):
        for j, piece in enumerate(pieces):

            @pl.when(chosen_ref[k] == j)
            def _(piece=piece, out_ref=out_ref, k=k):
                pltpu.make_async_copy(piece, out_ref, sem.at[k]).start()

    for k, out_ref in enumerate(outs):
        pltpu.make_async_copy(pieces[0], out_ref, sem.at[k]).wait()


def unpack_kernel(kind_ref, place_ref, *refs):
    whole, pieces, refs = refs[:3], refs[3 : 3 + NZH], refs[3 + NZH :]
    gate_ref, up_ref, down_ref, block, sem = refs
    kind = kind_ref[0]
    for chosen, ref in zip((kind == 0, kind == 1, kind >= 8), whole):

        @pl.when(chosen)
        def _(ref=ref):
            cp = pltpu.make_async_copy(ref, block, sem.at[NZH])
            cp.start()
            cp.wait()

    @pl.when((kind == 2) | (kind == 4))
    def _():
        copies = []
        for k, ref in enumerate(pieces):
            at = pl.multiple_of(((place_ref[1] - k) & (NZH - 1)) * PIECE, PIECE)
            cp = pltpu.make_async_copy(ref, block.at[pl.ds(at, PIECE)], sem.at[k])
            cp.start()
            copies.append(cp)
        for cp in copies:
            cp.wait()

    gate_ref[...] = block[0:SHARD, 0:HIDDEN]
    up_ref[...] = block[0:SHARD, HIDDEN:SIDE]
    down_ref[:, 0:SIDE] = block[SHARD : SHARD + DSHARD, :]
    for j in range(3):
        down_ref[32 * j : 32 * (j + 1), SIDE:WIDTH] = block[
            SHARD + DSHARD : PACK, 512 * j : 512 * (j + 1)
        ]


def dispatch_kernel(n, place_ref, *refs):
    sources, (out_ref, weight_ref) = refs[:n], refs[n:]
    zh, zl = place_ref[1], place_ref[3]
    before = lax.broadcasted_iota(jnp.int32, (128, 128), 0)
    after = lax.broadcasted_iota(jnp.int32, (128, 128), 1)
    upto = (before <= after).astype(F32).astype(BF)
    slot = (before & (MOST - 1)).astype(F32)
    for i, ref in enumerate(sources):
        ids = ref[ROWS : ROWS + META, 0:128].astype(F32)
        route = ref[ROWS : ROWS + META, 128:256].astype(F32)
        chosen, factor = [], []
        for p in range(PLACES):
            expert = ((p // NC * NZH + zh) * NC + p % NC) * NZL + zl
            named = jnp.where(ids == expert.astype(F32), 1.0, 0.0)
            chosen.append(jnp.sum(named, axis=0, keepdims=True))
            factor.append(jnp.sum(named * route, axis=0, keepdims=True))
        chosen = jnp.concatenate(chosen, axis=0)
        factor = jnp.concatenate(factor, axis=0)
        ranks = jnp.dot(chosen.astype(BF), upto, preferred_element_type=F32) - 1.0
        ranks = jnp.where(chosen > 0.0, ranks, -1.0)

        def spread(v):
            return jnp.broadcast_to(v[:, None, :], (PLACES, MOST, 128)).reshape(128, 128)

        taken = spread(ranks) == slot
        placing = jnp.where(taken, 1.0, 0.0).astype(BF)
        rows = jnp.dot(placing[:, 0:ROWS], ref[0:ROWS, :], preferred_element_type=F32).astype(BF)
        for p in range(PLACES):
            at = (p * n + i) * MOST
            out_ref[at : at + MOST, :] = rows[p * MOST : (p + 1) * MOST]
        weight_ref[i] = jnp.where(taken, spread(factor), 0.0).T.astype(BF)


def dispatch(place, sources):
    n = len(sources)
    return call(
        functools.partial(dispatch_kernel, n),
        [shape(PLACES * n * MOST, WIDTH), shape(n, 128, 128)],
        [SMEM] + [VMEM] * n,
        [VMEM] * 2,
        "dispatch",
        cost=pl.CostEstimate(flops=0, transcendentals=0, bytes_accessed=80 << 20),
    )(place, *sources)


def ffn_kernel(splits, block, place_ref, own_ref, swap_ref, *refs):
    n = len(splits)
    row_refs, out_refs = refs[:n], refs[n : 2 * n]
    side_v, down_v, rows_v, res_v, sem_w, sem_r, sem_o = refs[2 * n :]
    zl = place_ref[3]
    loads, gets, puts, starts, at = [], [], [], [], 0

    def load(src, dst):
        cp = pltpu.make_async_copy(src, dst, sem_w.at[len(loads)])
        cp.start()
        loads.append(cp)

    for i, rows in enumerate(splits):
        starts.append(at)
        cp = pltpu.make_async_copy(row_refs[i], rows_v.at[pl.ds(at, rows)], sem_r.at[i])
        cp.start()
        gets.append(cp)
        at += rows
    total = at
    for src, from_zl in ((own_ref, zl), (swap_ref, 1 - zl)):
        for y in range(NY):
            holder = y * NZL + from_zl
            base = pl.multiple_of(holder * SHARD, SHARD)
            load(src.at[y, pl.ds(0, SHARD)], side_v.at[pl.ds(base, SHARD)])
            base = pl.multiple_of(holder * DSHARD, DSHARD)
            load(src.at[y, pl.ds(SHARD, DSHARD)], down_v.at[pl.ds(base, DSHARD), 0:SIDE])
            for j in range(3):
                load(
                    src.at[y, pl.ds(SHARD + DSHARD, 32), 512 * j : 512 * (j + 1)],
                    down_v.at[pl.ds(base + 32 * j, 32), SIDE:WIDTH],
                )
    for cp in gets:
        cp.wait()
    for cp in loads:
        cp.wait()

    @pl.loop(0, total // block)
    def _(step):
        at = pl.multiple_of(step * block, block)
        both = jnp.dot(rows_v[pl.ds(at, block), :], side_v[...], preferred_element_type=F32)
        gate, up = both[:, 0:HIDDEN], both[:, HIDDEN:SIDE]
        hidden = (gate / (1.0 + jnp.exp(-gate)) * up).astype(BF)
        res_v[pl.ds(at, block), :] = jnp.dot(
            hidden, down_v[...], preferred_element_type=F32
        ).astype(BF)

    for i, rows in enumerate(splits):
        cp = pltpu.make_async_copy(res_v.at[pl.ds(starts[i], rows)], out_refs[i], sem_o.at[i])
        cp.start()
        puts.append(cp)
    for cp in puts:
        cp.wait()


def ffn(place, own, swapped, groups, block):
    splits = tuple(g.shape[0] for g in groups)
    total = sum(splits)
    return call(
        functools.partial(ffn_kernel, splits, block),
        [pltpu.HBM((r, WIDTH), BF) for r in splits],
        [SMEM] + [HBM] * (2 + len(groups)),
        [HBM] * len(groups),
        "expert_ffn",
        scratch=[
            pltpu.VMEM((WIDTH, SIDE), BF),
            pltpu.VMEM((HIDDEN, WIDTH), BF),
            pltpu.VMEM((total, WIDTH), BF),
            pltpu.VMEM((total, WIDTH), BF),
            pltpu.SemaphoreType.DMA((2 * NY * 5,)),
            pltpu.SemaphoreType.DMA((len(groups),)),
            pltpu.SemaphoreType.DMA((len(groups),)),
        ],
        cost=pl.CostEstimate(
            flops=6 * total * WIDTH * HIDDEN,
            transcendentals=total * HIDDEN,
            bytes_accessed=10 * WIDTH * HIDDEN,
        ),
    )(place, own, swapped, *groups)


def combine_kernel(n, weight_ref, back_ref, *outs):
    for i, out_ref in enumerate(outs):
        stack = jnp.concatenate(
            [back_ref[(p * n + i) * MOST : (p * n + i + 1) * MOST, :] for p in range(PLACES)],
            axis=0,
        )
        out_ref[...] = jnp.dot(
            weight_ref[i, 0:ROWS, :], stack, preferred_element_type=F32
        ).astype(out_ref.dtype)


def combine(weight, back, dtypes):
    n = len(dtypes)
    return call(
        functools.partial(combine_kernel, n),
        [shape(ROWS, WIDTH, dtype=t) for t in dtypes],
        [VMEM] * 2,
        [VMEM] * n,
        "combine",
    )(weight, back)


PLANE = ("x", "c")


def in_plane(rows):
    blocks = rows.reshape(PLACES, -1, WIDTH)
    return across(blocks, PLANE).reshape(-1, WIDTH)


def partner(value, axis, bit):
    count = {"x": NX, "zh": NZH, "c": NC, "zl": NZL}[axis]
    return lax.ppermute(value, axis, [(i, i ^ bit) for i in range(count)])


def joined(got, mine):
    return (got.astype(F32) + mine).astype(BF)


def body(
    tokens, norm_gain, expert_ids, route_weights, gate_weight, up_weight, down_weight, pair_list
):
    x_me, zh_me, c_me = (lax.axis_index(a) for a in EXPERT)
    zl_me = lax.axis_index("zl")
    place = jnp.stack([x_me, zh_me, c_me, zl_me]).astype(jnp.int32)

    near, own, other, first = call(
        prep_kernel,
        [shape(ROWS + META, WIDTH)] + [shape(PACK, SIDE)] * 3,
        [SMEM] + [HBM] * 7,
        [VMEM] * 4,
        "prep",
        scratch=[
            pltpu.VMEM((ROWS, WIDTH), BF),
            pltpu.VMEM((1, WIDTH), F32),
            pltpu.VMEM((TOP, ROWS), jnp.int32),
            pltpu.VMEM((TOP, ROWS), F32),
            pltpu.SemaphoreType.DMA((4,)),
            pltpu.SemaphoreType.DMA((18,)),
        ],
    )(
        place, *(
            pltpu.with_memory_space_constraint(v, pltpu.HBM)
            for v in (
                tokens, norm_gain[None, :], expert_ids.T, route_weights.T,
                gate_weight, up_weight, down_weight,
            )
        )
    )

    own_full = lax.all_gather(own, "y", axis=0, tiled=False)

    p1, m1 = along_z(near, 1), along_z(near, -1)
    p1, m1, other = fence(p1, m1, other)
    swapped = partner(other, "zl", 1)
    p2, m2 = along_z(p1, 1), along_z(m1, -1)
    d0, w0 = dispatch(place, (near, p1, m1))
    hx = across(first.reshape(NX, PACK // NX, SIDE), "x")
    hc = partner(first, "c", 1)
    d0, hx, hc = fence(d0, hx, hc)
    r0 = in_plane(d0)
    p2, m2, swapped = fence(p2, m2, swapped)
    p3, m3 = along_z(p2, 1), along_z(m2, -1)
    cut = call(
        cut_kernel, [shape(PIECE, SIDE)] * NZH, [SMEM, HBM], [VMEM] * NZH, "cut",
        scratch=[pltpu.SemaphoreType.DMA((NZH,))],
    )(place, first)
    d1, w1 = dispatch(place, (p2, m2))
    d1, r0, p3, m3, swapped, *cut = fence(d1, r0, p3, m3, swapped, *cut)
    swap_full = lax.all_gather(swapped, "y", axis=0, tiled=False)
    r1 = in_plane(d1)
    far = along_z(p3, 1)
    far, first, *cut = fence(far, first, *cut)
    held = [cut[0]] + [shift(cut[k], "zh", NZH, k) for k in range(1, NZH)]
    d2, w2 = dispatch(place, (p3, m3, far))
    d2, r1 = fence(d2, r1)
    r2 = in_plane(d2)
    x_turn = jnp.arange(NX, dtype=jnp.int32)
    x_from = jnp.take(pair_list, (x_turn * NZH + zh_me) * NC + c_me, mode="clip") >> 3
    hx = jnp.take(hx, x_from, axis=0, mode="clip")
    turn = (zh_me + jnp.arange(NZH, dtype=jnp.int32)) & (NZH - 1)
    matched = jnp.take(pair_list, (x_me * NZH + turn) * NC + c_me, mode="clip")
    chosen = ((zh_me - (matched >> 1)) & (NZH - 1)).astype(jnp.int32)
    r0, r1, r2, first, hx, chosen, *held = fence(r0, r1, r2, first, hx, chosen, *held)
    hx = across(hx, "x").reshape(PACK, SIDE)
    (s2,) = ffn(place, own_full, swap_full, (r2,), 384)
    s2, r1, r0, hx, *held = fence(s2, r1, r0, hx, *held)
    b2 = in_plane(s2)
    s1, s0 = ffn(place, own_full, swap_full, (r1, r0), 320)
    picked = call(
        pick_kernel, [shape(PIECE, SIDE)] * NZH, [SMEM] + [HBM] * NZH, [VMEM] * NZH, "pick",
        scratch=[pltpu.SemaphoreType.DMA((NZH,))],
    )(chosen, *held)
    held = [picked[0]] + [shift(picked[k], "zh", NZH, k) for k in range(1, NZH)]
    b2, s1, s0, *held = fence(b2, s1, s0, *held)
    c_m3, c_p3, c_4 = combine(w2, b2, (F32, BF, BF))
    down, rise = along_z(c_4, -1), along_z(c_p3, 1)
    b1 = in_plane(s1)
    down = along_z(joined(down, c_m3), -1)
    b1, s0, rise = fence(b1, s0, rise)
    b0 = in_plane(s0)
    c_m2, c_p2 = combine(w1, b1, (F32, F32))
    down = along_z(joined(down, c_m2), -1)
    rise = along_z(joined(rise, c_p2), 1)

    me = (x_me * NZH + zh_me) * NC + c_me
    bits = jnp.sum(jnp.where(jnp.arange(pair_list.shape[0]) == me, pair_list ^ me, 0))
    new = call(
        unpack_kernel,
        [shape(SHARD, HIDDEN), shape(SHARD, HIDDEN), shape(DSHARD, WIDTH)],
        [SMEM] * 2 + [HBM] * 7,
        [VMEM] * 3,
        "unpack",
        scratch=[pltpu.VMEM((PACK, SIDE), BF), pltpu.SemaphoreType.DMA((NZH + 1,))],
    )(bits.astype(jnp.int32).reshape(1), place, first, hc, hx, *held)

    c_0, c_m1, c_p1 = combine(w0, b0, (F32, F32, F32))
    down = along_z(joined(down, c_m1), -1)
    rise = along_z(joined(rise, c_p1), 1)
    mixed = (down.astype(F32) + rise.astype(F32) + c_0).astype(BF)
    return (mixed, *(v[None] for v in new))


def solution(mesh):
    split = Mesh(mesh.devices.reshape(NX, NZH, NC, NY, NZL), EXPERT_DP)
    rows = P(EXPERT_DP, None)
    blocks = P(EXPERT, DP, None)
    return jax.shard_map(
        body,
        mesh=split,
        in_specs=(rows, P(), rows, rows, blocks, blocks, blocks, P()),
        out_specs=(rows, blocks, blocks, blocks),
        check_vma=False,
    )
```
